128 devices in a mesh: owner: 32 (over y, x, core), helper: 4 (over z).
Axes of the slice: x: 4, y: 4, z: 4, core: 2. Of those that a mesh axis runs over, the one named last changes fastest.
Arguments:
- emb: bfloat16 [131072, 768], P(('owner', 'helper')), may hold values from -6 to 6
- home: int32 [131072, 1], P(('owner', 'helper')), may hold values from 0 to 31; in each aligned block of 1024 rows (0 to 1023, 1024 to 2047, ...) at most 64 rows name the same one
- member: int32 [131072, 1], P(('owner', 'helper')), may hold values from 0 to 15
- rank: int32 [131072], P(('owner', 'helper')), may hold values from 0 to 131071, each once
Outputs:
- best_cos: float32 [131072], P(('owner', 'helper'))
The draws below stay inside these ranges and needn't reach their ends.
Inputs may be any that keep to these rules, and one draw needn't show every extreme that they name: `home`: among the rows of one device, at most 64 name the same owner group, and in every draw some device has exactly 64 rows for one owner group. `rank`: every value of 0 to 131071 appears once.
All inputs are finite; a program needn't handle non-finite values.
Results may differ from the reference program's by a relative error of at most 0.0014.
Values may be sent and summed in bfloat16 or wider, within the bound.
No kernel may reach another device: no remote copies, remote signals or barrier semaphores. Data moves between devices by JAX's collectives and lax.ppermute only.
A program may use at most 64 MiB of HBM per device.

```python
import math
import jax
import jax.numpy as jnp
import numpy as np
from jax import lax

D = 768
ROWS_DEV = 1024
CL_OWN = 16
SEND = 64
ROWS = 131072
N_OWNER = 32


def plant(entries, stream_key, low, top_value):
    place = [jax.random.randint(jax.random.fold_in(stream_key, axis), (), 0, length) for axis, length in enumerate(entries.shape)]
    main_axis = entries.shape.index(max(entries.shape))
    next_to = place[:main_axis] + [(place[main_axis] + 1) % entries.shape[main_axis]] + place[main_axis + 1:]
    return entries.at[tuple(place)].set(low).at[tuple(next_to)].set(top_value)


def steps_of(rng, dims, cuts, low, top_value):
    def one(axis_at, parts):
        draws = jax.random.uniform(jax.random.fold_in(jax.random.fold_in(rng, 6), axis_at), (parts,), jnp.float32, low / len(cuts), top_value / len(cuts))
        return jnp.repeat(jnp.exp(draws), dims[axis_at] // parts).reshape((-1,) + (1,) * (len(dims) - axis_at - 1))

    loudness = one(*cuts[0])
    for cut in cuts[1:]:
        loudness = loudness * one(*cut)
    return loudness


def rank_table(number_of, lean):
    portions = [(1 << 20) // math.isqrt(standing ** lean) + 1 for standing in range(1, number_of + 1)]
    scale = 1 + sum(portions) // (1 << 30)
    return np.cumsum(np.array([max(1, weight // scale) for weight in portions]))


def skewed_ids(stream_key, shape, amount, slope):
    listing = rank_table(amount, slope)
    pick = jax.random.randint(jax.random.fold_in(stream_key, 1), shape, 0, int(listing[amount - 1]))
    rank = jnp.searchsorted(jnp.asarray(listing, jnp.int32), pick, side="right")
    return jax.random.permutation(jax.random.fold_in(stream_key, 2), amount)[rank].astype(jnp.int32)


def shared_out(own_key, own, number, rows, amount, top, reach, lean):
    sequence = jax.random.permutation(own_key, amount)
    crowded, common = shares(amount, rows * top, reach, lean, True), shares(amount, rows * top, reach, lean, False)
    places = jnp.arange(amount)

    def named(lengths, offset_by):
        used = int((lengths > 0).sum())
        fixed = max(1, used // 4)
        passed = fixed + (places - fixed + offset_by * (used - fixed)) % max(1, amount - fixed)
        return jnp.zeros((amount,), jnp.int32).at[sequence[jnp.where(places < fixed, places, passed)]].set(jnp.asarray(lengths, jnp.int32))

    lengths = jnp.where(number % 4 == 0, named(crowded, number // 4), named(common, number - number // 4 - 1))
    mixed = jax.random.permutation(jax.random.fold_in(own, 3), amount)
    giver, taker = mixed[0:amount // 2 * 2:2], mixed[1:amount // 2 * 2:2]
    slack = jnp.minimum(lengths[giver] - 1, reach - lengths[taker]) // 2
    slack = jnp.where((giver == sequence[0]) | (taker == sequence[0]) | (lengths[taker] == 0), 0, jnp.maximum(slack, 0))
    passed = jax.random.randint(jax.random.fold_in(own, 4), (amount // 2,), 0, 1 << 20) % (slack + 1)
    lengths = lengths.at[giver].add(-passed).at[taker].add(passed)
    labels = jnp.searchsorted(jnp.cumsum(lengths), jnp.arange(rows * top), side="right").astype(jnp.int32)
    listing = labels.reshape(top, rows).T
    listing = listing[jax.random.permutation(jax.random.fold_in(own, 1), rows)]
    offset_by = jax.random.randint(jax.random.fold_in(own, 2), (rows, 1), 0, top)
    return jnp.take_along_axis(listing, (jnp.arange(top)[None, :] + offset_by) % top, axis=1)


def shares(amount, total, bound, skew, full):
    portions = [(1 << 20) // math.isqrt(rank ** skew) + 1 for rank in range(1, amount + 1)]
    largest = bound if full else min(bound, max(-(-total // amount), total * portions[0] // sum(portions)))
    least = 1 if total - largest >= amount - 1 else 0
    counts, rest = [largest] + [least] * (amount - 1), total - largest - least * (amount - 1)
    while rest > 0:
        free = [i for i in range(1, amount) if counts[i] < largest] or [i for i in range(1, amount) if counts[i] < bound]
        mass, remaining = sum([portions[i] for i in free]), rest
        for i in free:
            addition = min(bound - counts[i], max(1, remaining * portions[i] // mass), rest)
            counts[i] = counts[i] + addition
            rest = rest - addition
    return np.array(counts)


def scatter_about(key, extent, width, bound, cuts=(), kind=jnp.bfloat16):
    level = steps_of(key, extent, cuts, -0.22, 0.18) if cuts else 1.0
    values = jax.random.normal(key, extent, jnp.float32) * width * level
    return jnp.minimum(jnp.maximum(values, -bound), bound).astype(kind)


def setup_inputs(seed: int = 0) -> dict:
    splits = jax.random.split(jax.random.key(seed), 5)
    emb = scatter_about(splits[0], (ROWS, D), 1.0, 6.0, ((0, 128),))
    home_keys = jax.random.split(jax.random.fold_in(splits[1], 1), ROWS // ROWS_DEV)
    home_turns = jax.random.permutation(jax.random.fold_in(splits[1], 3), ROWS // ROWS_DEV)
    home = jax.vmap(lambda own, number: shared_out(jax.random.fold_in(splits[1], 2), own, number, ROWS_DEV, N_OWNER, 1, SEND, 2))(home_keys, home_turns).reshape((ROWS, 1))
    member = plant(skewed_ids(splits[2], (ROWS, 1), CL_OWN, 2), jax.random.fold_in(splits[2], 3), 0, CL_OWN - 1).astype(jnp.int32)
    rank = jax.random.permutation(splits[3], ROWS).astype(jnp.int32)
    return {"emb": emb, "home": home, "member": member, "rank": rank}


def reference(emb, home, member, rank):
    values = emb.astype(jnp.float32)
    scaling = lax.rsqrt(lax.optimization_barrier(jnp.mean(values * values, axis=1, keepdims=True)) + 1e-06) * D ** (-0.5)
    unit_rows = (values * scaling).astype(jnp.bfloat16)
    cluster = (home[:, 0] * CL_OWN + member[:, 0]).astype(jnp.int32)
    row_total = cluster.shape[0]
    sort_key = cluster * row_total + rank
    sort_order = jnp.argsort(sort_key).astype(jnp.int32)
    sorted_unit = unit_rows[sort_order]
    sorted_cluster = cluster[sort_order]
    first_pos = jnp.searchsorted(sorted_cluster, sorted_cluster, side='left').astype(jnp.int32)
    block_rows = 256 if row_total % 256 == 0 else row_total
    block_count = row_total // block_rows
    positions = jnp.arange(block_rows, dtype=jnp.int32)

    def one_block(block_index):
        start_row = block_index * block_rows
        q_rows = lax.dynamic_slice_in_dim(sorted_unit, start_row, block_rows, 0)
        q_cluster = lax.dynamic_slice_in_dim(sorted_cluster, start_row, block_rows, 0)
        q_pos = start_row + positions
        low_block = first_pos[start_row] // block_rows

        def key_step(key_block, running):
            key_start = key_block * block_rows
            k_rows = lax.dynamic_slice_in_dim(sorted_unit, key_start, block_rows, 0)
            k_cluster = lax.dynamic_slice_in_dim(sorted_cluster, key_start, block_rows, 0)
            k_pos = key_start + positions
            scores = jnp.dot(q_rows, k_rows.T, preferred_element_type=jnp.float32)
            is_valid = (q_cluster[:, None] == k_cluster[None, :]) & (k_pos[None, :] < q_pos[:, None])
            return jnp.maximum(running, lax.optimization_barrier(jnp.max(jnp.where(is_valid, scores, -1.0), axis=1)))
        return lax.fori_loop(low_block, block_index + 1, key_step, jnp.full((block_rows,), -1.0, jnp.float32))
    best_sorted = lax.map(one_block, jnp.arange(block_count, dtype=jnp.int32)).reshape(-1)
    return jnp.zeros((row_total,), jnp.float32).at[sort_order].set(best_sorted)
```

```python
import functools

import jax
import jax.numpy as jnp
from jax import lax
from jax.experimental import pallas as pl
from jax.experimental.pallas import tpu as pltpu
from jax.sharding import Mesh, PartitionSpec as P

D = 768
ROWS = 1024
CLUSTERS = 512
MEMBERS = 16
CHIPS = 64
DEVICES = 128
LANES = 128
PIECES = CLUSTERS // LANES
BATCH = 32
FAST = 40
SLOW = 72
GROUP = 8
QB = 256
KB = 512
VMEM_BYTES = 56 << 20
CHIP_AXES = ("yx", "z")
ALL_AXES = ("yx", "core", "z")
F32, BF16, I32 = jnp.float32, jnp.bfloat16, jnp.int32
NT = (((1,), (1,)), ((), ()))


def iota(shape, dim):
    return lax.broadcasted_iota(I32, shape, dim)


def dot(a, b):
    return jnp.dot(a, b, preferred_element_type=F32)


def dot_nt(a, b):
    return lax.dot_general(a, b, NT, preferred_element_type=F32)


def ones_where(mask):
    return jnp.where(mask, 1.0, 0.0).astype(BF16)


def params():
    return pltpu.CompilerParams(vmem_limit_bytes=VMEM_BYTES)


def count_kernel(cl_ref, out_ref):
    cl = cl_ref[...]
    ones = jnp.ones((8, ROWS), BF16)
    sub8 = iota((8, LANES), 0)
    tile = jnp.zeros((8, LANES), F32)
    for r in range(PIECES):
        hot = ones_where(cl == iota((LANES, ROWS), 0) + r * LANES)
        tile = jnp.where(sub8 == r, dot_nt(ones, hot), tile)
    out_ref[...] = jnp.broadcast_to(tile.astype(BF16)[None], out_ref.shape)


def unit_kernel(emb_ref, unit_ref):
    values = emb_ref[...].astype(F32)
    mean = jnp.sum(values * values, axis=1, keepdims=True) * (1.0 / D)
    unit_ref[...] = (values * (lax.rsqrt(mean + 1e-06) * D ** (-0.5))).astype(BF16)


def assign_kernel(place_ref, counts_ref, asg_ref, boxes_ref, most_ref, sizes, bins, pairs):
    chip, core = place_ref[0], place_ref[1]
    lane = iota((LANES, LANES), 1)
    sub = iota((LANES, LANES), 0)
    eye = lane == sub
    lane1 = iota((1, LANES), 1)
    flat = counts_ref[...]
    total = dot(ones_where(iota((8, DEVICES * 8), 1) % 8 == iota((8, DEVICES * 8), 0)), flat)
    tot = [total[r : r + 1, :] for r in range(PIECES)]
    key = [tot[r] * CLUSTERS + (CLUSTERS - 1 - r * LANES - lane1).astype(F32) for r in range(PIECES)]
    col = [jnp.sum(jnp.where(eye, key[r], 0.0), axis=1, keepdims=True) for r in range(PIECES)]
    pos = []
    for r in range(PIECES):
        above = jnp.zeros((LANES, LANES), F32)
        for q in range(PIECES):
            above = above + jnp.where(col[q] > key[r], 1.0, 0.0)
        pos.append(jnp.sum(above, axis=0, keepdims=True).astype(I32))
    for q in range(PIECES):
        here = jnp.zeros((LANES, LANES), F32)
        for r in range(PIECES):
            here = here + jnp.where(pos[r] == sub + q * LANES, tot[r], 0.0)
        sizes[q * LANES : (q + 1) * LANES, :] = jnp.broadcast_to(
            jnp.sum(here, axis=1, keepdims=True), (LANES, LANES)
        )
    lane_c = iota((CHIPS, LANES), 1)
    eye_c = lane_c == iota((CHIPS, LANES), 0)
    lane_b = iota((BATCH, LANES), 1)
    sub_b = iota((BATCH, LANES), 0)

    def one_batch(step, load):
        order = jnp.where(lane1 < CHIPS, load * CHIPS + lane1.astype(F32), 3.0e7)
        order_col = jnp.sum(jnp.where(eye_c, order, 0.0), axis=1, keepdims=True)
        place = jnp.sum(jnp.where(order_col < order, 1.0, 0.0), axis=0, keepdims=True).astype(I32)
        chosen = place == sub_b
        rows = pl.ds(pl.multiple_of(step * BATCH, BATCH), BATCH)
        bins[rows, :] = jnp.broadcast_to(
            jnp.sum(jnp.where(chosen, lane_b, 0), axis=1, keepdims=True), (BATCH, LANES)
        )
        return load + jnp.sum(jnp.where(chosen, sizes[rows, :], 0.0), axis=0, keepdims=True)

    lax.fori_loop(0, CLUSTERS // BATCH, one_batch, jnp.zeros((1, LANES), F32))
    asg = []
    for r in range(PIECES):
        found = jnp.zeros((LANES, LANES), I32)
        for q in range(PIECES):
            rows = bins[q * LANES : (q + 1) * LANES, :]
            found = found + jnp.where(pos[r] == sub + q * LANES, rows, 0)
        asg.append(jnp.sum(found, axis=0, keepdims=True))
    row8 = iota((DEVICES * 8, LANES), 0) % 8

    def pair_counts(table):
        per_row = jnp.zeros((DEVICES * 8, LANES), F32)
        for r in range(PIECES):
            per_row = jnp.where(row8 == r, dot_nt(flat, ones_where(table[r] == sub)), per_row)
        return jnp.sum(per_row.reshape(DEVICES, 8, LANES), axis=1)

    def put(table):
        sub8 = iota((8, LANES), 0)
        tile = jnp.zeros((8, LANES), I32)
        for r in range(PIECES):
            tile = jnp.where(sub8 == r, table[r], tile)
        asg_ref[...] = tile

    pairs[...] = pair_counts(asg)
    put(asg)
    most = jnp.max(pairs[...]).astype(I32)
    most_ref[0] = most

    @pl.when(most > FAST - 1)
    def _():
        fixed = []
        for r in range(PIECES):
            cluster = lane1 + r * LANES
            fixed.append((cluster // MEMBERS) * 2 + (cluster % MEMBERS) // 8)
        pairs[...] = pair_counts(fixed)
        put(fixed)

    mine = jnp.sum(jnp.where(lane == chip, pairs[...], 0.0), axis=1, keepdims=True)
    box = lane % CHIPS
    source_core = jnp.where(lane < CHIPS, core, 1 - core)
    source = ((box // 4) * 2 + source_core) * 4 + box % 4
    boxes_ref[...] = jnp.sum(jnp.where(sub == source, mine, 0.0), axis=0, keepdims=True).astype(I32)


def route_kernel(asg_ref, cl_ref, rank_ref, unit_ref, out_ref, where_ref, index, labels, *, slots):
    group = pl.program_id(0)

    @pl.when(group == 0)
    def _():
        cl = cl_ref[...]
        rank = rank_ref[...]
        sub = iota((CHIPS, LANES), 0)
        to_chip = jnp.zeros((CHIPS, ROWS), F32)
        for r in range(PIECES):
            hot = ones_where(cl == iota((LANES, ROWS), 0) + r * LANES)
            to_chip = to_chip + dot(ones_where(asg_ref[r : r + 1, :] == sub), hot)
        before = ones_where(iota((LANES, LANES), 0) < iota((LANES, LANES), 1))
        carry = jnp.zeros((CHIPS, 1), F32)
        slot_parts, chip_parts = [], []
        for b in range(ROWS // LANES):
            part = to_chip[:, b * LANES : (b + 1) * LANES]
            earlier = dot(part.astype(BF16), before) + carry
            slot_parts.append(jnp.sum(part * earlier, axis=0, keepdims=True))
            chip_parts.append(jnp.sum(part * sub.astype(F32), axis=0, keepdims=True))
            carry = carry + jnp.sum(part, axis=1, keepdims=True)
        slot = jnp.concatenate(slot_parts, axis=1).astype(I32)
        chip = jnp.concatenate(chip_parts, axis=1).astype(I32)
        index[...] = chip * slots + slot
        where_ref[0:1, :] = chip
        where_ref[1:2, :] = slot
        slot_hot = ones_where(slot == iota((LANES, ROWS), 0))
        pieces = (rank >> 9, (rank >> 1) & 255, (rank & 1) + 2 * (cl // MEMBERS), cl % MEMBERS + 1)
        for k, piece in enumerate(pieces):
            weighted = (to_chip * piece.astype(F32)).astype(BF16)
            labels[:, k * LANES : (k + 1) * LANES] = dot_nt(weighted, slot_hot).astype(BF16)

    size = GROUP * slots
    first = group * size
    hot = ones_where(index[...] == iota((size, ROWS), 0) + first)
    rows = dot(hot, unit_ref[...])
    last = (iota((size, CHIPS), 1) - group * GROUP) * slots + slots - 1
    text = dot(ones_where(last == iota((size, CHIPS), 0)), labels[...])
    out_ref[:, : PIECES * LANES] = (rows[:, : PIECES * LANES] + text).astype(BF16)
    out_ref[:, PIECES * LANES :] = rows[:, PIECES * LANES :].astype(BF16)


def match_kernel(boxes_ref, mine_ref, other_ref, out_ref, keys, ids, boxed, best, starts, *, slots):
    size = GROUP * slots
    lane_g = iota((size, LANES), 1)
    row_g = iota((size, LANES), 0)
    diagonal = lane_g == row_g % slots
    box_of_row = ones_where(iota((size, GROUP), 0) // slots == iota((size, GROUP), 1))
    label_row = ones_where(iota((GROUP, size), 1) == iota((GROUP, size), 0) * slots + slots - 1)

    def offsets(b, at):
        starts[b] = at
        return at + ((boxes_ref[0, b] + 7) // 8) * 8

    n_mine = lax.fori_loop(0, CHIPS, offsets, 0)
    n_all = lax.fori_loop(CHIPS, 2 * CHIPS, offsets, n_mine)

    for half, box_rows in enumerate((mine_ref, other_ref)):

        def label_group(g, carry, box_rows=box_rows, half=half):
            rows = pl.ds(pl.multiple_of(g * size, 16), size)
            blocks = pl.ds(g * (size // 8), size // 8)
            held = box_rows[blocks, :, : PIECES * LANES].reshape(size, PIECES * LANES)
            text = dot(label_row, held).astype(BF16)
            spread = dot(box_of_row, text)
            rank = jnp.zeros((size, LANES), F32)
            cluster = jnp.zeros((size, LANES), F32)
            for k, (to_rank, to_cluster) in enumerate(((512, 0), (2, 0), (1, 0), (0, 1))):
                piece = jnp.where(diagonal, spread[:, k * LANES : (k + 1) * LANES], 0.0)
                if k == 2:
                    home = jnp.floor(piece * 0.5)
                    piece = piece - 2.0 * home
                    cluster = cluster + dot(home.astype(BF16), jnp.full((LANES, LANES), MEMBERS, BF16))
                if to_rank:
                    rank = rank + dot(piece.astype(BF16), jnp.full((LANES, LANES), to_rank, BF16))
                if to_cluster:
                    cluster = cluster + dot(piece.astype(BF16), jnp.ones((LANES, LANES), BF16))
                    filled = dot(piece.astype(BF16), jnp.ones((LANES, LANES), BF16))
            ident = (cluster.astype(I32) << 17) + rank.astype(I32)
            boxed[rows, :] = jnp.where(filled > 0.5, ident, -1)
            return carry

        lax.fori_loop(0, CHIPS // GROUP, label_group, 0)

        def pack(b, carry, box_rows=box_rows, half=half):
            start = starts[half * CHIPS + b]
            keys[pl.ds(start // 8, slots // 8)] = box_rows[pl.ds(b * (slots // 8), slots // 8)]
            source = pl.ds(pl.multiple_of(b * slots, 8), slots)
            ids[pl.ds(pl.multiple_of(start, 8), slots), :] = boxed[source, :]
            return carry

        lax.fori_loop(0, CHIPS, pack, 0)

    ids[pl.ds(pl.multiple_of(n_all, 8), KB), :] = jnp.full((KB, LANES), -1, I32)
    eye = iota((LANES, LANES), 0) == iota((LANES, LANES), 1)

    def queries(q, carry):
        rows = pl.multiple_of(q * QB, QB)
        query = keys[pl.ds(q * (QB // 8), QB // 8)].reshape(QB, D)
        high, low = [], []
        for half in range(QB // LANES):
            ident = ids[pl.ds(rows + half * LANES, LANES), :]
            line = jnp.sum(jnp.where(eye, ident, 0), axis=0, keepdims=True)
            high.append(line)
            low.append((line >> 17) << 17)

        def key_block(k, acc):
            at = pl.ds(pl.multiple_of(k * KB, KB), KB)
            score = dot_nt(keys[pl.ds(k * (KB // 8), KB // 8)].reshape(KB, D), query)
            ident = ids[at, :]
            parts = []
            for half in range(QB // LANES):
                piece = score[:, half * LANES : (half + 1) * LANES]
                valid = (ident >= low[half]) & (ident < high[half])
                piece = jnp.where(valid, piece, -1.0)
                parts.append(jnp.maximum(acc[half], jnp.max(piece.reshape(KB // 8, 8, LANES), axis=0)))
            return tuple(parts)

        floor = jnp.full((8, LANES), -1.0, F32)
        acc = lax.fori_loop(0, (n_all + KB - 1) // KB, key_block, (floor,) * (QB // LANES))
        for half in range(QB // LANES):
            line = jnp.max(acc[half], axis=0, keepdims=True)
            column = jnp.sum(jnp.where(eye, line, 0.0), axis=1, keepdims=True)
            best[pl.ds(rows + half * LANES, LANES), :] = jnp.broadcast_to(column, (LANES, LANES))
        return carry

    lax.fori_loop(0, (n_mine + QB - 1) // QB, queries, 0)
    lane8 = iota((8, LANES), 1)
    sub8 = iota((8, LANES), 0)

    def unpack(b, carry):
        start = starts[b]
        tile = jnp.zeros((8, LANES), F32)
        for t in range(slots // 8):
            part = best[pl.ds(pl.multiple_of(start + 8 * t, 8), 8), :]
            tile = tile + jnp.where(lane8 == sub8 + 8 * t, part, 0.0)
        out_ref[b] = jnp.where(lane8 < boxes_ref[0, b], tile, 0.0)
        return carry

    lax.fori_loop(0, CHIPS, unpack, 0)


def result_kernel(back_ref, where_ref, out_ref):
    table = jnp.sum(back_ref[...], axis=1)
    table = jnp.concatenate([table, jnp.zeros((LANES - CHIPS, LANES), F32)], axis=0).T
    to_chip = jnp.where(where_ref[0:1, :] == iota((LANES, ROWS), 0), 1.0, 0.0)
    by_slot = jnp.dot(
        table, to_chip, preferred_element_type=F32, precision=lax.Precision.HIGHEST
    )
    picked = jnp.where(where_ref[1:2, :] == iota((LANES, ROWS), 0), by_slot, 0.0)
    out_ref[...] = jnp.sum(picked, axis=0, keepdims=True)


def exchange(slots, asg, cl, rank, unit, boxes):
    size = GROUP * slots
    outbox, where = pl.pallas_call(
        functools.partial(route_kernel, slots=slots),
        grid=(CHIPS // GROUP,),
        in_specs=[
            pl.BlockSpec((8, LANES), lambda g: (0, 0)),
            pl.BlockSpec((1, ROWS), lambda g: (0, 0)),
            pl.BlockSpec((1, ROWS), lambda g: (0, 0)),
            pl.BlockSpec((ROWS, D), lambda g: (0, 0)),
        ],
        out_specs=[
            pl.BlockSpec((size, D), lambda g: (g, 0)),
            pl.BlockSpec((2, ROWS), lambda g: (0, 0)),
        ],
        out_shape=[
            jax.ShapeDtypeStruct((CHIPS * slots, D), BF16),
            jax.ShapeDtypeStruct((2, ROWS), I32),
        ],
        scratch_shapes=[pltpu.VMEM((1, ROWS), I32), pltpu.VMEM((CHIPS, PIECES * LANES), BF16)],
        compiler_params=params(),
        name="route",
    )(asg, cl, rank, unit)
    mine = lax.all_to_all(outbox.reshape(CHIPS, slots, D), CHIP_AXES, 0, 0, tiled=True)
    mine = mine.reshape(CHIPS * slots // 8, 8, D)
    other = lax.ppermute(mine, "core", [(0, 1), (1, 0)])
    most = 2 * CHIPS * (slots // 8) * 8 + slots
    whole = -(-most // KB) * KB + KB
    half = -(-(CHIPS * slots) // QB) * QB + QB
    results = pl.pallas_call(
        functools.partial(match_kernel, slots=slots),
        in_specs=[
            pl.BlockSpec(memory_space=pltpu.SMEM),
            pl.BlockSpec(memory_space=pltpu.VMEM),
            pl.BlockSpec(memory_space=pltpu.VMEM),
        ],
        out_specs=pl.BlockSpec(memory_space=pltpu.VMEM),
        out_shape=jax.ShapeDtypeStruct((CHIPS, 8, LANES), F32),
        scratch_shapes=[
            pltpu.VMEM((whole // 8, 8, D), BF16),
            pltpu.VMEM((whole, LANES), I32),
            pltpu.VMEM((CHIPS * slots, LANES), I32),
            pltpu.VMEM((half, LANES), F32),
            pltpu.SMEM((2 * CHIPS,), I32),
        ],
        compiler_params=params(),
        name="match",
    )(boxes, mine, other)
    back = lax.all_to_all(results, CHIP_AXES, 0, 0, tiled=True)
    return pl.pallas_call(
        result_kernel,
        out_shape=jax.ShapeDtypeStruct((1, ROWS), F32),
        compiler_params=params(),
        name="result",
    )(back, where)


def body(emb, home, member, rank):
    cl = home.reshape(1, ROWS) * MEMBERS + member.reshape(1, ROWS)
    rank = rank.reshape(1, ROWS)
    counts = pl.pallas_call(
        count_kernel,
        out_shape=jax.ShapeDtypeStruct((DEVICES, 8, LANES), BF16),
        compiler_params=params(),
        name="count",
    )(cl)
    counts = lax.all_to_all(counts, ALL_AXES, 0, 0, tiled=True).reshape(DEVICES * 8, LANES)
    unit = pl.pallas_call(
        unit_kernel,
        grid=(4,),
        in_specs=[pl.BlockSpec((ROWS // 4, D), lambda i: (i, 0))],
        out_specs=pl.BlockSpec((ROWS // 4, D), lambda i: (i, 0)),
        out_shape=jax.ShapeDtypeStruct((ROWS, D), BF16),
        compiler_params=params(),
        cost_estimate=pl.CostEstimate(flops=4 * ROWS * D, bytes_accessed=4 * ROWS * D, transcendentals=ROWS),
        name="unit",
    )(emb)
    chip = lax.axis_index("yx") * lax.axis_size("z") + lax.axis_index("z")
    place = jnp.stack([chip, lax.axis_index("core")]).astype(I32)
    asg, boxes, most = pl.pallas_call(
        assign_kernel,
        in_specs=[
            pl.BlockSpec(memory_space=pltpu.SMEM),
            pl.BlockSpec(memory_space=pltpu.VMEM),
        ],
        out_specs=[
            pl.BlockSpec(memory_space=pltpu.VMEM),
            pl.BlockSpec(memory_space=pltpu.VMEM),
            pl.BlockSpec(memory_space=pltpu.SMEM),
        ],
        out_shape=[
            jax.ShapeDtypeStruct((8, LANES), I32),
            jax.ShapeDtypeStruct((1, LANES), I32),
            jax.ShapeDtypeStruct((1,), I32),
        ],
        scratch_shapes=[
            pltpu.VMEM((CLUSTERS, LANES), F32),
            pltpu.VMEM((CLUSTERS, LANES), I32),
            pltpu.VMEM((DEVICES, LANES), F32),
        ],
        compiler_params=params(),
        name="assign",
    )(place, counts)
    out = lax.cond(
        most[0] < FAST,
        functools.partial(exchange, FAST),
        functools.partial(exchange, SLOW),
        asg,
        cl,
        rank,
        unit,
        boxes,
    )
    return out.reshape(ROWS)


def solution(mesh):
    chips = Mesh(mesh.devices.reshape(-1, 2, mesh.devices.shape[1]), ALL_AXES)
    rows = P(ALL_AXES)
    return jax.shard_map(
        body,
        mesh=chips,
        in_specs=(P(ALL_AXES, None), P(ALL_AXES, None), P(ALL_AXES, None), rows),
        out_specs=rows,
        check_vma=False,
    )
```

```python
import functools

import jax
import jax.numpy as jnp
from jax import lax
from jax.experimental import pallas as pl
from jax.experimental.pallas import tpu as pltpu
from jax.sharding import Mesh, PartitionSpec as P

D = 768
ROWS = 1024
CLUSTERS = 512
MEMBERS = 16
CHIPS = 64
DEVICES = 128
LANES = 128
PIECES = CLUSTERS // LANES
BATCH = 32
FAST = 40
SLOW = 72
GROUP = 8
QB = 512
KB = 1024
UNROLL = 32
VMEM_BYTES = 56 << 20
CHIP_AXES = ("yx", "z")
ALL_AXES = ("yx", "core", "z")
F32, BF16, I32 = jnp.float32, jnp.bfloat16, jnp.int32
NT = (((1,), (1,)), ((), ()))


def iota(shape, dim):
    return lax.broadcasted_iota(I32, shape, dim)


def dot(a, b):
    return jnp.dot(a, b, preferred_element_type=F32)


def dot_nt(a, b):
    return lax.dot_general(a, b, NT, preferred_element_type=F32)


def ones_where(mask):
    return jnp.where(mask, 1.0, 0.0).astype(BF16)


def params():
    return pltpu.CompilerParams(vmem_limit_bytes=VMEM_BYTES)


def count_kernel(cl_ref, out_ref):
    cl = cl_ref[...]
    ones = jnp.ones((8, ROWS), BF16)
    sub8 = iota((8, LANES), 0)
    tile = jnp.zeros((8, LANES), F32)
    for r in range(PIECES):
        hot = ones_where(cl == iota((LANES, ROWS), 0) + r * LANES)
        tile = jnp.where(sub8 == r, dot_nt(ones, hot), tile)
    out_ref[...] = jnp.broadcast_to(tile.astype(BF16)[None], out_ref.shape)


def unit_kernel(emb_ref, unit_ref):
    values = emb_ref[...].astype(F32)
    mean = jnp.sum(values * values, axis=1, keepdims=True) * (1.0 / D)
    unit_ref[...] = (values * (lax.rsqrt(mean + 1e-06) * D ** (-0.5))).astype(BF16)


def assign_kernel(place_ref, counts_ref, asg_ref, boxes_ref, most_ref, sizes, bins, pairs):
    chip, core = place_ref[0], place_ref[1]
    lane = iota((LANES, LANES), 1)
    sub = iota((LANES, LANES), 0)
    eye = lane == sub
    lane1 = iota((1, LANES), 1)
    flat = counts_ref[...]
    total = dot(ones_where(iota((8, DEVICES * 8), 1) % 8 == iota((8, DEVICES * 8), 0)), flat)
    tot = [total[r : r + 1, :] for r in range(PIECES)]
    key = [tot[r] * CLUSTERS + (CLUSTERS - 1 - r * LANES - lane1).astype(F32) for r in range(PIECES)]
    col = [jnp.sum(jnp.where(eye, key[r], 0.0), axis=1, keepdims=True) for r in range(PIECES)]
    pos = []
    for r in range(PIECES):
        above = jnp.zeros((LANES, LANES), F32)
        for q in range(PIECES):
            above = above + jnp.where(col[q] > key[r], 1.0, 0.0)
        pos.append(jnp.sum(above, axis=0, keepdims=True).astype(I32))
    for q in range(PIECES):
        here = jnp.zeros((LANES, LANES), F32)
        for r in range(PIECES):
            here = here + jnp.where(pos[r] == sub + q * LANES, tot[r], 0.0)
        sizes[q * LANES : (q + 1) * LANES, :] = jnp.broadcast_to(
            jnp.sum(here, axis=1, keepdims=True), (LANES, LANES)
        )
    lane_c = iota((CHIPS, LANES), 1)
    eye_c = lane_c == iota((CHIPS, LANES), 0)
    lane_b = iota((BATCH, LANES), 1)
    sub_b = iota((BATCH, LANES), 0)

    def one_batch(step, load):
        order = jnp.where(lane1 < CHIPS, load * CHIPS + lane1.astype(F32), 3.0e7)
        order_col = jnp.sum(jnp.where(eye_c, order, 0.0), axis=1, keepdims=True)
        place = jnp.sum(jnp.where(order_col < order, 1.0, 0.0), axis=0, keepdims=True).astype(I32)
        chosen = place == sub_b
        rows = pl.ds(pl.multiple_of(step * BATCH, BATCH), BATCH)
        bins[rows, :] = jnp.broadcast_to(
            jnp.sum(jnp.where(chosen, lane_b, 0), axis=1, keepdims=True), (BATCH, LANES)
        )
        return load + jnp.sum(jnp.where(chosen, sizes[rows, :], 0.0), axis=0, keepdims=True)

    lax.fori_loop(0, CLUSTERS // BATCH, one_batch, jnp.zeros((1, LANES), F32))
    asg = []
    for r in range(PIECES):
        found = jnp.zeros((LANES, LANES), I32)
        for q in range(PIECES):
            rows = bins[q * LANES : (q + 1) * LANES, :]
            found = found + jnp.where(pos[r] == sub + q * LANES, rows, 0)
        asg.append(jnp.sum(found, axis=0, keepdims=True))
    row8 = iota((DEVICES * 8, LANES), 0) % 8

    def pair_counts(table):
        per_row = jnp.zeros((DEVICES * 8, LANES), F32)
        for r in range(PIECES):
            per_row = jnp.where(row8 == r, dot_nt(flat, ones_where(table[r] == sub)), per_row)
        return jnp.sum(per_row.reshape(DEVICES, 8, LANES), axis=1)

    def put(table):
        sub8 = iota((8, LANES), 0)
        tile = jnp.zeros((8, LANES), I32)
        for r in range(PIECES):
            tile = jnp.where(sub8 == r, table[r], tile)
        asg_ref[...] = tile

    pairs[...] = pair_counts(asg)
    put(asg)
    most = jnp.max(pairs[...]).astype(I32)
    most_ref[0] = most

    @pl.when(most > FAST - 1)
    def _():
        fixed = []
        for r in range(PIECES):
            cluster = lane1 + r * LANES
            fixed.append((cluster // MEMBERS) * 2 + (cluster % MEMBERS) // 8)
        pairs[...] = pair_counts(fixed)
        put(fixed)

    mine = jnp.sum(jnp.where(lane == chip, pairs[...], 0.0), axis=1, keepdims=True)
    box = lane % CHIPS
    source_core = jnp.where(lane < CHIPS, core, 1 - core)
    source = ((box // 4) * 2 + source_core) * 4 + box % 4
    boxes = jnp.sum(jnp.where(sub == source, mine, 0.0), axis=0, keepdims=True).astype(I32)
    rounded = (((boxes + 7) // 8) * 8).astype(F32).astype(BF16)
    boxes_ref[0:1, :] = boxes
    boxes_ref[1:2, :] = dot(rounded, ones_where(sub < lane)).astype(I32)


def route_kernel(asg_ref, cl_ref, rank_ref, unit_ref, out_ref, where_ref, index, labels, *, slots):
    group = pl.program_id(0)

    @pl.when(group == 0)
    def _():
        cl = cl_ref[...]
        rank = rank_ref[...]
        sub = iota((CHIPS, LANES), 0)
        to_chip = jnp.zeros((CHIPS, ROWS), F32)
        for r in range(PIECES):
            hot = ones_where(cl == iota((LANES, ROWS), 0) + r * LANES)
            to_chip = to_chip + dot(ones_where(asg_ref[r : r + 1, :] == sub), hot)
        before = ones_where(iota((LANES, LANES), 0) < iota((LANES, LANES), 1))
        carry = jnp.zeros((CHIPS, 1), F32)
        slot_parts, chip_parts = [], []
        for b in range(ROWS // LANES):
            part = to_chip[:, b * LANES : (b + 1) * LANES]
            earlier = dot(part.astype(BF16), before) + carry
            slot_parts.append(jnp.sum(part * earlier, axis=0, keepdims=True))
            chip_parts.append(jnp.sum(part * sub.astype(F32), axis=0, keepdims=True))
            carry = carry + jnp.sum(part, axis=1, keepdims=True)
        slot = jnp.concatenate(slot_parts, axis=1).astype(I32)
        chip = jnp.concatenate(chip_parts, axis=1).astype(I32)
        index[...] = chip * slots + slot
        where_ref[0:1, :] = chip
        where_ref[1:2, :] = slot
        slot_hot = ones_where(slot == iota((LANES, ROWS), 0))
        pieces = (rank >> 9, (rank >> 1) & 255, (rank & 1) + 2 * (cl // MEMBERS), cl % MEMBERS + 1)
        for k, piece in enumerate(pieces):
            weighted = (to_chip * piece.astype(F32)).astype(BF16)
            labels[:, k * LANES : (k + 1) * LANES] = dot_nt(weighted, slot_hot).astype(BF16)

    size = GROUP * slots
    first = group * size
    hot = ones_where(index[...] == iota((size, ROWS), 0) + first)
    rows = dot(hot, unit_ref[...])
    last = (iota((size, CHIPS), 1) - group * GROUP) * slots + slots - 1
    text = dot(ones_where(last == iota((size, CHIPS), 0)), labels[...])
    out_ref[:, : PIECES * LANES] = (rows[:, : PIECES * LANES] + text).astype(BF16)
    out_ref[:, PIECES * LANES :] = rows[:, PIECES * LANES :].astype(BF16)


def match_kernel(boxes_ref, mine_ref, other_ref, out_ref, keys, ids, columns, text, best, *, slots):
    tiles = slots // 8
    lane1 = iota((1, LANES), 1)
    n_mine = boxes_ref[1, CHIPS]
    n_all = boxes_ref[1, 2 * CHIPS - 1] + ((boxes_ref[0, 2 * CHIPS - 1] + 7) // 8) * 8
    ids[...] = jnp.full(ids.shape, -1, I32)
    label_row = ones_where(iota((CHIPS, CHIPS * 8), 1) == iota((CHIPS, CHIPS * 8), 0) * 8 + 7)
    for half, box_rows in enumerate((mine_ref, other_ref)):
        held = box_rows[:, tiles - 1, :, : PIECES * LANES].reshape(CHIPS * 8, PIECES * LANES)
        words = dot(label_row, held).astype(I32)
        high, low, mixed, filled = (words[:, k * LANES : (k + 1) * LANES] for k in range(PIECES))
        rank = (high << 9) + (low << 1) + (mixed & 1)
        cluster = ((mixed >> 1) << 4) + filled - 1
        text[half] = jnp.where(filled > 0, (cluster << 17) + rank, -1)

        def pack(b, carry, box_rows=box_rows, half=half):
            start = boxes_ref[1, half * CHIPS + b]
            keys[pl.ds(start // 8, tiles)] = box_rows[b]
            shift = lax.rem(start, LANES)
            row = start // LANES
            line = pltpu.roll(text[half, pl.ds(b, 1), :], shift, 1)
            ids[pl.ds(row, 1), :] = jnp.where(lane1 >= shift, line, ids[pl.ds(row, 1), :])
            ids[pl.ds(row + 1, 1), :] = jnp.where(lane1 < shift, line, -1)
            return carry

        lax.fori_loop(0, CHIPS, pack, 0, unroll=UNROLL)

    k_blocks = (n_all + KB - 1) // KB
    per_block = KB // LANES

    def column(k, carry):
        for r in range(per_block):
            line = jnp.broadcast_to(ids[pl.ds(k * per_block + r, 1), :], (LANES, LANES))
            rows = pl.ds(pl.multiple_of(k * KB + r * LANES, LANES), LANES)
            columns[rows, :] = jnp.transpose(line)
        return carry

    lax.fori_loop(0, k_blocks, column, 0)
    parts = QB // LANES

    def queries(q, carry):
        query = keys[pl.ds(q * (QB // 8), QB // 8)].reshape(QB, D)
        high = [ids[pl.ds(q * parts + p, 1), :] for p in range(parts)]
        low = [(h >> 17) << 17 for h in high]

        def key_block(k, acc):
            score = dot_nt(keys[pl.ds(k * (KB // 8), KB // 8)].reshape(KB, D), query)
            ident = columns[pl.ds(pl.multiple_of(k * KB, KB), KB), :]
            new = []
            for p in range(parts):
                piece = score[:, p * LANES : (p + 1) * LANES]
                valid = (ident >= low[p]) & (ident < high[p])
                piece = jnp.where(valid, piece, -1.0)
                new.append(jnp.maximum(acc[p], jnp.max(piece.reshape(KB // 8, 8, LANES), axis=0)))
            return tuple(new)

        acc = lax.fori_loop(0, k_blocks, key_block, (jnp.full((8, LANES), -1.0, F32),) * parts)
        for p in range(parts):
            best[pl.ds(q * parts + p, 1), :] = jnp.max(acc[p], axis=0, keepdims=True)
        return carry

    lax.fori_loop(0, (n_mine + QB - 1) // QB, queries, 0)
    sub8 = iota((8, LANES), 0)

    def unpack(b, carry):
        start = boxes_ref[1, b]
        shift = lax.rem(start, LANES)
        row = start // LANES
        two = jnp.where(lane1 >= shift, best[pl.ds(row, 1), :], best[pl.ds(row + 1, 1), :])
        line = pltpu.roll(two, lax.rem(LANES - shift, LANES), 1)
        line = jnp.where(lane1 < boxes_ref[0, b], line, 0.0)
        out_ref[b] = jnp.where(sub8 == 0, line, 0.0)
        return carry

    lax.fori_loop(0, CHIPS, unpack, 0, unroll=UNROLL)


def result_kernel(back_ref, where_ref, out_ref):
    table = jnp.sum(back_ref[...], axis=1)
    table = jnp.concatenate([table, jnp.zeros((LANES - CHIPS, LANES), F32)], axis=0).T
    to_chip = jnp.where(where_ref[0:1, :] == iota((LANES, ROWS), 0), 1.0, 0.0)
    by_slot = jnp.dot(
        table, to_chip, preferred_element_type=F32, precision=lax.Precision.HIGHEST
    )
    picked = jnp.where(where_ref[1:2, :] == iota((LANES, ROWS), 0), by_slot, 0.0)
    out_ref[...] = jnp.sum(picked, axis=0, keepdims=True)


def exchange(slots, asg, cl, rank, unit, boxes):
    size = GROUP * slots
    outbox, where = pl.pallas_call(
        functools.partial(route_kernel, slots=slots),
        grid=(CHIPS // GROUP,),
        in_specs=[
            pl.BlockSpec((8, LANES), lambda g: (0, 0)),
            pl.BlockSpec((1, ROWS), lambda g: (0, 0)),
            pl.BlockSpec((1, ROWS), lambda g: (0, 0)),
            pl.BlockSpec((ROWS, D), lambda g: (0, 0)),
        ],
        out_specs=[
            pl.BlockSpec((size, D), lambda g: (g, 0)),
            pl.BlockSpec((2, ROWS), lambda g: (0, 0)),
        ],
        out_shape=[
            jax.ShapeDtypeStruct((CHIPS * slots, D), BF16),
            jax.ShapeDtypeStruct((2, ROWS), I32),
        ],
        scratch_shapes=[pltpu.VMEM((1, ROWS), I32), pltpu.VMEM((CHIPS, PIECES * LANES), BF16)],
        compiler_params=params(),
        name="route",
    )(asg, cl, rank, unit)
    mine = lax.all_to_all(outbox.reshape(CHIPS, slots, D), CHIP_AXES, 0, 0, tiled=True)
    mine = mine.reshape(CHIPS, slots // 8, 8, D)
    other = lax.ppermute(mine, "core", [(0, 1), (1, 0)])
    whole = -(-(2 * CHIPS * slots + slots) // KB) * KB + KB
    half = -(-(CHIPS * slots) // QB) * QB + QB
    results = pl.pallas_call(
        functools.partial(match_kernel, slots=slots),
        in_specs=[
            pl.BlockSpec(memory_space=pltpu.SMEM),
            pl.BlockSpec(memory_space=pltpu.VMEM),
            pl.BlockSpec(memory_space=pltpu.VMEM),
        ],
        out_specs=pl.BlockSpec(memory_space=pltpu.VMEM),
        out_shape=jax.ShapeDtypeStruct((CHIPS, 8, LANES), F32),
        scratch_shapes=[
            pltpu.VMEM((whole // 8, 8, D), BF16),
            pltpu.VMEM((whole // LANES + 8, LANES), I32),
            pltpu.VMEM((whole, LANES), I32),
            pltpu.VMEM((2, CHIPS, LANES), I32),
            pltpu.VMEM((half // LANES + 8, LANES), F32),
        ],
        compiler_params=params(),
        name="match",
    )(boxes, mine, other)
    back = lax.all_to_all(results, CHIP_AXES, 0, 0, tiled=True)
    return pl.pallas_call(
        result_kernel,
        out_shape=jax.ShapeDtypeStruct((1, ROWS), F32),
        compiler_params=params(),
        name="result",
    )(back, where)


def body(emb, home, member, rank):
    cl = home.reshape(1, ROWS) * MEMBERS + member.reshape(1, ROWS)
    rank = rank.reshape(1, ROWS)
    counts = pl.pallas_call(
        count_kernel,
        out_shape=jax.ShapeDtypeStruct((DEVICES, 8, LANES), BF16),
        compiler_params=params(),
        name="count",
    )(cl)
    counts = lax.all_to_all(counts, ALL_AXES, 0, 0, tiled=True).reshape(DEVICES * 8, LANES)
    unit = pl.pallas_call(
        unit_kernel,
        grid=(4,),
        in_specs=[pl.BlockSpec((ROWS // 4, D), lambda i: (i, 0))],
        out_specs=pl.BlockSpec((ROWS // 4, D), lambda i: (i, 0)),
        out_shape=jax.ShapeDtypeStruct((ROWS, D), BF16),
        compiler_params=params(),
        cost_estimate=pl.CostEstimate(flops=4 * ROWS * D, bytes_accessed=4 * ROWS * D, transcendentals=ROWS),
        name="unit",
    )(emb)
    chip = lax.axis_index("yx") * lax.axis_size("z") + lax.axis_index("z")
    place = jnp.stack([chip, lax.axis_index("core")]).astype(I32)
    asg, boxes, most = pl.pallas_call(
        assign_kernel,
        in_specs=[
            pl.BlockSpec(memory_space=pltpu.SMEM),
            pl.BlockSpec(memory_space=pltpu.VMEM),
        ],
        out_specs=[
            pl.BlockSpec(memory_space=pltpu.VMEM),
            pl.BlockSpec(memory_space=pltpu.VMEM),
            pl.BlockSpec(memory_space=pltpu.SMEM),
        ],
        out_shape=[
            jax.ShapeDtypeStruct((8, LANES), I32),
            jax.ShapeDtypeStruct((2, LANES), I32),
            jax.ShapeDtypeStruct((1,), I32),
        ],
        scratch_shapes=[
            pltpu.VMEM((CLUSTERS, LANES), F32),
            pltpu.VMEM((CLUSTERS, LANES), I32),
            pltpu.VMEM((DEVICES, LANES), F32),
        ],
        compiler_params=params(),
        name="assign",
    )(place, counts)
    out = lax.cond(
        most[0] < FAST,
        functools.partial(exchange, FAST),
        functools.partial(exchange, SLOW),
        asg,
        cl,
        rank,
        unit,
        boxes,
    )
    return out.reshape(ROWS)


def solution(mesh):
    chips = Mesh(mesh.devices.reshape(-1, 2, mesh.devices.shape[1]), ALL_AXES)
    rows = P(ALL_AXES)
    return jax.shard_map(
        body,
        mesh=chips,
        in_specs=(P(ALL_AXES, None), P(ALL_AXES, None), P(ALL_AXES, None), rows),
        out_specs=rows,
        check_vma=False,
    )
```

```python
import functools

import jax
import jax.numpy as jnp
from jax import lax
from jax.experimental import pallas as pl
from jax.experimental.pallas import tpu as pltpu
from jax.sharding import Mesh, PartitionSpec as P

D = 768
ROWS = 1024
CLUSTERS = 512
MEMBERS = 16
CHIPS = 64
DEVICES = 128
LANES = 128
PIECES = CLUSTERS // LANES
BATCH = 32
FAST = 32
SLOW = 72
GROUP = 8
QB = 512
KB = 1024
UNROLL = 32
EXTRA = 128
RANK_BITS = 17
VMEM_BYTES = 56 << 20
CHIP_AXES = ("yx", "z")
ALL_AXES = ("yx", "core", "z")
F32, BF16, I32 = jnp.float32, jnp.bfloat16, jnp.int32
NT = (((1,), (1,)), ((), ()))


def iota(shape, dim):
    return lax.broadcasted_iota(I32, shape, dim)


def dot(a, b):
    return jnp.dot(a, b, preferred_element_type=F32)


def dot_nt(a, b):
    return lax.dot_general(a, b, NT, preferred_element_type=F32)


def ones_where(mask):
    return jnp.where(mask, 1.0, 0.0).astype(BF16)


def params():
    return pltpu.CompilerParams(vmem_limit_bytes=VMEM_BYTES)


def count_kernel(home_ref, member_ref, rank_ref, ident_ref, out_ref):
    cl = home_ref[...] * MEMBERS + member_ref[...]
    ident_ref[...] = (cl << RANK_BITS) + rank_ref[...]
    ones = jnp.ones((8, ROWS), BF16)
    sub8 = iota((8, LANES), 0)
    tile = jnp.zeros((8, LANES), F32)
    for r in range(PIECES):
        hot = ones_where(cl == iota((LANES, ROWS), 0) + r * LANES)
        tile = jnp.where(sub8 == r, dot_nt(ones, hot), tile)
    out_ref[...] = jnp.broadcast_to(tile.astype(BF16)[None], out_ref.shape)


def normalized(values):
    mean = jnp.sum(values * values, axis=1, keepdims=True) * (1.0 / D)
    return (values * (lax.rsqrt(mean + 1e-06) * D ** (-0.5))).astype(BF16)


def unit_kernel(emb_ref, unit_ref):
    unit_ref[...] = normalized(emb_ref[...].astype(F32))


def assign_kernel(place_ref, counts_ref, asg_ref, boxes_ref, fast_ref, sizes, bins, pairs):
    chip, core = place_ref[0], place_ref[1]
    lane = iota((LANES, LANES), 1)
    sub = iota((LANES, LANES), 0)
    eye = lane == sub
    lane1 = iota((1, LANES), 1)
    flat = counts_ref[...]
    total = dot(ones_where(iota((8, DEVICES * 8), 1) % 8 == iota((8, DEVICES * 8), 0)), flat)
    tot = [total[r : r + 1, :] for r in range(PIECES)]
    key = [tot[r] * CLUSTERS + (CLUSTERS - 1 - r * LANES - lane1).astype(F32) for r in range(PIECES)]
    col = [jnp.sum(jnp.where(eye, key[r], 0.0), axis=1, keepdims=True) for r in range(PIECES)]
    pos = []
    for r in range(PIECES):
        above = jnp.zeros((LANES, LANES), F32)
        for q in range(PIECES):
            above = above + jnp.where(col[q] > key[r], 1.0, 0.0)
        pos.append(jnp.sum(above, axis=0, keepdims=True).astype(I32))
    for q in range(PIECES):
        here = jnp.zeros((LANES, LANES), F32)
        for r in range(PIECES):
            here = here + jnp.where(pos[r] == sub + q * LANES, tot[r], 0.0)
        sizes[q * LANES : (q + 1) * LANES, :] = jnp.broadcast_to(
            jnp.sum(here, axis=1, keepdims=True), (LANES, LANES)
        )
    lane_c = iota((CHIPS, LANES), 1)
    eye_c = lane_c == iota((CHIPS, LANES), 0)
    lane_b = iota((BATCH, LANES), 1)
    sub_b = iota((BATCH, LANES), 0)

    def one_batch(step, load):
        order = jnp.where(lane1 < CHIPS, load * CHIPS + lane1.astype(F32), 3.0e7)
        order_col = jnp.sum(jnp.where(eye_c, order, 0.0), axis=1, keepdims=True)
        place = jnp.sum(jnp.where(order_col < order, 1.0, 0.0), axis=0, keepdims=True).astype(I32)
        chosen = place == sub_b
        rows = pl.ds(pl.multiple_of(step * BATCH, BATCH), BATCH)
        bins[rows, :] = jnp.broadcast_to(
            jnp.sum(jnp.where(chosen, lane_b, 0), axis=1, keepdims=True), (BATCH, LANES)
        )
        return load + jnp.sum(jnp.where(chosen, sizes[rows, :], 0.0), axis=0, keepdims=True)

    lax.fori_loop(0, CLUSTERS // BATCH, one_batch, jnp.zeros((1, LANES), F32))
    asg = []
    for r in range(PIECES):
        found = jnp.zeros((LANES, LANES), I32)
        for q in range(PIECES):
            rows = bins[q * LANES : (q + 1) * LANES, :]
            found = found + jnp.where(pos[r] == sub + q * LANES, rows, 0)
        asg.append(jnp.sum(found, axis=0, keepdims=True))
    row8 = iota((DEVICES * 8, LANES), 0) % 8

    def pair_counts(table):
        per_row = jnp.zeros((DEVICES * 8, LANES), F32)
        for r in range(PIECES):
            per_row = jnp.where(row8 == r, dot_nt(flat, ones_where(table[r] == sub)), per_row)
        return jnp.sum(per_row.reshape(DEVICES, 8, LANES), axis=1)

    def put(table):
        sub8 = iota((8, LANES), 0)
        tile = jnp.zeros((8, LANES), I32)
        for r in range(PIECES):
            tile = jnp.where(sub8 == r, table[r], tile)
        asg_ref[...] = tile

    pairs[...] = pair_counts(asg)
    put(asg)
    device = iota((CHIPS, DEVICES), 1)
    both_cores = ones_where((device >> 3) * 4 + device % 4 == iota((CHIPS, DEVICES), 0))
    most = jnp.max(dot(both_cores, pairs[...].astype(BF16)))
    over = jnp.max(jnp.sum(jnp.maximum(pairs[...] - (FAST - 1), 0.0), axis=1, keepdims=True))
    fast = (most.astype(I32) <= 2 * (FAST - 1)) & (over.astype(I32) <= EXTRA)
    fast_ref[0] = fast.astype(I32)

    @pl.when(jnp.logical_not(fast))
    def _():
        fixed = []
        for r in range(PIECES):
            cluster = lane1 + r * LANES
            fixed.append((cluster // MEMBERS) * 2 + (cluster % MEMBERS) // 8)
        pairs[...] = pair_counts(fixed)
        put(fixed)

    mine = jnp.sum(jnp.where(lane == chip, pairs[...], 0.0), axis=1, keepdims=True)
    box = lane % CHIPS
    source_core = jnp.where(lane < CHIPS, core, 1 - core)

    def from_core(which):
        source = ((box // 4) * 2 + which) * 4 + box % 4
        return jnp.sum(jnp.where(sub == source, mine, 0.0), axis=0, keepdims=True).astype(I32)

    room = jnp.where(fast, FAST - 1, SLOW - 1)
    boxes = jnp.minimum(from_core(source_core), room)
    boxes = boxes + jnp.maximum(from_core(1 - source_core) - room, 0)
    rounded = (((boxes + 7) // 8) * 8).astype(F32).astype(BF16)
    boxes_ref[0:1, :] = boxes
    boxes_ref[1:2, :] = dot(rounded, ones_where(sub < lane)).astype(I32)


def label_pieces(ident):
    cl, rank = ident >> RANK_BITS, ident & ((1 << RANK_BITS) - 1)
    return rank >> 9, (rank >> 1) & 255, (rank & 1) + 2 * (cl >> 4), (cl & 15) + 1


def route_kernel(
    asg_ref, mine_ref, other_ref, unit_ref, emb2_ref, out_ref, where_ref, index, index2, labels, extra, *, slots
):
    group = pl.program_id(0)
    room = slots - 1

    @pl.when(group == 0)
    def _():
        sub = iota((CHIPS, LANES), 0)
        lane_sub = iota((LANES, ROWS), 0)
        before = ones_where(iota((LANES, LANES), 0) < iota((LANES, LANES), 1))
        chips_of, number_of, chip_of, sums = [], [], [], []
        for ident_ref in (mine_ref, other_ref):
            cl = ident_ref[...] >> RANK_BITS
            to_chip = jnp.zeros((CHIPS, ROWS), F32)
            for r in range(PIECES):
                hot = ones_where(cl == lane_sub + r * LANES)
                to_chip = to_chip + dot(ones_where(asg_ref[r : r + 1, :] == sub), hot)
            carry = jnp.zeros((CHIPS, 1), F32)
            number_parts, chip_parts = [], []
            for b in range(ROWS // LANES):
                part = to_chip[:, b * LANES : (b + 1) * LANES]
                earlier = dot(part.astype(BF16), before) + carry
                number_parts.append(jnp.sum(part * earlier, axis=0, keepdims=True))
                chip_parts.append(jnp.sum(part * sub.astype(F32), axis=0, keepdims=True))
                carry = carry + jnp.sum(part, axis=1, keepdims=True)
            chips_of.append(to_chip)
            number_of.append(jnp.concatenate(number_parts, axis=1).astype(I32))
            chip_of.append(jnp.concatenate(chip_parts, axis=1).astype(I32))
            sums.append(carry)
        taken = [
            jnp.sum(chips_of[half] * sums[1 - half], axis=0, keepdims=True).astype(I32) for half in range(2)
        ]
        spill = [taken[half] + number_of[half] - room for half in range(2)]
        stays = number_of[0] < room
        index[...] = jnp.where(stays, chip_of[0] * slots + number_of[0], -1)
        where_ref[0:1, :] = jnp.where(stays, chip_of[0], chip_of[0] + CHIPS)
        where_ref[1:2, :] = jnp.where(stays, number_of[0], spill[0])

        comes = jnp.where(number_of[1] >= room, 1.0, 0.0)
        carry = jnp.zeros((1, 1), F32)
        order_parts = []
        for b in range(ROWS // LANES):
            part = comes[:, b * LANES : (b + 1) * LANES]
            tile = jnp.broadcast_to(part, (8, LANES)).astype(BF16)
            order_parts.append(dot(tile, before)[0:1, :] + carry)
            carry = carry + jnp.sum(part, axis=1, keepdims=True)
        order = jnp.where(comes > 0.5, jnp.concatenate(order_parts, axis=1), -1.0).astype(I32)
        chosen = ones_where(order == lane_sub)
        zero = jnp.zeros((1, ROWS), I32)
        facts = label_pieces(other_ref[...]) + (chip_of[1], jnp.maximum(spill[1], 0), zero, zero)
        facts = dot_nt(jnp.concatenate(facts, axis=0).astype(F32).astype(BF16), chosen)
        came = facts[3:4, :] > 0.5
        chip2, slot2 = facts[4:5, :].astype(I32), facts[5:6, :].astype(I32)
        index2[...] = jnp.where(came, chip2 * slots + slot2, -1)
        extra[...] = normalized(dot(chosen, emb2_ref[...]))

        to_chip2 = jnp.where(came & (chip2 == sub), 1.0, 0.0)
        pieces = label_pieces(mine_ref[...])
        text = jnp.concatenate([chips_of[0] * piece.astype(F32) for piece in pieces], axis=0)
        text2 = jnp.concatenate([to_chip2 * facts[k : k + 1, :] for k in range(PIECES)], axis=0)
        slot_hot = ones_where(jnp.where(stays, number_of[0], -1) == lane_sub)
        slot_hot2 = ones_where(jnp.where(came, slot2, -1) == iota((LANES, LANES), 0))
        text = dot_nt(text.astype(BF16), slot_hot) + dot_nt(text2.astype(BF16), slot_hot2)
        for k in range(PIECES):
            labels[:, k * LANES : (k + 1) * LANES] = text[k * CHIPS : (k + 1) * CHIPS, :].astype(BF16)

    size = GROUP * slots
    first = group * size
    rows = dot(ones_where(index[...] == iota((size, ROWS), 0) + first), unit_ref[...])
    rows = rows + dot(ones_where(index2[...] == iota((size, EXTRA), 0) + first), extra[...])
    last = (iota((size, CHIPS), 1) - group * GROUP) * slots + slots - 1
    text = dot(ones_where(last == iota((size, CHIPS), 0)), labels[...])
    out_ref[:, : PIECES * LANES] = (rows[:, : PIECES * LANES] + text).astype(BF16)
    out_ref[:, PIECES * LANES :] = rows[:, PIECES * LANES :].astype(BF16)


def match_kernel(boxes_ref, mine_ref, other_ref, out_ref, keys, ids, columns, text, best, *, slots):
    tiles = slots // 8
    lane1 = iota((1, LANES), 1)
    n_mine = boxes_ref[1, CHIPS]
    n_all = boxes_ref[1, 2 * CHIPS - 1] + ((boxes_ref[0, 2 * CHIPS - 1] + 7) // 8) * 8
    ids[...] = jnp.full(ids.shape, -1, I32)
    label_row = ones_where(iota((CHIPS, CHIPS * 8), 1) == iota((CHIPS, CHIPS * 8), 0) * 8 + 7)
    for half, box_rows in enumerate((mine_ref, other_ref)):
        held = box_rows[:, tiles - 1, :, : PIECES * LANES].reshape(CHIPS * 8, PIECES * LANES)
        words = dot(label_row, held).astype(I32)
        high, low, mixed, filled = (words[:, k * LANES : (k + 1) * LANES] for k in range(PIECES))
        rank = (high << 9) + (low << 1) + (mixed & 1)
        cluster = ((mixed >> 1) << 4) + filled - 1
        text[half] = jnp.where(filled > 0, (cluster << 17) + rank, -1)

        def pack(b, carry, box_rows=box_rows, half=half):
            start = boxes_ref[1, half * CHIPS + b]
            keys[pl.ds(start // 8, tiles)] = box_rows[b]
            shift = lax.rem(start, LANES)
            row = start // LANES
            line = pltpu.roll(text[half, pl.ds(b, 1), :], shift, 1)
            ids[pl.ds(row, 1), :] = jnp.where(lane1 >= shift, line, ids[pl.ds(row, 1), :])
            ids[pl.ds(row + 1, 1), :] = jnp.where(lane1 < shift, line, -1)
            return carry

        lax.fori_loop(0, CHIPS, pack, 0, unroll=UNROLL)

    k_blocks = (n_all + KB - 1) // KB
    per_block = KB // LANES

    def column(k, carry):
        for r in range(per_block):
            line = jnp.broadcast_to(ids[pl.ds(k * per_block + r, 1), :], (LANES, LANES))
            rows = pl.ds(pl.multiple_of(k * KB + r * LANES, LANES), LANES)
            columns[rows, :] = jnp.transpose(line)
        return carry

    lax.fori_loop(0, k_blocks, column, 0)
    parts = QB // LANES

    def queries(q, carry):
        query = keys[pl.ds(q * (QB // 8), QB // 8)].reshape(QB, D)
        high = [ids[pl.ds(q * parts + p, 1), :] for p in range(parts)]
        low = [(h >> 17) << 17 for h in high]

        def key_block(k, acc):
            score = dot_nt(keys[pl.ds(k * (KB // 8), KB // 8)].reshape(KB, D), query)
            ident = columns[pl.ds(pl.multiple_of(k * KB, KB), KB), :]
            new = []
            for p in range(parts):
                piece = score[:, p * LANES : (p + 1) * LANES]
                valid = (ident >= low[p]) & (ident < high[p])
                piece = jnp.where(valid, piece, -1.0)
                new.append(jnp.maximum(acc[p], jnp.max(piece.reshape(KB // 8, 8, LANES), axis=0)))
            return tuple(new)

        acc = lax.fori_loop(0, k_blocks, key_block, (jnp.full((8, LANES), -1.0, F32),) * parts)
        for p in range(parts):
            best[pl.ds(q * parts + p, 1), :] = jnp.max(acc[p], axis=0, keepdims=True)
        return carry

    lax.fori_loop(0, (n_mine + QB - 1) // QB, queries, 0)
    sub8 = iota((8, LANES), 0)

    def unpack(b, carry):
        start = boxes_ref[1, b]
        shift = lax.rem(start, LANES)
        row = start // LANES
        two = jnp.where(lane1 >= shift, best[pl.ds(row, 1), :], best[pl.ds(row + 1, 1), :])
        line = pltpu.roll(two, lax.rem(LANES - shift, LANES), 1)
        line = jnp.where(lane1 < boxes_ref[0, b], line, 0.0)
        out_ref[b] = jnp.where(sub8 == 0, line, 0.0)
        return carry

    lax.fori_loop(0, CHIPS, unpack, 0, unroll=UNROLL)


def result_kernel(back_ref, back2_ref, where_ref, out_ref):
    table = jnp.concatenate([jnp.sum(back_ref[...], axis=1), jnp.sum(back2_ref[...], axis=1)], axis=0).T
    to_chip = jnp.where(where_ref[0:1, :] == iota((LANES, ROWS), 0), 1.0, 0.0)
    by_slot = jnp.dot(
        table, to_chip, preferred_element_type=F32, precision=lax.Precision.HIGHEST
    )
    picked = jnp.where(where_ref[1:2, :] == iota((LANES, ROWS), 0), by_slot, 0.0)
    out_ref[...] = jnp.sum(picked, axis=0, keepdims=True)


def swap(x):
    return lax.ppermute(x, "core", [(0, 1), (1, 0)])


def exchange(slots, asg, mine, other, unit, emb2, boxes):
    size = GROUP * slots
    outbox, where = pl.pallas_call(
        functools.partial(route_kernel, slots=slots),
        grid=(CHIPS // GROUP,),
        in_specs=[
            pl.BlockSpec((8, LANES), lambda g: (0, 0)),
            pl.BlockSpec((1, ROWS), lambda g: (0, 0)),
            pl.BlockSpec((1, ROWS), lambda g: (0, 0)),
            pl.BlockSpec((ROWS, D), lambda g: (0, 0)),
            pl.BlockSpec((ROWS, D), lambda g: (0, 0)),
        ],
        out_specs=[
            pl.BlockSpec((size, D), lambda g: (g, 0)),
            pl.BlockSpec((2, ROWS), lambda g: (0, 0)),
        ],
        out_shape=[
            jax.ShapeDtypeStruct((CHIPS * slots, D), BF16),
            jax.ShapeDtypeStruct((2, ROWS), I32),
        ],
        scratch_shapes=[
            pltpu.VMEM((1, ROWS), I32),
            pltpu.VMEM((1, EXTRA), I32),
            pltpu.VMEM((CHIPS, PIECES * LANES), BF16),
            pltpu.VMEM((EXTRA, D), BF16),
        ],
        compiler_params=params(),
        name="route",
    )(asg, mine, other, unit, emb2)
    mine = lax.all_to_all(outbox.reshape(CHIPS, slots, D), CHIP_AXES, 0, 0, tiled=True)
    mine = mine.reshape(CHIPS, slots // 8, 8, D)
    other = swap(mine)
    whole = -(-(2 * CHIPS * slots + slots) // KB) * KB + KB
    half = -(-(CHIPS * slots) // QB) * QB + QB
    results = pl.pallas_call(
        functools.partial(match_kernel, slots=slots),
        in_specs=[
            pl.BlockSpec(memory_space=pltpu.SMEM),
            pl.BlockSpec(memory_space=pltpu.VMEM),
            pl.BlockSpec(memory_space=pltpu.VMEM),
        ],
        out_specs=pl.BlockSpec(memory_space=pltpu.VMEM),
        out_shape=jax.ShapeDtypeStruct((CHIPS, 8, LANES), F32),
        scratch_shapes=[
            pltpu.VMEM((whole // 8, 8, D), BF16),
            pltpu.VMEM((whole // LANES + 8, LANES), I32),
            pltpu.VMEM((whole, LANES), I32),
            pltpu.VMEM((2, CHIPS, LANES), I32),
            pltpu.VMEM((half // LANES + 8, LANES), F32),
        ],
        compiler_params=params(),
        name="match",
    )(boxes, mine, other)
    back = lax.all_to_all(results, CHIP_AXES, 0, 0, tiled=True)
    return pl.pallas_call(
        result_kernel,
        out_shape=jax.ShapeDtypeStruct((1, ROWS), F32),
        compiler_params=params(),
        name="result",
    )(back, swap(back), where)


def unit_rows(emb):
    return pl.pallas_call(
        unit_kernel,
        grid=(4,),
        in_specs=[pl.BlockSpec((ROWS // 4, D), lambda i: (i, 0))],
        out_specs=pl.BlockSpec((ROWS // 4, D), lambda i: (i, 0)),
        out_shape=jax.ShapeDtypeStruct((ROWS, D), BF16),
        compiler_params=params(),
        cost_estimate=pl.CostEstimate(flops=4 * ROWS * D, bytes_accessed=4 * ROWS * D, transcendentals=ROWS),
        name="unit",
    )(emb)


def body(emb, home, member, rank):
    emb2 = swap(emb)
    mine, counts = pl.pallas_call(
        count_kernel,
        out_shape=[
            jax.ShapeDtypeStruct((1, ROWS), I32),
            jax.ShapeDtypeStruct((DEVICES, 8, LANES), BF16),
        ],
        compiler_params=params(),
        name="count",
    )(home.reshape(1, ROWS), member.reshape(1, ROWS), rank.reshape(1, ROWS))
    other = swap(mine)
    counts = lax.all_to_all(counts, ALL_AXES, 0, 0, tiled=True).reshape(DEVICES * 8, LANES)
    unit = unit_rows(emb)
    chip = lax.axis_index("yx") * lax.axis_size("z") + lax.axis_index("z")
    place = jnp.stack([chip, lax.axis_index("core")]).astype(I32)
    asg, boxes, fast = pl.pallas_call(
        assign_kernel,
        in_specs=[
            pl.BlockSpec(memory_space=pltpu.SMEM),
            pl.BlockSpec(memory_space=pltpu.VMEM),
        ],
        out_specs=[
            pl.BlockSpec(memory_space=pltpu.VMEM),
            pl.BlockSpec(memory_space=pltpu.VMEM),
            pl.BlockSpec(memory_space=pltpu.SMEM),
        ],
        out_shape=[
            jax.ShapeDtypeStruct((8, LANES), I32),
            jax.ShapeDtypeStruct((2, LANES), I32),
            jax.ShapeDtypeStruct((1,), I32),
        ],
        scratch_shapes=[
            pltpu.VMEM((CLUSTERS, LANES), F32),
            pltpu.VMEM((CLUSTERS, LANES), I32),
            pltpu.VMEM((DEVICES, LANES), F32),
        ],
        compiler_params=params(),
        name="assign",
    )(place, counts)
    out = lax.cond(
        fast[0] == 1,
        functools.partial(exchange, FAST),
        functools.partial(exchange, SLOW),
        asg,
        mine,
        other,
        unit,
        emb2,
        boxes,
    )
    return out.reshape(ROWS)


def solution(mesh):
    chips = Mesh(mesh.devices.reshape(-1, 2, mesh.devices.shape[1]), ALL_AXES)
    rows = P(ALL_AXES)
    return jax.shard_map(
        body,
        mesh=chips,
        in_specs=(P(ALL_AXES, None), P(ALL_AXES, None), P(ALL_AXES, None), rows),
        out_specs=rows,
        check_vma=False,
    )
```

```python
import functools

import jax
import jax.numpy as jnp
from jax import lax
from jax.experimental import pallas as pl
from jax.experimental.pallas import tpu as pltpu
from jax.sharding import Mesh, PartitionSpec as P

D = 768
ROWS = 1024
CLUSTERS = 512
MEMBERS = 16
CHIPS = 64
DEVICES = 128
LANES = 128
PIECES = CLUSTERS // LANES
BATCH = 32
FAST = 32
SLOW = 72
GROUP = 16
QB = 512
KB = 768
UNROLL = 32
CHUNK = 16
EXTRA = 128
PARTS = ROWS // LANES
RANK_BITS = 17
CHIP_AXES = ("yx", "z")
ALL_AXES = ("yx", "core", "z")
F32, BF16, I32 = jnp.float32, jnp.bfloat16, jnp.int32
NT = (((1,), (1,)), ((), ()))


def iota(shape, dim):
    return lax.broadcasted_iota(I32, shape, dim)


def dot(a, b):
    return jnp.dot(a, b, preferred_element_type=F32)


def dot_nt(a, b):
    return lax.dot_general(a, b, NT, preferred_element_type=F32)


def ones_where(mask):
    return jnp.where(mask, 1.0, 0.0).astype(BF16)


def params(mib=16):
    return pltpu.CompilerParams(vmem_limit_bytes=mib << 20)


def count_kernel(home_ref, member_ref, rank_ref, ident_ref, out_ref):
    cl = home_ref[...] * MEMBERS + member_ref[...]
    ident_ref[...] = (cl << RANK_BITS) + rank_ref[...]
    sub = iota((LANES, LANES), 0)
    sub8 = iota((8, LANES), 0)
    tile = jnp.zeros((8, LANES), F32)
    for r in range(PIECES):
        found = jnp.zeros((LANES, LANES), F32)
        for b in range(PARTS):
            found = found + jnp.where(cl[b : b + 1, :] == sub + r * LANES, 1.0, 0.0)
        tile = jnp.where(sub8 == r, dot_nt(jnp.ones((8, LANES), BF16), found.astype(BF16)), tile)
    out_ref[...] = jnp.broadcast_to(tile.astype(BF16)[None], out_ref.shape)


def normalized(values):
    mean = jnp.sum(values * values, axis=1, keepdims=True) * (1.0 / D)
    return (values * (lax.rsqrt(mean + 1e-06) * D ** (-0.5))).astype(BF16)


def unit_kernel(emb_ref, unit_ref):
    unit_ref[...] = normalized(emb_ref[...].astype(F32))


def assign_kernel(place_ref, counts_ref, asg_ref, boxes_ref, fast_ref, sizes, bins, pairs):
    chip, core = place_ref[0], place_ref[1]
    lane = iota((LANES, LANES), 1)
    sub = iota((LANES, LANES), 0)
    eye = lane == sub
    lane1 = iota((1, LANES), 1)
    flat = counts_ref[...]
    total = dot(ones_where(iota((8, DEVICES * 8), 1) % 8 == iota((8, DEVICES * 8), 0)), flat)
    tot = [total[r : r + 1, :] for r in range(PIECES)]
    key = [tot[r] * CLUSTERS + (CLUSTERS - 1 - r * LANES - lane1).astype(F32) for r in range(PIECES)]
    col = [jnp.sum(jnp.where(eye, key[r], 0.0), axis=1, keepdims=True) for r in range(PIECES)]
    pos = []
    for r in range(PIECES):
        above = jnp.zeros((LANES, LANES), F32)
        for q in range(PIECES):
            above = above + jnp.where(col[q] > key[r], 1.0, 0.0)
        pos.append(jnp.sum(above, axis=0, keepdims=True).astype(I32))
    for q in range(PIECES):
        here = jnp.zeros((LANES, LANES), F32)
        for r in range(PIECES):
            here = here + jnp.where(pos[r] == sub + q * LANES, tot[r], 0.0)
        sizes[q * LANES : (q + 1) * LANES, :] = jnp.broadcast_to(
            jnp.sum(here, axis=1, keepdims=True), (LANES, LANES)
        )
    lane_c = iota((CHIPS, LANES), 1)
    eye_c = lane_c == iota((CHIPS, LANES), 0)
    lane_b = iota((BATCH, LANES), 1)
    sub_b = iota((BATCH, LANES), 0)

    def one_batch(step, load):
        order = jnp.where(lane1 < CHIPS, load * CHIPS + lane1.astype(F32), 3.0e7)
        order_col = jnp.sum(jnp.where(eye_c, order, 0.0), axis=1, keepdims=True)
        place = jnp.sum(jnp.where(order_col < order, 1.0, 0.0), axis=0, keepdims=True).astype(I32)
        chosen = place == sub_b
        rows = pl.ds(pl.multiple_of(step * BATCH, BATCH), BATCH)
        bins[rows, :] = jnp.broadcast_to(
            jnp.sum(jnp.where(chosen, lane_b, 0), axis=1, keepdims=True), (BATCH, LANES)
        )
        return load + jnp.sum(jnp.where(chosen, sizes[rows, :], 0.0), axis=0, keepdims=True)

    lax.fori_loop(0, CLUSTERS // BATCH, one_batch, jnp.zeros((1, LANES), F32))
    asg = []
    for r in range(PIECES):
        found = jnp.zeros((LANES, LANES), I32)
        for q in range(PIECES):
            rows = bins[q * LANES : (q + 1) * LANES, :]
            found = found + jnp.where(pos[r] == sub + q * LANES, rows, 0)
        asg.append(jnp.sum(found, axis=0, keepdims=True))
    row8 = iota((DEVICES * 8, LANES), 0) % 8

    def pair_counts(table):
        per_row = jnp.zeros((DEVICES * 8, LANES), F32)
        for r in range(PIECES):
            per_row = jnp.where(row8 == r, dot_nt(flat, ones_where(table[r] == sub)), per_row)
        return jnp.sum(per_row.reshape(DEVICES, 8, LANES), axis=1)

    def put(table):
        sub8 = iota((8, LANES), 0)
        tile = jnp.zeros((8, LANES), I32)
        for r in range(PIECES):
            tile = jnp.where(sub8 == r, table[r], tile)
        asg_ref[...] = tile

    pairs[...] = pair_counts(asg)
    put(asg)
    device = iota((CHIPS, DEVICES), 1)
    both_cores = ones_where((device >> 3) * 4 + device % 4 == iota((CHIPS, DEVICES), 0))
    most = jnp.max(dot(both_cores, pairs[...].astype(BF16)))
    over = jnp.max(jnp.sum(jnp.maximum(pairs[...] - (FAST - 1), 0.0), axis=1, keepdims=True))
    fast = (most.astype(I32) <= 2 * (FAST - 1)) & (over.astype(I32) <= EXTRA)
    fast_ref[0] = fast.astype(I32)

    @pl.when(jnp.logical_not(fast))
    def _():
        fixed = []
        for r in range(PIECES):
            cluster = lane1 + r * LANES
            fixed.append((cluster // MEMBERS) * 2 + (cluster % MEMBERS) // 8)
        pairs[...] = pair_counts(fixed)
        put(fixed)

    mine = jnp.sum(jnp.where(lane == chip, pairs[...], 0.0), axis=1, keepdims=True)
    box = lane % CHIPS
    source_core = jnp.where(lane < CHIPS, core, 1 - core)

    def from_core(which):
        source = ((box // 4) * 2 + which) * 4 + box % 4
        return jnp.sum(jnp.where(sub == source, mine, 0.0), axis=0, keepdims=True).astype(I32)

    room = jnp.where(fast, FAST - 1, SLOW - 1)
    boxes = jnp.minimum(from_core(source_core), room)
    boxes = boxes + jnp.maximum(from_core(1 - source_core) - room, 0)
    rounded = (((boxes + 7) // 8) * 8).astype(F32).astype(BF16)
    boxes_ref[0:1, :] = boxes
    earlier = (sub < lane) & (sub // CHIPS == lane // CHIPS)
    boxes_ref[1:2, :] = dot(rounded, ones_where(earlier)).astype(I32)


def label_pieces(ident):
    cl, rank = ident >> RANK_BITS, ident & ((1 << RANK_BITS) - 1)
    return rank >> 9, (rank >> 1) & 255, (rank & 1) + 2 * (cl >> 4), (cl & 15) + 1


def route_kernel(
    asg_ref, mine_ref, other_ref, unit_ref, emb2_ref, out_ref, where_ref, index, index2, labels, extra, *, slots
):
    group = pl.program_id(0)
    room = slots - 1

    @pl.when(group == 0)
    def _():
        sub = iota((CHIPS, LANES), 0)
        lane_sub = iota((LANES, LANES), 0)
        before = ones_where(lane_sub < iota((LANES, LANES), 1))
        chip_of, chips_of, number_of, sums = [], [], [], []
        for ident_ref in (mine_ref, other_ref):
            cl = ident_ref[...] >> RANK_BITS
            chip = jnp.zeros((PARTS, LANES), I32)
            for r in range(PIECES):
                table = jnp.broadcast_to(asg_ref[r : r + 1, :], (PARTS, LANES))
                found = jnp.take_along_axis(table, cl & (LANES - 1), axis=1, mode="promise_in_bounds")
                chip = jnp.where((cl >> 7) == r, found, chip)
            to_chip = [jnp.where(chip[b : b + 1, :] == sub, 1.0, 0.0) for b in range(PARTS)]
            earlier = dot(jnp.concatenate(to_chip, axis=0).astype(BF16), before)
            carry = jnp.zeros((CHIPS, 1), F32)
            rows = []
            for b in range(PARTS):
                until = earlier[b * CHIPS : (b + 1) * CHIPS, :] + carry
                rows.append(jnp.sum(to_chip[b] * until, axis=0, keepdims=True))
                carry = carry + jnp.sum(to_chip[b], axis=1, keepdims=True)
            chip_of.append(chip)
            chips_of.append(to_chip)
            number_of.append(jnp.concatenate(rows, axis=0).astype(I32))
            sums.append(carry)
        spill = []
        for half in range(2):
            taken = [jnp.sum(part * sums[1 - half], axis=0, keepdims=True) for part in chips_of[half]]
            spill.append(jnp.concatenate(taken, axis=0).astype(I32) + number_of[half] - room)
        stays = number_of[0] < room
        target = jnp.where(stays, chip_of[0] * slots + number_of[0], -1)
        back_chip = jnp.where(stays, chip_of[0], chip_of[0] + CHIPS)
        back_slot = jnp.where(stays, number_of[0], spill[0])
        for b in range(PARTS):
            at = slice(b * LANES, (b + 1) * LANES)
            index[:, at] = target[b : b + 1, :]
            where_ref[0:1, at] = back_chip[b : b + 1, :]
            where_ref[1:2, at] = back_slot[b : b + 1, :]

        comes = jnp.where(number_of[1] >= room, 1.0, 0.0)
        within = dot(comes.astype(BF16), before)
        carry = jnp.zeros((1, 1), F32)
        chosen, zero = [], jnp.zeros((1, LANES), I32)
        pieces2 = label_pieces(other_ref[...]) + (chip_of[1], jnp.maximum(spill[1], 0))
        facts = jnp.zeros((8, LANES), F32)
        for b in range(PARTS):
            part = comes[b : b + 1, :]
            order = jnp.where(part > 0.5, within[b : b + 1, :] + carry, -1.0).astype(I32)
            carry = carry + jnp.sum(part, axis=1, keepdims=True)
            chosen.append(ones_where(order == lane_sub))
            lines = [piece[b : b + 1, :] for piece in pieces2] + [zero, zero]
            facts = facts + dot_nt(jnp.concatenate(lines, axis=0).astype(F32).astype(BF16), chosen[b])
        chosen = jnp.concatenate(chosen, axis=1)
        came = facts[3:4, :] > 0.5
        chip2, slot2 = facts[4:5, :].astype(I32), facts[5:6, :].astype(I32)
        index2[...] = jnp.where(came, chip2 * slots + slot2, -1)
        extra[...] = normalized(dot(chosen, emb2_ref[...]))

        to_chip2 = jnp.where(came & (chip2 == sub), 1.0, 0.0)
        pieces = label_pieces(mine_ref[...])
        text, slot_hot = [], []
        held = jnp.where(stays, number_of[0], -1)
        for b in range(PARTS):
            lines = [chips_of[0][b] * piece[b : b + 1, :].astype(F32) for piece in pieces]
            text.append(jnp.concatenate(lines, axis=0).astype(BF16))
            slot_hot.append(ones_where(held[b : b + 1, :] == lane_sub))
        text, slot_hot = jnp.concatenate(text, axis=1), jnp.concatenate(slot_hot, axis=1)
        text2 = jnp.concatenate([to_chip2 * facts[k : k + 1, :] for k in range(PIECES)], axis=0)
        slot_hot2 = ones_where(jnp.where(came, slot2, -1) == lane_sub)
        text = dot_nt(text, slot_hot) + dot_nt(text2.astype(BF16), slot_hot2)
        for k in range(PIECES):
            labels[:, k * LANES : (k + 1) * LANES] = text[k * CHIPS : (k + 1) * CHIPS, :].astype(BF16)

    size = GROUP * slots
    first = group * size
    rows = dot(ones_where(index[...] == iota((size, ROWS), 0) + first), unit_ref[...])
    rows = rows + dot(ones_where(index2[...] == iota((size, EXTRA), 0) + first), extra[...])
    last = (iota((size, CHIPS), 1) - group * GROUP) * slots + slots - 1
    text = dot(ones_where(last == iota((size, CHIPS), 0)), labels[...])
    out_ref[:, : PIECES * LANES] = (rows[:, : PIECES * LANES] + text).astype(BF16)
    out_ref[:, PIECES * LANES :] = rows[:, PIECES * LANES :].astype(BF16)


def pack_boxes(boxes_ref, held_boxes, box_rows, sems, keys, ids, columns, text, half, tiles):
    copies = []
    for c in range(CHIPS // CHUNK):
        some = pl.ds(c * CHUNK, CHUNK)
        copies.append(pltpu.make_async_copy(held_boxes.at[some], box_rows.at[some], sems.at[c]))
        copies[c].start()
    lane1 = iota((1, LANES), 1)
    ids[...] = jnp.full(ids.shape, -1, I32)
    label_row = ones_where(iota((CHUNK, CHUNK * 8), 1) == iota((CHUNK, CHUNK * 8), 0) * 8 + 7)
    for c in range(CHIPS // CHUNK):
        copies[c].wait()
        first = c * CHUNK
        held = box_rows[first : first + CHUNK, tiles - 1, :, : PIECES * LANES]
        words = dot(label_row, held.reshape(CHUNK * 8, PIECES * LANES)).astype(I32)
        high, low, mixed, filled = (words[:, k * LANES : (k + 1) * LANES] for k in range(PIECES))
        rank = (high << 9) + (low << 1) + (mixed & 1)
        cluster = ((mixed >> 1) << 4) + filled - 1
        text[first : first + CHUNK, :] = jnp.where(filled > 0, (cluster << RANK_BITS) + rank, -1)

        def pack(i, carry, first=first):
            b = first + i
            start = boxes_ref[1, half * CHIPS + b]
            keys[pl.ds(start // 8, tiles)] = box_rows[b]
            shift = lax.rem(start, LANES)
            row = start // LANES
            line = pltpu.roll(text[pl.ds(b, 1), :], shift, 1)
            ids[pl.ds(row, 1), :] = jnp.where(lane1 >= shift, line, ids[pl.ds(row, 1), :])
            ids[pl.ds(row + 1, 1), :] = jnp.where(lane1 < shift, line, -1)
            return carry

        lax.fori_loop(0, CHUNK, pack, 0, unroll=CHUNK)
    end = half * CHIPS + CHIPS - 1
    count = boxes_ref[1, end] + ((boxes_ref[0, end] + 7) // 8) * 8
    per_block = KB // LANES

    def column(k, carry):
        for r in range(per_block):
            line = jnp.broadcast_to(ids[pl.ds(k * per_block + r, 1), :], (LANES, LANES))
            rows = pl.ds(pl.multiple_of(k * KB + r * LANES, LANES), LANES)
            columns[rows, :] = jnp.transpose(line)
        return carry

    lax.fori_loop(0, (count + KB - 1) // KB, column, 0)
    return count


def compare(queries, q_ids, n_queries, keys, columns, n_keys, first, finish):
    parts = QB // LANES

    def block(q, carry):
        query = queries[pl.ds(q * (QB // 8), QB // 8)].reshape(QB, D)
        high = [q_ids[pl.ds(q * parts + p, 1), :] for p in range(parts)]
        low = [(h >> RANK_BITS) << RANK_BITS for h in high]

        def key_block(k, acc):
            score = dot_nt(keys[pl.ds(k * (KB // 8), KB // 8)].reshape(KB, D), query)
            ident = columns[pl.ds(pl.multiple_of(k * KB, KB), KB), :]
            new = []
            for p in range(parts):
                piece = score[:, p * LANES : (p + 1) * LANES]
                valid = (ident >= low[p]) & (ident < high[p])
                piece = jnp.where(valid, piece, -1.0)
                new.append(jnp.maximum(acc[p], jnp.max(piece.reshape(KB // 8, 8, LANES), axis=0)))
            return tuple(new)

        acc = tuple(first(q * parts + p) for p in range(parts))
        acc = lax.fori_loop(0, (n_keys + KB - 1) // KB, key_block, acc)
        for p in range(parts):
            finish(q * parts + p, acc[p])
        return carry

    lax.fori_loop(0, (n_queries + QB - 1) // QB, block, 0)


def own_kernel(
    boxes_ref, mine_ref, keys_ref, ids, most_ref, columns, text, box_rows, keys, sems, keys_sem, *, slots
):
    count = pack_boxes(boxes_ref, mine_ref, box_rows, sems, keys, ids, columns, text, 0, slots // 8)
    kept = pltpu.make_async_copy(keys, keys_ref, keys_sem)
    kept.start()

    def finish(p, acc):
        most_ref[p] = acc

    compare(keys, ids, count, keys, columns, count, lambda p: jnp.full((8, LANES), -1.0, F32), finish)
    kept.wait()


def other_kernel(
    boxes_ref, other_ref, queries_ref, q_ids, most_ref, out_ref, columns, text, box_rows, keys, sems, keys_sem,
    queries, ids, best, *, slots
):
    asked = pltpu.make_async_copy(queries_ref, queries, keys_sem)
    asked.start()
    count = pack_boxes(boxes_ref, other_ref, box_rows, sems, keys, ids, columns, text, 1, slots // 8)
    asked.wait()
    n_queries = boxes_ref[1, CHIPS - 1] + ((boxes_ref[0, CHIPS - 1] + 7) // 8) * 8

    def finish(p, acc):
        best[pl.ds(p, 1), :] = jnp.max(acc, axis=0, keepdims=True)

    compare(queries, q_ids, n_queries, keys, columns, count, lambda p: most_ref[p], finish)
    lane1 = iota((1, LANES), 1)
    sub8 = iota((8, LANES), 0)

    def unpack(b, carry):
        start = boxes_ref[1, b]
        shift = lax.rem(start, LANES)
        row = start // LANES
        two = jnp.where(lane1 >= shift, best[pl.ds(row, 1), :], best[pl.ds(row + 1, 1), :])
        line = pltpu.roll(two, lax.rem(LANES - shift, LANES), 1)
        line = jnp.where(lane1 < boxes_ref[0, b], line, 0.0)
        out_ref[b] = jnp.where(sub8 == 0, line, 0.0)
        return carry

    lax.fori_loop(0, CHIPS, unpack, 0, unroll=UNROLL)


def result_kernel(back_ref, back2_ref, where_ref, out_ref):
    table = jnp.concatenate([jnp.sum(back_ref[...], axis=1), jnp.sum(back2_ref[...], axis=1)], axis=0).T
    to_chip = jnp.where(where_ref[0:1, :] == iota((LANES, ROWS), 0), 1.0, 0.0)
    by_slot = jnp.dot(
        table, to_chip, preferred_element_type=F32, precision=lax.Precision.HIGHEST
    )
    picked = jnp.where(where_ref[1:2, :] == iota((LANES, ROWS), 0), by_slot, 0.0)
    out_ref[...] = jnp.sum(picked, axis=0, keepdims=True)


def swap(x):
    return lax.ppermute(x, "core", [(0, 1), (1, 0)])


def exchange(slots, asg, mine, other, unit, emb2, boxes):
    size = GROUP * slots
    big = 28 if slots == FAST else 44
    outbox, where = pl.pallas_call(
        functools.partial(route_kernel, slots=slots),
        grid=(CHIPS // GROUP,),
        in_specs=[
            pl.BlockSpec((8, LANES), lambda g: (0, 0)),
            pl.BlockSpec((PARTS, LANES), lambda g: (0, 0)),
            pl.BlockSpec((PARTS, LANES), lambda g: (0, 0)),
            pl.BlockSpec((ROWS, D), lambda g: (0, 0)),
            pl.BlockSpec((ROWS, D), lambda g: (0, 0)),
        ],
        out_specs=[
            pl.BlockSpec((size, D), lambda g: (g, 0)),
            pl.BlockSpec((2, ROWS), lambda g: (0, 0)),
        ],
        out_shape=[
            jax.ShapeDtypeStruct((CHIPS * slots, D), BF16),
            jax.ShapeDtypeStruct((2, ROWS), I32),
        ],
        scratch_shapes=[
            pltpu.VMEM((1, ROWS), I32),
            pltpu.VMEM((1, EXTRA), I32),
            pltpu.VMEM((CHIPS, PIECES * LANES), BF16),
            pltpu.VMEM((EXTRA, D), BF16),
        ],
        compiler_params=params(big),
        name="route",
    )(asg, mine, other, unit, emb2)
    mine = lax.all_to_all(outbox.reshape(CHIPS, slots, D), CHIP_AXES, 0, 0, tiled=True)
    mine = mine.reshape(CHIPS, slots // 8, 8, D)
    other = swap(mine)
    n_rows = CHIPS * slots
    q_rows, k_rows = -(-n_rows // QB) * QB, -(-n_rows // KB) * KB
    n_keys = max(q_rows, k_rows)
    n_ids = n_keys // LANES + 8
    vmem = pl.BlockSpec(memory_space=pltpu.VMEM)
    smem = pl.BlockSpec(memory_space=pltpu.SMEM)
    hbm = pl.BlockSpec(memory_space=pl.ANY)
    keys = jax.ShapeDtypeStruct((n_keys // 8, 8, D), BF16)
    ids = jax.ShapeDtypeStruct((n_ids, LANES), I32)
    most = jax.ShapeDtypeStruct((q_rows // LANES, 8, LANES), F32)
    scratch = [
        pltpu.VMEM((k_rows, LANES), I32),
        pltpu.VMEM((CHIPS, LANES), I32),
        pltpu.VMEM((CHIPS, slots // 8, 8, D), BF16),
        pltpu.VMEM(keys.shape, BF16),
        pltpu.SemaphoreType.DMA((CHIPS // CHUNK,)),
        pltpu.SemaphoreType.DMA,
    ]
    own = pl.pallas_call(
        functools.partial(own_kernel, slots=slots),
        in_specs=[smem, hbm],
        out_specs=[hbm, vmem, vmem],
        out_shape=[keys, ids, most],
        scratch_shapes=scratch,
        compiler_params=params(big),
        cost_estimate=pl.CostEstimate(flops=8 * 10**9, bytes_accessed=4 * n_rows * D, transcendentals=0),
        name="own",
    )(boxes, mine)
    results = pl.pallas_call(
        functools.partial(other_kernel, slots=slots),
        in_specs=[smem, hbm, hbm, vmem, vmem],
        out_specs=vmem,
        out_shape=jax.ShapeDtypeStruct((CHIPS, 8, LANES), F32),
        scratch_shapes=scratch
        + [
            pltpu.VMEM(keys.shape, BF16),
            pltpu.VMEM(ids.shape, I32),
            pltpu.VMEM((q_rows // LANES + 8, LANES), F32),
        ],
        compiler_params=params(big),
        name="other",
    )(boxes, other, *own)
    back = lax.all_to_all(results, CHIP_AXES, 0, 0, tiled=True)
    return pl.pallas_call(
        result_kernel,
        out_shape=jax.ShapeDtypeStruct((1, ROWS), F32),
        compiler_params=params(),
        name="result",
    )(back, swap(back), where)


def unit_rows(emb):
    return pl.pallas_call(
        unit_kernel,
        grid=(4,),
        in_specs=[pl.BlockSpec((ROWS // 4, D), lambda i: (i, 0))],
        out_specs=pl.BlockSpec((ROWS // 4, D), lambda i: (i, 0)),
        out_shape=jax.ShapeDtypeStruct((ROWS, D), BF16),
        compiler_params=params(),
        cost_estimate=pl.CostEstimate(flops=4 * ROWS * D, bytes_accessed=4 * ROWS * D, transcendentals=ROWS),
        name="unit",
    )(emb)


def body(emb, home, member, rank):
    emb2 = swap(emb)
    mine, counts = pl.pallas_call(
        count_kernel,
        out_shape=[
            jax.ShapeDtypeStruct((PARTS, LANES), I32),
            jax.ShapeDtypeStruct((DEVICES, 8, LANES), BF16),
        ],
        compiler_params=params(56),
        name="count",
    )(*(x.reshape(PARTS, LANES) for x in (home, member, rank)))
    other = swap(mine)
    counts = lax.all_to_all(counts, ALL_AXES, 0, 0, tiled=True).reshape(DEVICES * 8, LANES)
    unit = unit_rows(emb)
    chip = lax.axis_index("yx") * lax.axis_size("z") + lax.axis_index("z")
    place = jnp.stack([chip, lax.axis_index("core")]).astype(I32)
    asg, boxes, fast = pl.pallas_call(
        assign_kernel,
        in_specs=[
            pl.BlockSpec(memory_space=pltpu.SMEM),
            pl.BlockSpec(memory_space=pltpu.VMEM),
        ],
        out_specs=[
            pl.BlockSpec(memory_space=pltpu.VMEM),
            pl.BlockSpec(memory_space=pltpu.VMEM),
            pl.BlockSpec(memory_space=pltpu.SMEM),
        ],
        out_shape=[
            jax.ShapeDtypeStruct((8, LANES), I32),
            jax.ShapeDtypeStruct((2, LANES), I32),
            jax.ShapeDtypeStruct((1,), I32),
        ],
        scratch_shapes=[
            pltpu.VMEM((CLUSTERS, LANES), F32),
            pltpu.VMEM((CLUSTERS, LANES), I32),
            pltpu.VMEM((DEVICES, LANES), F32),
        ],
        compiler_params=params(),
        name="assign",
    )(place, counts)
    out = lax.cond(
        fast[0] == 1,
        functools.partial(exchange, FAST),
        functools.partial(exchange, SLOW),
        asg,
        mine,
        other,
        unit,
        emb2,
        boxes,
    )
    return out.reshape(ROWS)


def solution(mesh):
    chips = Mesh(mesh.devices.reshape(-1, 2, mesh.devices.shape[1]), ALL_AXES)
    rows = P(ALL_AXES)
    return jax.shard_map(
        body,
        mesh=chips,
        in_specs=(P(ALL_AXES, None), P(ALL_AXES, None), P(ALL_AXES, None), rows),
        out_specs=rows,
        check_vma=False,
    )
```

```python
import functools

import jax
import jax.numpy as jnp
from jax import lax
from jax.experimental import pallas as pl
from jax.experimental.pallas import tpu as pltpu
from jax.sharding import Mesh, PartitionSpec as P

D = 768
ROWS = 1024
CLUSTERS = 512
MEMBERS = 16
CHIPS = 64
DEVICES = 128
LANES = 128
PIECES = CLUSTERS // LANES
BATCH = 32
FAST = 32
SLOW = 72
GROUP = 32
QB = 512
KB = 768
UNROLL = 32
CHUNK = 16
EXTRA = 128
PARTS = ROWS // LANES
RANK_BITS = 17
CHIP_AXES = ("yx", "z")
ALL_AXES = ("yx", "core", "z")
F32, BF16, I32, U32 = jnp.float32, jnp.bfloat16, jnp.int32, jnp.uint32
NT = (((1,), (1,)), ((), ()))


def iota(shape, dim):
    return lax.broadcasted_iota(I32, shape, dim)


def dot(a, b):
    return jnp.dot(a, b, preferred_element_type=F32)


def dot_nt(a, b):
    return lax.dot_general(a, b, NT, preferred_element_type=F32)


def ones_where(mask):
    return jnp.where(mask, 1.0, 0.0).astype(BF16)


def params(mib=16):
    return pltpu.CompilerParams(vmem_limit_bytes=mib << 20)


def count_kernel(home_ref, member_ref, rank_ref, ident_ref, out_ref):
    cl = home_ref[...] * MEMBERS + member_ref[...]
    ident_ref[...] = (cl << RANK_BITS) + rank_ref[...]
    sub = iota((LANES, LANES), 0)
    sub8 = iota((8, LANES), 0)
    tile = jnp.zeros((8, LANES), F32)
    for r in range(PIECES):
        found = jnp.zeros((LANES, LANES), F32)
        for b in range(PARTS):
            found = found + jnp.where(cl[b : b + 1, :] == sub + r * LANES, 1.0, 0.0)
        tile = jnp.where(sub8 == r, dot_nt(jnp.ones((8, LANES), BF16), found.astype(BF16)), tile)
    out_ref[...] = jnp.broadcast_to(tile.astype(BF16)[None], out_ref.shape)


def normalized(values):
    mean = jnp.sum(values * values, axis=1, keepdims=True) * (1.0 / D)
    return (values * (lax.rsqrt(mean + 1e-06) * D ** (-0.5))).astype(BF16)


def unit_kernel(emb_ref, unit_ref):
    unit_ref[...] = normalized(emb_ref[...].astype(F32))


def assign_kernel(place_ref, counts_ref, asg_ref, boxes_ref, fast_ref, sizes, bins, pairs):
    chip, core = place_ref[0], place_ref[1]
    lane = iota((LANES, LANES), 1)
    sub = iota((LANES, LANES), 0)
    eye = lane == sub
    lane1 = iota((1, LANES), 1)
    flat = counts_ref[...]
    total = dot(ones_where(iota((8, DEVICES * 8), 1) % 8 == iota((8, DEVICES * 8), 0)), flat)
    tot = [total[r : r + 1, :] for r in range(PIECES)]
    key = [tot[r] * CLUSTERS + (CLUSTERS - 1 - r * LANES - lane1).astype(F32) for r in range(PIECES)]
    col = [jnp.sum(jnp.where(eye, key[r], 0.0), axis=1, keepdims=True) for r in range(PIECES)]
    pos = []
    for r in range(PIECES):
        above = jnp.zeros((LANES, LANES), F32)
        for q in range(PIECES):
            above = above + jnp.where(col[q] > key[r], 1.0, 0.0)
        pos.append(jnp.sum(above, axis=0, keepdims=True).astype(I32))
    for q in range(PIECES):
        here = jnp.zeros((LANES, LANES), F32)
        for r in range(PIECES):
            here = here + jnp.where(pos[r] == sub + q * LANES, tot[r], 0.0)
        sizes[q * LANES : (q + 1) * LANES, :] = jnp.broadcast_to(
            jnp.sum(here, axis=1, keepdims=True), (LANES, LANES)
        )
    lane_c = iota((CHIPS, LANES), 1)
    eye_c = lane_c == iota((CHIPS, LANES), 0)
    lane_b = iota((BATCH, LANES), 1)
    sub_b = iota((BATCH, LANES), 0)

    def one_batch(step, load):
        order = jnp.where(lane1 < CHIPS, load * CHIPS + lane1.astype(F32), 3.0e7)
        order_col = jnp.sum(jnp.where(eye_c, order, 0.0), axis=1, keepdims=True)
        place = jnp.sum(jnp.where(order_col < order, 1.0, 0.0), axis=0, keepdims=True).astype(I32)
        chosen = place == sub_b
        rows = pl.ds(pl.multiple_of(step * BATCH, BATCH), BATCH)
        bins[rows, :] = jnp.broadcast_to(
            jnp.sum(jnp.where(chosen, lane_b, 0), axis=1, keepdims=True), (BATCH, LANES)
        )
        return load + jnp.sum(jnp.where(chosen, sizes[rows, :], 0.0), axis=0, keepdims=True)

    lax.fori_loop(0, CLUSTERS // BATCH, one_batch, jnp.zeros((1, LANES), F32))
    asg = []
    for r in range(PIECES):
        found = jnp.zeros((LANES, LANES), I32)
        for q in range(PIECES):
            rows = bins[q * LANES : (q + 1) * LANES, :]
            found = found + jnp.where(pos[r] == sub + q * LANES, rows, 0)
        asg.append(jnp.sum(found, axis=0, keepdims=True))
    row8 = iota((DEVICES * 8, LANES), 0) % 8

    def pair_counts(table):
        per_row = jnp.zeros((DEVICES * 8, LANES), F32)
        for r in range(PIECES):
            per_row = jnp.where(row8 == r, dot_nt(flat, ones_where(table[r] == sub)), per_row)
        return jnp.sum(per_row.reshape(DEVICES, 8, LANES), axis=1)

    def put(table):
        sub8 = iota((8, LANES), 0)
        tile = jnp.zeros((8, LANES), I32)
        for r in range(PIECES):
            tile = jnp.where(sub8 == r, table[r], tile)
        asg_ref[...] = tile

    pairs[...] = pair_counts(asg)
    put(asg)
    device = iota((CHIPS, DEVICES), 1)
    both_cores = ones_where((device >> 3) * 4 + device % 4 == iota((CHIPS, DEVICES), 0))
    most = jnp.max(dot(both_cores, pairs[...].astype(BF16)))
    over = jnp.max(jnp.sum(jnp.maximum(pairs[...] - (FAST - 1), 0.0), axis=1, keepdims=True))
    fast = (most.astype(I32) <= 2 * (FAST - 1)) & (over.astype(I32) <= EXTRA)
    fast_ref[0] = fast.astype(I32)

    @pl.when(jnp.logical_not(fast))
    def _():
        fixed = []
        for r in range(PIECES):
            cluster = lane1 + r * LANES
            fixed.append((cluster // MEMBERS) * 2 + (cluster % MEMBERS) // 8)
        pairs[...] = pair_counts(fixed)
        put(fixed)

    mine = jnp.sum(jnp.where(lane == chip, pairs[...], 0.0), axis=1, keepdims=True)
    box = lane % CHIPS
    source_core = jnp.where(lane < CHIPS, core, 1 - core)

    def from_core(which):
        source = ((box // 4) * 2 + which) * 4 + box % 4
        return jnp.sum(jnp.where(sub == source, mine, 0.0), axis=0, keepdims=True).astype(I32)

    room = jnp.where(fast, FAST - 1, SLOW - 1)
    boxes = jnp.minimum(from_core(source_core), room)
    boxes = boxes + jnp.maximum(from_core(1 - source_core) - room, 0)
    rounded = (((boxes + 7) // 8) * 8).astype(F32).astype(BF16)
    boxes_ref[0:1, :] = boxes
    earlier = (sub < lane) & (sub // CHIPS == lane // CHIPS)
    boxes_ref[1:2, :] = dot(rounded, ones_where(earlier)).astype(I32)


def label_pieces(ident):
    cl, rank = ident >> RANK_BITS, ident & ((1 << RANK_BITS) - 1)
    return rank >> 9, (rank >> 1) & 255, (rank & 1) + 2 * (cl >> 4), (cl & 15) + 1


def route_kernel(
    asg_ref, mine_ref, other_ref, unit_ref, emb2_ref, out_ref, where_ref, index, index2, labels, extra, *, slots
):
    group = pl.program_id(0)
    room = slots - 1

    @pl.when(group == 0)
    def _():
        sub = iota((CHIPS, LANES), 0)
        lane_sub = iota((LANES, LANES), 0)
        before = ones_where(lane_sub < iota((LANES, LANES), 1))
        chip_of, chips_of, number_of, sums = [], [], [], []
        for ident_ref in (mine_ref, other_ref):
            cl = ident_ref[...] >> RANK_BITS
            chip = jnp.zeros((PARTS, LANES), I32)
            for r in range(PIECES):
                table = jnp.broadcast_to(asg_ref[r : r + 1, :], (PARTS, LANES))
                found = jnp.take_along_axis(table, cl & (LANES - 1), axis=1, mode="promise_in_bounds")
                chip = jnp.where((cl >> 7) == r, found, chip)
            to_chip = [jnp.where(chip[b : b + 1, :] == sub, 1.0, 0.0) for b in range(PARTS)]
            earlier = dot(jnp.concatenate(to_chip, axis=0).astype(BF16), before)
            carry = jnp.zeros((CHIPS, 1), F32)
            rows = []
            for b in range(PARTS):
                until = earlier[b * CHIPS : (b + 1) * CHIPS, :] + carry
                rows.append(jnp.sum(to_chip[b] * until, axis=0, keepdims=True))
                carry = carry + jnp.sum(to_chip[b], axis=1, keepdims=True)
            chip_of.append(chip)
            chips_of.append(to_chip)
            number_of.append(jnp.concatenate(rows, axis=0).astype(I32))
            sums.append(carry)
        spill = []
        for half in range(2):
            taken = [jnp.sum(part * sums[1 - half], axis=0, keepdims=True) for part in chips_of[half]]
            spill.append(jnp.concatenate(taken, axis=0).astype(I32) + number_of[half] - room)
        stays = number_of[0] < room
        target = jnp.where(stays, chip_of[0] * slots + number_of[0], -1)
        back_chip = jnp.where(stays, chip_of[0], chip_of[0] + CHIPS)
        back_slot = jnp.where(stays, number_of[0], spill[0])
        for b in range(PARTS):
            at = slice(b * LANES, (b + 1) * LANES)
            index[:, at] = target[b : b + 1, :]
            where_ref[0:1, at] = back_chip[b : b + 1, :]
            where_ref[1:2, at] = back_slot[b : b + 1, :]

        comes = jnp.where(number_of[1] >= room, 1.0, 0.0)
        within = dot(comes.astype(BF16), before)
        carry = jnp.zeros((1, 1), F32)
        chosen, zero = [], jnp.zeros((1, LANES), I32)
        pieces2 = label_pieces(other_ref[...]) + (chip_of[1], jnp.maximum(spill[1], 0))
        facts = jnp.zeros((8, LANES), F32)
        for b in range(PARTS):
            part = comes[b : b + 1, :]
            order = jnp.where(part > 0.5, within[b : b + 1, :] + carry, -1.0).astype(I32)
            carry = carry + jnp.sum(part, axis=1, keepdims=True)
            chosen.append(ones_where(order == lane_sub))
            lines = [piece[b : b + 1, :] for piece in pieces2] + [zero, zero]
            facts = facts + dot_nt(jnp.concatenate(lines, axis=0).astype(F32).astype(BF16), chosen[b])
        chosen = jnp.concatenate(chosen, axis=1)
        came = facts[3:4, :] > 0.5
        chip2, slot2 = facts[4:5, :].astype(I32), facts[5:6, :].astype(I32)
        index2[...] = jnp.where(came, chip2 * slots + slot2, -1)
        extra[...] = normalized(dot(chosen, emb2_ref[...]))

        to_chip2 = jnp.where(came & (chip2 == sub), 1.0, 0.0)
        pieces = label_pieces(mine_ref[...])
        text, slot_hot = [], []
        held = jnp.where(stays, number_of[0], -1)
        for b in range(PARTS):
            lines = [chips_of[0][b] * piece[b : b + 1, :].astype(F32) for piece in pieces]
            text.append(jnp.concatenate(lines, axis=0).astype(BF16))
            slot_hot.append(ones_where(held[b : b + 1, :] == lane_sub))
        text, slot_hot = jnp.concatenate(text, axis=1), jnp.concatenate(slot_hot, axis=1)
        text2 = jnp.concatenate([to_chip2 * facts[k : k + 1, :] for k in range(PIECES)], axis=0)
        slot_hot2 = ones_where(jnp.where(came, slot2, -1) == lane_sub)
        text = dot_nt(text, slot_hot) + dot_nt(text2.astype(BF16), slot_hot2)
        for k in range(PIECES):
            labels[:, k * LANES : (k + 1) * LANES] = text[k * CHIPS : (k + 1) * CHIPS, :].astype(BF16)

    size = GROUP * slots
    first = group * size
    rows = dot(ones_where(index[...] == iota((size, ROWS), 0) + first), unit_ref[...])
    rows = rows + dot(ones_where(index2[...] == iota((size, EXTRA), 0) + first), extra[...])
    last = (iota((size, CHIPS), 1) - group * GROUP) * slots + slots - 1
    text = dot(ones_where(last == iota((size, CHIPS), 0)), labels[...])
    out_ref[:, : PIECES * LANES] = (rows[:, : PIECES * LANES] + text).astype(BF16)
    out_ref[:, PIECES * LANES :] = rows[:, PIECES * LANES :].astype(BF16)


def pack_boxes(boxes_ref, held_boxes, box_rows, sems, keys, ids, columns, text, half, tiles):
    copies = []
    for c in range(CHIPS // CHUNK):
        some = pl.ds(c * CHUNK, CHUNK)
        copies.append(pltpu.make_async_copy(held_boxes.at[some], box_rows.at[some], sems.at[c]))
        copies[c].start()
    lane1 = iota((1, LANES), 1)
    ids[...] = jnp.full(ids.shape, -1, I32)
    label_row = ones_where(iota((CHUNK, CHUNK * 8), 1) == iota((CHUNK, CHUNK * 8), 0) * 8 + 7)
    for c in range(CHIPS // CHUNK):
        copies[c].wait()
        first = c * CHUNK
        held = box_rows[first : first + CHUNK, tiles - 1, :, : PIECES * LANES]
        words = dot(label_row, held.reshape(CHUNK * 8, PIECES * LANES)).astype(I32)
        high, low, mixed, filled = (words[:, k * LANES : (k + 1) * LANES] for k in range(PIECES))
        rank = (high << 9) + (low << 1) + (mixed & 1)
        cluster = ((mixed >> 1) << 4) + filled - 1
        text[first : first + CHUNK, :] = jnp.where(filled > 0, (cluster << RANK_BITS) + rank, -1)

        def pack(i, carry, first=first):
            b = first + i
            start = boxes_ref[1, half * CHIPS + b]
            keys[pl.ds(start // 8, tiles)] = box_rows[b]
            shift = lax.rem(start, LANES)
            row = start // LANES
            line = pltpu.roll(text[pl.ds(b, 1), :], shift, 1)
            ids[pl.ds(row, 1), :] = jnp.where(lane1 >= shift, line, ids[pl.ds(row, 1), :])
            ids[pl.ds(row + 1, 1), :] = jnp.where(lane1 < shift, line, -1)
            return carry

        lax.fori_loop(0, CHUNK, pack, 0, unroll=CHUNK)
    end = half * CHIPS + CHIPS - 1
    count = boxes_ref[1, end] + ((boxes_ref[0, end] + 7) // 8) * 8
    per_block = KB // LANES

    def column(k, carry):
        for r in range(per_block):
            line = jnp.broadcast_to(ids[pl.ds(k * per_block + r, 1), :], (LANES, LANES))
            rows = pl.ds(pl.multiple_of(k * KB + r * LANES, LANES), LANES)
            columns[rows, :] = jnp.transpose(line)
        return carry

    lax.fori_loop(0, (count + KB - 1) // KB, column, 0)
    return count


def compare(queries, q_ids, n_queries, keys, columns, n_keys, first, finish):
    parts = QB // LANES

    def block(q, carry):
        query = queries[pl.ds(q * (QB // 8), QB // 8)].reshape(QB, D)
        high = [q_ids[pl.ds(q * parts + p, 1), :] for p in range(parts)]
        low = [(h >> RANK_BITS) << RANK_BITS for h in high]
        span = [(h - l).astype(U32) for h, l in zip(high, low)]

        def key_block(k, acc):
            score = dot_nt(keys[pl.ds(k * (KB // 8), KB // 8)].reshape(KB, D), query)
            ident = columns[pl.ds(pl.multiple_of(k * KB, KB), KB), :]
            new = []
            for p in range(parts):
                piece = score[:, p * LANES : (p + 1) * LANES]
                valid = (ident - low[p]).astype(U32) < span[p]
                piece = jnp.where(valid, piece, -1.0)
                new.append(jnp.maximum(acc[p], jnp.max(piece.reshape(KB // 8, 8, LANES), axis=0)))
            return tuple(new)

        acc = tuple(first(q * parts + p) for p in range(parts))
        acc = lax.fori_loop(0, (n_keys + KB - 1) // KB, key_block, acc)
        for p in range(parts):
            finish(q * parts + p, acc[p])
        return carry

    lax.fori_loop(0, (n_queries + QB - 1) // QB, block, 0)


def own_kernel(
    boxes_ref, mine_ref, keys_ref, ids, most_ref, columns, text, box_rows, keys, sems, keys_sem, *, slots
):
    count = pack_boxes(boxes_ref, mine_ref, box_rows, sems, keys, ids, columns, text, 0, slots // 8)
    kept = pltpu.make_async_copy(keys, keys_ref, keys_sem)
    kept.start()

    def finish(p, acc):
        most_ref[p] = acc

    compare(keys, ids, count, keys, columns, count, lambda p: jnp.full((8, LANES), -1.0, F32), finish)
    kept.wait()


def other_kernel(
    boxes_ref, other_ref, queries_ref, q_ids, most_ref, out_ref, columns, text, box_rows, keys, sems, keys_sem,
    queries, ids, best, *, slots
):
    asked = pltpu.make_async_copy(queries_ref, queries, keys_sem)
    asked.start()
    count = pack_boxes(boxes_ref, other_ref, box_rows, sems, keys, ids, columns, text, 1, slots // 8)
    asked.wait()
    n_queries = boxes_ref[1, CHIPS - 1] + ((boxes_ref[0, CHIPS - 1] + 7) // 8) * 8

    def finish(p, acc):
        best[pl.ds(p, 1), :] = jnp.max(acc, axis=0, keepdims=True)

    compare(queries, q_ids, n_queries, keys, columns, count, lambda p: most_ref[p], finish)
    lane1 = iota((1, LANES), 1)

    def unpack(b, carry):
        start = boxes_ref[1, b]
        shift = lax.rem(start, LANES)
        row = start // LANES
        two = jnp.where(lane1 >= shift, best[pl.ds(row, 1), :], best[pl.ds(row + 1, 1), :])
        line = pltpu.roll(two, lax.rem(LANES - shift, LANES), 1)
        line = jnp.where(lane1 < boxes_ref[0, b], line, 0.0)
        out_ref[b] = line
        return carry

    lax.fori_loop(0, CHIPS, unpack, 0, unroll=UNROLL)


def result_kernel(back_ref, back2_ref, where_ref, out_ref):
    table = jnp.concatenate([back_ref[:, 0, :], back2_ref[:, 0, :]], axis=0).T
    to_chip = jnp.where(where_ref[0:1, :] == iota((LANES, ROWS), 0), 1.0, 0.0)
    by_slot = jnp.dot(
        table, to_chip, preferred_element_type=F32, precision=lax.Precision.HIGHEST
    )
    picked = jnp.where(where_ref[1:2, :] == iota((LANES, ROWS), 0), by_slot, 0.0)
    out_ref[...] = jnp.sum(picked, axis=0, keepdims=True)


def swap(x):
    return lax.ppermute(x, "core", [(0, 1), (1, 0)])


def exchange(slots, asg, mine, other, unit, emb2, boxes):
    size = GROUP * slots
    big = 28 if slots == FAST else 44
    outbox, where = pl.pallas_call(
        functools.partial(route_kernel, slots=slots),
        grid=(CHIPS // GROUP,),
        in_specs=[
            pl.BlockSpec((8, LANES), lambda g: (0, 0)),
            pl.BlockSpec((PARTS, LANES), lambda g: (0, 0)),
            pl.BlockSpec((PARTS, LANES), lambda g: (0, 0)),
            pl.BlockSpec((ROWS, D), lambda g: (0, 0)),
            pl.BlockSpec((ROWS, D), lambda g: (0, 0)),
        ],
        out_specs=[
            pl.BlockSpec((size, D), lambda g: (g, 0)),
            pl.BlockSpec((2, ROWS), lambda g: (0, 0)),
        ],
        out_shape=[
            jax.ShapeDtypeStruct((CHIPS * slots, D), BF16),
            jax.ShapeDtypeStruct((2, ROWS), I32),
        ],
        scratch_shapes=[
            pltpu.VMEM((1, ROWS), I32),
            pltpu.VMEM((1, EXTRA), I32),
            pltpu.VMEM((CHIPS, PIECES * LANES), BF16),
            pltpu.VMEM((EXTRA, D), BF16),
        ],
        compiler_params=params(big),
        name="route",
    )(asg, mine, other, unit, emb2)
    mine = lax.all_to_all(outbox.reshape(CHIPS, slots, D), CHIP_AXES, 0, 0, tiled=True)
    mine = mine.reshape(CHIPS, slots // 8, 8, D)
    other = swap(mine)
    n_rows = CHIPS * slots
    q_rows, k_rows = -(-n_rows // QB) * QB, -(-n_rows // KB) * KB
    n_keys = max(q_rows, k_rows)
    n_ids = n_keys // LANES + 8
    vmem = pl.BlockSpec(memory_space=pltpu.VMEM)
    smem = pl.BlockSpec(memory_space=pltpu.SMEM)
    hbm = pl.BlockSpec(memory_space=pl.ANY)
    keys = jax.ShapeDtypeStruct((n_keys // 8, 8, D), BF16)
    ids = jax.ShapeDtypeStruct((n_ids, LANES), I32)
    most = jax.ShapeDtypeStruct((q_rows // LANES, 8, LANES), F32)
    scratch = [
        pltpu.VMEM((k_rows, LANES), I32),
        pltpu.VMEM((CHIPS, LANES), I32),
        pltpu.VMEM((CHIPS, slots // 8, 8, D), BF16),
        pltpu.VMEM(keys.shape, BF16),
        pltpu.SemaphoreType.DMA((CHIPS // CHUNK,)),
        pltpu.SemaphoreType.DMA,
    ]
    own = pl.pallas_call(
        functools.partial(own_kernel, slots=slots),
        in_specs=[smem, hbm],
        out_specs=[hbm, vmem, vmem],
        out_shape=[keys, ids, most],
        scratch_shapes=scratch,
        compiler_params=params(big),
        cost_estimate=pl.CostEstimate(flops=8 * 10**9, bytes_accessed=4 * n_rows * D, transcendentals=0),
        name="own",
    )(boxes, mine)
    results = pl.pallas_call(
        functools.partial(other_kernel, slots=slots),
        in_specs=[smem, hbm, hbm, vmem, vmem],
        out_specs=vmem,
        out_shape=jax.ShapeDtypeStruct((CHIPS, 1, LANES), F32),
        scratch_shapes=scratch
        + [
            pltpu.VMEM(keys.shape, BF16),
            pltpu.VMEM(ids.shape, I32),
            pltpu.VMEM((q_rows // LANES + 8, LANES), F32),
        ],
        compiler_params=params(big),
        name="other",
    )(boxes, other, *own)
    return lax.all_to_all(results, CHIP_AXES, 0, 0, tiled=True), where


def unit_rows(emb):
    return pl.pallas_call(
        unit_kernel,
        grid=(4,),
        in_specs=[pl.BlockSpec((ROWS // 4, D), lambda i: (i, 0))],
        out_specs=pl.BlockSpec((ROWS // 4, D), lambda i: (i, 0)),
        out_shape=jax.ShapeDtypeStruct((ROWS, D), BF16),
        compiler_params=params(),
        cost_estimate=pl.CostEstimate(flops=4 * ROWS * D, bytes_accessed=4 * ROWS * D, transcendentals=ROWS),
        name="unit",
    )(emb)


def body(emb, home, member, rank):
    emb2 = swap(emb)
    mine, counts = pl.pallas_call(
        count_kernel,
        out_shape=[
            jax.ShapeDtypeStruct((PARTS, LANES), I32),
            jax.ShapeDtypeStruct((DEVICES, 8, LANES), BF16),
        ],
        compiler_params=params(56),
        name="count",
    )(*(x.reshape(PARTS, LANES) for x in (home, member, rank)))
    other = swap(mine)
    counts = lax.all_to_all(counts, ALL_AXES, 0, 0, tiled=True).reshape(DEVICES * 8, LANES)
    unit = unit_rows(emb)
    chip = lax.axis_index("yx") * lax.axis_size("z") + lax.axis_index("z")
    place = jnp.stack([chip, lax.axis_index("core")]).astype(I32)
    asg, boxes, fast = pl.pallas_call(
        assign_kernel,
        in_specs=[
            pl.BlockSpec(memory_space=pltpu.SMEM),
            pl.BlockSpec(memory_space=pltpu.VMEM),
        ],
        out_specs=[
            pl.BlockSpec(memory_space=pltpu.VMEM),
            pl.BlockSpec(memory_space=pltpu.VMEM),
            pl.BlockSpec(memory_space=pltpu.SMEM),
        ],
        out_shape=[
            jax.ShapeDtypeStruct((8, LANES), I32),
            jax.ShapeDtypeStruct((2, LANES), I32),
            jax.ShapeDtypeStruct((1,), I32),
        ],
        scratch_shapes=[
            pltpu.VMEM((CLUSTERS, LANES), F32),
            pltpu.VMEM((CLUSTERS, LANES), I32),
            pltpu.VMEM((DEVICES, LANES), F32),
        ],
        compiler_params=params(),
        name="assign",
    )(place, counts)
    back, where = lax.cond(
        fast[0] == 1,
        functools.partial(exchange, FAST),
        functools.partial(exchange, SLOW),
        asg,
        mine,
        other,
        unit,
        emb2,
        boxes,
    )
    out = pl.pallas_call(
        result_kernel,
        out_shape=jax.ShapeDtypeStruct((1, ROWS), F32),
        compiler_params=params(),
        name="result",
    )(back, swap(back), where)
    return out.reshape(ROWS)


def solution(mesh):
    chips = Mesh(mesh.devices.reshape(-1, 2, mesh.devices.shape[1]), ALL_AXES)
    rows = P(ALL_AXES)
    return jax.shard_map(
        body,
        mesh=chips,
        in_specs=(P(ALL_AXES, None), P(ALL_AXES, None), P(ALL_AXES, None), rows),
        out_specs=rows,
        check_vma=False,
    )
```

```python
import functools

import jax
import jax.numpy as jnp
from jax import lax
from jax.experimental import pallas as pl
from jax.experimental.pallas import tpu as pltpu
from jax.sharding import Mesh, PartitionSpec as P

D = 768
ROWS = 1024
CLUSTERS = 512
MEMBERS = 16
CHIPS = 64
DEVICES = 128
LANES = 128
PIECES = CLUSTERS // LANES
BATCH = 40
BATCHES = -(-(CLUSTERS - CHIPS) // BATCH)
PLACES = CHIPS + BATCHES * BATCH
FAST = 32
SLOW = 72
GROUP = 32
QB = 768
KB = 768
UNROLL = 32
CHUNK = 16
EXTRA = 128
PARTS = ROWS // LANES
RANK_BITS = 17
CHIP_AXES = ("yx", "z")
ALL_AXES = ("yx", "core", "z")
F32, BF16, I32, U32 = jnp.float32, jnp.bfloat16, jnp.int32, jnp.uint32
NT = (((1,), (1,)), ((), ()))


def iota(shape, dim):
    return lax.broadcasted_iota(I32, shape, dim)


def dot(a, b):
    return jnp.dot(a, b, preferred_element_type=F32)


def dot_nt(a, b):
    return lax.dot_general(a, b, NT, preferred_element_type=F32)


def ones_where(mask):
    return jnp.where(mask, 1.0, 0.0).astype(BF16)


def params(mib=16):
    return pltpu.CompilerParams(vmem_limit_bytes=mib << 20)


def count_kernel(home_ref, member_ref, rank_ref, ident_ref, out_ref):
    cl = home_ref[...] * MEMBERS + member_ref[...]
    ident_ref[...] = (cl << RANK_BITS) + rank_ref[...]
    sub = iota((LANES, LANES), 0)
    sub8 = iota((8, LANES), 0)
    tile = jnp.zeros((8, LANES), F32)
    for r in range(PIECES):
        found = jnp.zeros((LANES, LANES), F32)
        for b in range(PARTS):
            found = found + jnp.where(cl[b : b + 1, :] == sub + r * LANES, 1.0, 0.0)
        tile = jnp.where(sub8 == r, dot_nt(jnp.ones((8, LANES), BF16), found.astype(BF16)), tile)
    out_ref[...] = jnp.broadcast_to(tile.astype(BF16)[None], out_ref.shape)


def normalized(values):
    mean = jnp.sum(values * values, axis=1, keepdims=True) * (1.0 / D)
    return (values * (lax.rsqrt(mean + 1e-06) * D ** (-0.5))).astype(BF16)


def unit_kernel(emb_ref, unit_ref):
    unit_ref[...] = normalized(emb_ref[...].astype(F32))


def assign_kernel(place_ref, counts_ref, asg_ref, boxes_ref, fast_ref, sizes, bins, pairs):
    chip, core = place_ref[0], place_ref[1]
    lane = iota((LANES, LANES), 1)
    sub = iota((LANES, LANES), 0)
    eye = lane == sub
    lane1 = iota((1, LANES), 1)
    flat = counts_ref[...]
    total = dot(ones_where(iota((8, DEVICES * 8), 1) % 8 == iota((8, DEVICES * 8), 0)), flat)
    tot = [total[r : r + 1, :] for r in range(PIECES)]
    key = [tot[r] * CLUSTERS + (CLUSTERS - 1 - r * LANES - lane1).astype(F32) for r in range(PIECES)]
    col = [jnp.sum(jnp.where(eye, key[r], 0.0), axis=1, keepdims=True) for r in range(PIECES)]
    pos = []
    for r in range(PIECES):
        above = jnp.zeros((LANES, LANES), F32)
        for q in range(PIECES):
            above = above + jnp.where(col[q] > key[r], 1.0, 0.0)
        pos.append(jnp.sum(above, axis=0, keepdims=True).astype(I32))
    for q in range(PIECES):
        here = jnp.zeros((LANES, LANES), F32)
        for r in range(PIECES):
            here = here + jnp.where(pos[r] == sub + q * LANES, tot[r], 0.0)
        sizes[q * LANES : (q + 1) * LANES, :] = jnp.broadcast_to(
            jnp.sum(here, axis=1, keepdims=True), (LANES, LANES)
        )
    lane_c = iota((CHIPS, LANES), 1)
    eye_c = lane_c == iota((CHIPS, LANES), 0)
    lane_b = iota((BATCH, LANES), 1)
    sub_b = iota((BATCH, LANES), 0)

    def one_batch(step, load):
        order = jnp.where(lane1 < CHIPS, load * CHIPS + lane1.astype(F32), 3.0e7)
        order_col = jnp.sum(jnp.where(eye_c, order, 0.0), axis=1, keepdims=True)
        place = jnp.sum(jnp.where(order_col < order, 1.0, 0.0), axis=0, keepdims=True).astype(I32)
        chosen = place == sub_b
        rows = pl.ds(pl.multiple_of(CHIPS + step * BATCH, 8), BATCH)
        bins[rows, :] = jnp.broadcast_to(
            jnp.sum(jnp.where(chosen, lane_b, 0), axis=1, keepdims=True), (BATCH, LANES)
        )
        return load + jnp.sum(jnp.where(chosen, sizes[rows, :], 0.0), axis=0, keepdims=True)

    sizes[CLUSTERS:, :] = jnp.zeros((PLACES - CLUSTERS, LANES), F32)
    bins[:CHIPS, :] = iota((CHIPS, LANES), 0)
    largest = jnp.sum(jnp.where(eye_c, sizes[:CHIPS, :], 0.0), axis=0, keepdims=True)
    lax.fori_loop(0, BATCHES, one_batch, largest)
    asg = []
    for r in range(PIECES):
        found = jnp.zeros((LANES, LANES), I32)
        for q in range(PIECES):
            rows = bins[q * LANES : (q + 1) * LANES, :]
            found = found + jnp.where(pos[r] == sub + q * LANES, rows, 0)
        asg.append(jnp.sum(found, axis=0, keepdims=True))
    row8 = iota((DEVICES * 8, LANES), 0) % 8

    def pair_counts(table):
        per_row = jnp.zeros((DEVICES * 8, LANES), F32)
        for r in range(PIECES):
            per_row = jnp.where(row8 == r, dot_nt(flat, ones_where(table[r] == sub)), per_row)
        return jnp.sum(per_row.reshape(DEVICES, 8, LANES), axis=1)

    def put(table):
        sub8 = iota((8, LANES), 0)
        tile = jnp.zeros((8, LANES), I32)
        for r in range(PIECES):
            tile = jnp.where(sub8 == r, table[r], tile)
        asg_ref[...] = tile

    pairs[...] = pair_counts(asg)
    put(asg)
    device = iota((CHIPS, DEVICES), 1)
    both_cores = ones_where((device >> 3) * 4 + device % 4 == iota((CHIPS, DEVICES), 0))
    most = jnp.max(dot(both_cores, pairs[...].astype(BF16)))
    over = jnp.max(jnp.sum(jnp.maximum(pairs[...] - (FAST - 1), 0.0), axis=1, keepdims=True))
    fast = (most.astype(I32) <= 2 * (FAST - 1)) & (over.astype(I32) <= EXTRA)
    fast_ref[0] = fast.astype(I32)

    @pl.when(jnp.logical_not(fast))
    def _():
        fixed = []
        for r in range(PIECES):
            cluster = lane1 + r * LANES
            fixed.append((cluster // MEMBERS) * 2 + (cluster % MEMBERS) // 8)
        pairs[...] = pair_counts(fixed)
        put(fixed)

    mine = jnp.sum(jnp.where(lane == chip, pairs[...], 0.0), axis=1, keepdims=True)
    box = lane % CHIPS
    source_core = jnp.where(lane < CHIPS, core, 1 - core)

    def from_core(which):
        source = ((box // 4) * 2 + which) * 4 + box % 4
        return jnp.sum(jnp.where(sub == source, mine, 0.0), axis=0, keepdims=True).astype(I32)

    room = jnp.where(fast, FAST - 1, SLOW - 1)
    boxes = jnp.minimum(from_core(source_core), room)
    boxes = boxes + jnp.maximum(from_core(1 - source_core) - room, 0)
    rounded = (((boxes + 7) // 8) * 8).astype(F32).astype(BF16)
    boxes_ref[0:1, :] = boxes
    earlier = (sub < lane) & (sub // CHIPS == lane // CHIPS)
    boxes_ref[1:2, :] = dot(rounded, ones_where(earlier)).astype(I32)


def label_pieces(ident):
    cl, rank = ident >> RANK_BITS, ident & ((1 << RANK_BITS) - 1)
    return rank >> 9, (rank >> 1) & 255, (rank & 1) + 2 * (cl >> 4), (cl & 15) + 1


def route_kernel(
    asg_ref, mine_ref, other_ref, unit_ref, emb2_ref, out_ref, where_ref, index, index2, labels, extra, *, slots
):
    group = pl.program_id(0)
    room = slots - 1

    @pl.when(group == 0)
    def _():
        sub = iota((CHIPS, LANES), 0)
        lane_sub = iota((LANES, LANES), 0)
        before = ones_where(lane_sub < iota((LANES, LANES), 1))
        chip_of, chips_of, number_of, sums = [], [], [], []
        for ident_ref in (mine_ref, other_ref):
            cl = ident_ref[...] >> RANK_BITS
            chip = jnp.zeros((PARTS, LANES), I32)
            for r in range(PIECES):
                table = jnp.broadcast_to(asg_ref[r : r + 1, :], (PARTS, LANES))
                found = jnp.take_along_axis(table, cl & (LANES - 1), axis=1, mode="promise_in_bounds")
                chip = jnp.where((cl >> 7) == r, found, chip)
            to_chip = [jnp.where(chip[b : b + 1, :] == sub, 1.0, 0.0) for b in range(PARTS)]
            earlier = dot(jnp.concatenate(to_chip, axis=0).astype(BF16), before)
            carry = jnp.zeros((CHIPS, 1), F32)
            rows = []
            for b in range(PARTS):
                until = earlier[b * CHIPS : (b + 1) * CHIPS, :] + carry
                rows.append(jnp.sum(to_chip[b] * until, axis=0, keepdims=True))
                carry = carry + jnp.sum(to_chip[b], axis=1, keepdims=True)
            chip_of.append(chip)
            chips_of.append(to_chip)
            number_of.append(jnp.concatenate(rows, axis=0).astype(I32))
            sums.append(carry)
        spill = []
        for half in range(2):
            taken = [jnp.sum(part * sums[1 - half], axis=0, keepdims=True) for part in chips_of[half]]
            spill.append(jnp.concatenate(taken, axis=0).astype(I32) + number_of[half] - room)
        stays = number_of[0] < room
        target = jnp.where(stays, chip_of[0] * slots + number_of[0], -1)
        back_chip = jnp.where(stays, chip_of[0], chip_of[0] + CHIPS)
        back_slot = jnp.where(stays, number_of[0], spill[0])
        for b in range(PARTS):
            at = slice(b * LANES, (b + 1) * LANES)
            index[:, at] = target[b : b + 1, :]
            where_ref[0:1, at] = back_chip[b : b + 1, :]
            where_ref[1:2, at] = back_slot[b : b + 1, :]

        comes = jnp.where(number_of[1] >= room, 1.0, 0.0)
        within = dot(comes.astype(BF16), before)
        carry = jnp.zeros((1, 1), F32)
        chosen, zero = [], jnp.zeros((1, LANES), I32)
        pieces2 = label_pieces(other_ref[...]) + (chip_of[1], jnp.maximum(spill[1], 0))
        facts = jnp.zeros((8, LANES), F32)
        for b in range(PARTS):
            part = comes[b : b + 1, :]
            order = jnp.where(part > 0.5, within[b : b + 1, :] + carry, -1.0).astype(I32)
            carry = carry + jnp.sum(part, axis=1, keepdims=True)
            chosen.append(ones_where(order == lane_sub))
            lines = [piece[b : b + 1, :] for piece in pieces2] + [zero, zero]
            facts = facts + dot_nt(jnp.concatenate(lines, axis=0).astype(F32).astype(BF16), chosen[b])
        chosen = jnp.concatenate(chosen, axis=1)
        came = facts[3:4, :] > 0.5
        chip2, slot2 = facts[4:5, :].astype(I32), facts[5:6, :].astype(I32)
        index2[...] = jnp.where(came, chip2 * slots + slot2, -1)
        extra[...] = normalized(dot(chosen, emb2_ref[...]))

        to_chip2 = jnp.where(came & (chip2 == sub), 1.0, 0.0)
        pieces = label_pieces(mine_ref[...])
        text, slot_hot = [], []
        held = jnp.where(stays, number_of[0], -1)
        for b in range(PARTS):
            lines = [chips_of[0][b] * piece[b : b + 1, :].astype(F32) for piece in pieces]
            text.append(jnp.concatenate(lines, axis=0).astype(BF16))
            slot_hot.append(ones_where(held[b : b + 1, :] == lane_sub))
        text, slot_hot = jnp.concatenate(text, axis=1), jnp.concatenate(slot_hot, axis=1)
        text2 = jnp.concatenate([to_chip2 * facts[k : k + 1, :] for k in range(PIECES)], axis=0)
        slot_hot2 = ones_where(jnp.where(came, slot2, -1) == lane_sub)
        text = dot_nt(text, slot_hot) + dot_nt(text2.astype(BF16), slot_hot2)
        for k in range(PIECES):
            labels[:, k * LANES : (k + 1) * LANES] = text[k * CHIPS : (k + 1) * CHIPS, :].astype(BF16)

    size = GROUP * slots
    first = group * size
    rows = dot(ones_where(index[...] == iota((size, ROWS), 0) + first), unit_ref[...])
    rows = rows + dot(ones_where(index2[...] == iota((size, EXTRA), 0) + first), extra[...])
    last = (iota((size, CHIPS), 1) - group * GROUP) * slots + slots - 1
    text = dot(ones_where(last == iota((size, CHIPS), 0)), labels[...])
    out_ref[:, : PIECES * LANES] = (rows[:, : PIECES * LANES] + text).astype(BF16)
    out_ref[:, PIECES * LANES :] = rows[:, PIECES * LANES :].astype(BF16)


def pack_boxes(boxes_ref, held_boxes, box_rows, sems, keys, ids, columns, text, half, tiles):
    copies = []
    for c in range(CHIPS // CHUNK):
        some = pl.ds(c * CHUNK, CHUNK)
        copies.append(pltpu.make_async_copy(held_boxes.at[some], box_rows.at[some], sems.at[c]))
        copies[c].start()
    lane1 = iota((1, LANES), 1)
    ids[...] = jnp.full(ids.shape, -1, I32)
    label_row = ones_where(iota((CHUNK, CHUNK * 8), 1) == iota((CHUNK, CHUNK * 8), 0) * 8 + 7)
    for c in range(CHIPS // CHUNK):
        copies[c].wait()
        first = c * CHUNK
        held = box_rows[first : first + CHUNK, tiles - 1, :, : PIECES * LANES]
        words = dot(label_row, held.reshape(CHUNK * 8, PIECES * LANES)).astype(I32)
        high, low, mixed, filled = (words[:, k * LANES : (k + 1) * LANES] for k in range(PIECES))
        rank = (high << 9) + (low << 1) + (mixed & 1)
        cluster = ((mixed >> 1) << 4) + filled - 1
        text[first : first + CHUNK, :] = jnp.where(filled > 0, (cluster << RANK_BITS) + rank, -1)

        def pack(i, carry, first=first):
            b = first + i
            start = boxes_ref[1, half * CHIPS + b]
            keys[pl.ds(start // 8, tiles)] = box_rows[b]
            shift = lax.rem(start, LANES)
            row = start // LANES
            line = pltpu.roll(text[pl.ds(b, 1), :], shift, 1)
            ids[pl.ds(row, 1), :] = jnp.where(lane1 >= shift, line, ids[pl.ds(row, 1), :])
            ids[pl.ds(row + 1, 1), :] = jnp.where(lane1 < shift, line, -1)
            return carry

        lax.fori_loop(0, CHUNK, pack, 0, unroll=CHUNK)
    end = half * CHIPS + CHIPS - 1
    count = boxes_ref[1, end] + ((boxes_ref[0, end] + 7) // 8) * 8
    per_block = KB // LANES

    def column(k, carry):
        for r in range(per_block):
            line = jnp.broadcast_to(ids[pl.ds(k * per_block + r, 1), :], (LANES, LANES))
            rows = pl.ds(pl.multiple_of(k * KB + r * LANES, LANES), LANES)
            columns[rows, :] = jnp.transpose(line)
        return carry

    lax.fori_loop(0, (count + KB - 1) // KB, column, 0)
    return count


def compare(queries, q_ids, n_queries, keys, columns, n_keys, first, finish):
    parts = QB // LANES

    def block(q, carry):
        query = queries[pl.ds(q * (QB // 8), QB // 8)].reshape(QB, D)
        high = [q_ids[pl.ds(q * parts + p, 1), :] for p in range(parts)]
        low = [(h >> RANK_BITS) << RANK_BITS for h in high]
        span = [(h - l).astype(U32) for h, l in zip(high, low)]

        def key_block(k, acc):
            score = dot_nt(keys[pl.ds(k * (KB // 8), KB // 8)].reshape(KB, D), query)
            ident = columns[pl.ds(pl.multiple_of(k * KB, KB), KB), :]
            new = []
            for p in range(parts):
                piece = score[:, p * LANES : (p + 1) * LANES]
                valid = (ident - low[p]).astype(U32) < span[p]
                piece = jnp.where(valid, piece, -1.0)
                new.append(jnp.maximum(acc[p], jnp.max(piece.reshape(KB // 8, 8, LANES), axis=0)))
            return tuple(new)

        acc = tuple(first(q * parts + p) for p in range(parts))
        acc = lax.fori_loop(0, (n_keys + KB - 1) // KB, key_block, acc)
        for p in range(parts):
            finish(q * parts + p, acc[p])
        return carry

    lax.fori_loop(0, (n_queries + QB - 1) // QB, block, 0)


def own_kernel(
    boxes_ref, mine_ref, keys_ref, ids, most_ref, columns, text, box_rows, keys, sems, keys_sem, *, slots
):
    count = pack_boxes(boxes_ref, mine_ref, box_rows, sems, keys, ids, columns, text, 0, slots // 8)
    kept = pltpu.make_async_copy(keys, keys_ref, keys_sem)
    kept.start()

    def finish(p, acc):
        most_ref[p] = acc

    compare(keys, ids, count, keys, columns, count, lambda p: jnp.full((8, LANES), -1.0, F32), finish)
    kept.wait()


def other_kernel(
    boxes_ref, other_ref, queries_ref, q_ids, most_ref, out_ref, columns, text, box_rows, keys, sems, keys_sem,
    queries, ids, best, *, slots
):
    asked = pltpu.make_async_copy(queries_ref, queries, keys_sem)
    asked.start()
    count = pack_boxes(boxes_ref, other_ref, box_rows, sems, keys, ids, columns, text, 1, slots // 8)
    asked.wait()
    n_queries = boxes_ref[1, CHIPS - 1] + ((boxes_ref[0, CHIPS - 1] + 7) // 8) * 8

    def finish(p, acc):
        best[pl.ds(p, 1), :] = jnp.max(acc, axis=0, keepdims=True)

    compare(queries, q_ids, n_queries, keys, columns, count, lambda p: most_ref[p], finish)
    lane1 = iota((1, LANES), 1)

    def unpack(b, carry):
        start = boxes_ref[1, b]
        shift = lax.rem(start, LANES)
        row = start // LANES
        two = jnp.where(lane1 >= shift, best[pl.ds(row, 1), :], best[pl.ds(row + 1, 1), :])
        line = pltpu.roll(two, lax.rem(LANES - shift, LANES), 1)
        line = jnp.where(lane1 < boxes_ref[0, b], line, 0.0)
        out_ref[b] = line
        return carry

    lax.fori_loop(0, CHIPS, unpack, 0, unroll=UNROLL)


def result_kernel(back_ref, back2_ref, where_ref, out_ref):
    table = jnp.concatenate([back_ref[:, 0, :], back2_ref[:, 0, :]], axis=0).T
    to_chip = jnp.where(where_ref[0:1, :] == iota((LANES, ROWS), 0), 1.0, 0.0)
    by_slot = jnp.dot(
        table, to_chip, preferred_element_type=F32, precision=lax.Precision.HIGHEST
    )
    picked = jnp.where(where_ref[1:2, :] == iota((LANES, ROWS), 0), by_slot, 0.0)
    out_ref[...] = jnp.sum(picked, axis=0, keepdims=True)


def swap(x):
    return lax.ppermute(x, "core", [(0, 1), (1, 0)])


def exchange(slots, asg, mine, other, unit, emb2, boxes):
    size = GROUP * slots
    big = 28 if slots == FAST else 44
    outbox, where = pl.pallas_call(
        functools.partial(route_kernel, slots=slots),
        grid=(CHIPS // GROUP,),
        in_specs=[
            pl.BlockSpec((8, LANES), lambda g: (0, 0)),
            pl.BlockSpec((PARTS, LANES), lambda g: (0, 0)),
            pl.BlockSpec((PARTS, LANES), lambda g: (0, 0)),
            pl.BlockSpec((ROWS, D), lambda g: (0, 0)),
            pl.BlockSpec((ROWS, D), lambda g: (0, 0)),
        ],
        out_specs=[
            pl.BlockSpec((size, D), lambda g: (g, 0)),
            pl.BlockSpec((2, ROWS), lambda g: (0, 0)),
        ],
        out_shape=[
            jax.ShapeDtypeStruct((CHIPS * slots, D), BF16),
            jax.ShapeDtypeStruct((2, ROWS), I32),
        ],
        scratch_shapes=[
            pltpu.VMEM((1, ROWS), I32),
            pltpu.VMEM((1, EXTRA), I32),
            pltpu.VMEM((CHIPS, PIECES * LANES), BF16),
            pltpu.VMEM((EXTRA, D), BF16),
        ],
        compiler_params=params(big),
        name="route",
    )(asg, mine, other, unit, emb2)
    mine = lax.all_to_all(outbox.reshape(CHIPS, slots, D), CHIP_AXES, 0, 0, tiled=True)
    mine = mine.reshape(CHIPS, slots // 8, 8, D)
    other = swap(mine)
    n_rows = CHIPS * slots
    q_rows, k_rows = -(-n_rows // QB) * QB, -(-n_rows // KB) * KB
    n_keys = max(q_rows, k_rows)
    n_ids = n_keys // LANES + 8
    vmem = pl.BlockSpec(memory_space=pltpu.VMEM)
    smem = pl.BlockSpec(memory_space=pltpu.SMEM)
    hbm = pl.BlockSpec(memory_space=pl.ANY)
    keys = jax.ShapeDtypeStruct((n_keys // 8, 8, D), BF16)
    ids = jax.ShapeDtypeStruct((n_ids, LANES), I32)
    most = jax.ShapeDtypeStruct((q_rows // LANES, 8, LANES), F32)
    scratch = [
        pltpu.VMEM((k_rows, LANES), I32),
        pltpu.VMEM((CHIPS, LANES), I32),
        pltpu.VMEM((CHIPS, slots // 8, 8, D), BF16),
        pltpu.VMEM(keys.shape, BF16),
        pltpu.SemaphoreType.DMA((CHIPS // CHUNK,)),
        pltpu.SemaphoreType.DMA,
    ]
    own = pl.pallas_call(
        functools.partial(own_kernel, slots=slots),
        in_specs=[smem, hbm],
        out_specs=[hbm, vmem, vmem],
        out_shape=[keys, ids, most],
        scratch_shapes=scratch,
        compiler_params=params(big),
        cost_estimate=pl.CostEstimate(flops=8 * 10**9, bytes_accessed=4 * n_rows * D, transcendentals=0),
        name="own",
    )(boxes, mine)
    results = pl.pallas_call(
        functools.partial(other_kernel, slots=slots),
        in_specs=[smem, hbm, hbm, vmem, vmem],
        out_specs=vmem,
        out_shape=jax.ShapeDtypeStruct((CHIPS, 1, LANES), F32),
        scratch_shapes=scratch
        + [
            pltpu.VMEM(keys.shape, BF16),
            pltpu.VMEM(ids.shape, I32),
            pltpu.VMEM((q_rows // LANES + 8, LANES), F32),
        ],
        compiler_params=params(big),
        name="other",
    )(boxes, other, *own)
    return lax.all_to_all(results, CHIP_AXES, 0, 0, tiled=True), where


def unit_rows(emb):
    return pl.pallas_call(
        unit_kernel,
        grid=(4,),
        in_specs=[pl.BlockSpec((ROWS // 4, D), lambda i: (i, 0))],
        out_specs=pl.BlockSpec((ROWS // 4, D), lambda i: (i, 0)),
        out_shape=jax.ShapeDtypeStruct((ROWS, D), BF16),
        compiler_params=params(),
        cost_estimate=pl.CostEstimate(flops=4 * ROWS * D, bytes_accessed=4 * ROWS * D, transcendentals=ROWS),
        name="unit",
    )(emb)


def body(emb, home, member, rank):
    emb2 = swap(emb)
    mine, counts = pl.pallas_call(
        count_kernel,
        out_shape=[
            jax.ShapeDtypeStruct((PARTS, LANES), I32),
            jax.ShapeDtypeStruct((DEVICES, 8, LANES), BF16),
        ],
        compiler_params=params(56),
        name="count",
    )(*(x.reshape(PARTS, LANES) for x in (home, member, rank)))
    other = swap(mine)
    counts = lax.all_to_all(counts, ALL_AXES, 0, 0, tiled=True).reshape(DEVICES * 8, LANES)
    unit = unit_rows(emb)
    chip = lax.axis_index("yx") * lax.axis_size("z") + lax.axis_index("z")
    place = jnp.stack([chip, lax.axis_index("core")]).astype(I32)
    asg, boxes, fast = pl.pallas_call(
        assign_kernel,
        in_specs=[
            pl.BlockSpec(memory_space=pltpu.SMEM),
            pl.BlockSpec(memory_space=pltpu.VMEM),
        ],
        out_specs=[
            pl.BlockSpec(memory_space=pltpu.VMEM),
            pl.BlockSpec(memory_space=pltpu.VMEM),
            pl.BlockSpec(memory_space=pltpu.SMEM),
        ],
        out_shape=[
            jax.ShapeDtypeStruct((8, LANES), I32),
            jax.ShapeDtypeStruct((2, LANES), I32),
            jax.ShapeDtypeStruct((1,), I32),
        ],
        scratch_shapes=[
            pltpu.VMEM((PLACES, LANES), F32),
            pltpu.VMEM((PLACES, LANES), I32),
            pltpu.VMEM((DEVICES, LANES), F32),
        ],
        compiler_params=params(),
        name="assign",
    )(place, counts)
    back, where = lax.cond(
        fast[0] == 1,
        functools.partial(exchange, FAST),
        functools.partial(exchange, SLOW),
        asg,
        mine,
        other,
        unit,
        emb2,
        boxes,
    )
    out = pl.pallas_call(
        result_kernel,
        out_shape=jax.ShapeDtypeStruct((1, ROWS), F32),
        compiler_params=params(),
        name="result",
    )(back, swap(back), where)
    return out.reshape(ROWS)


def solution(mesh):
    chips = Mesh(mesh.devices.reshape(-1, 2, mesh.devices.shape[1]), ALL_AXES)
    rows = P(ALL_AXES)
    return jax.shard_map(
        body,
        mesh=chips,
        in_specs=(P(ALL_AXES, None), P(ALL_AXES, None), P(ALL_AXES, None), rows),
        out_specs=rows,
        check_vma=False,
    )
```

```python
import functools

import jax
import jax.numpy as jnp
from jax import lax
from jax.experimental import pallas as pl
from jax.experimental.pallas import tpu as pltpu
from jax.sharding import Mesh, PartitionSpec as P

D = 768
ROWS = 1024
CLUSTERS = 512
MEMBERS = 16
CHIPS = 64
DEVICES = 128
LANES = 128
PIECES = CLUSTERS // LANES
BATCH = 40
BATCHES = -(-(CLUSTERS - CHIPS) // BATCH)
PLACES = CHIPS + BATCHES * BATCH
FAST = 32
SLOW = 72
GROUP = 32
QB = 768
KB = 1536
UNROLL = 32
CHUNK = 16
EXTRA = 128
PARTS = ROWS // LANES
RANK_BITS = 17
CHIP_AXES = ("yx", "z")
ALL_AXES = ("yx", "core", "z")
F32, BF16, I32, U32 = jnp.float32, jnp.bfloat16, jnp.int32, jnp.uint32
NT = (((1,), (1,)), ((), ()))


def iota(shape, dim):
    return lax.broadcasted_iota(I32, shape, dim)


def dot(a, b):
    return jnp.dot(a, b, preferred_element_type=F32)


def dot_nt(a, b):
    return lax.dot_general(a, b, NT, preferred_element_type=F32)


def ones_where(mask):
    return jnp.where(mask, 1.0, 0.0).astype(BF16)


def params(mib=16):
    return pltpu.CompilerParams(vmem_limit_bytes=mib << 20)


def count_kernel(home_ref, member_ref, rank_ref, ident_ref, out_ref):
    cl = home_ref[...] * MEMBERS + member_ref[...]
    ident_ref[...] = (cl << RANK_BITS) + rank_ref[...]
    sub = iota((LANES, LANES), 0)
    sub8 = iota((8, LANES), 0)
    tile = jnp.zeros((8, LANES), F32)
    for r in range(PIECES):
        found = jnp.zeros((LANES, LANES), F32)
        for b in range(PARTS):
            found = found + jnp.where(cl[b : b + 1, :] == sub + r * LANES, 1.0, 0.0)
        tile = jnp.where(sub8 == r, dot_nt(jnp.ones((8, LANES), BF16), found.astype(BF16)), tile)
    out_ref[...] = jnp.broadcast_to(tile.astype(BF16)[None], out_ref.shape)


def normalized(values):
    mean = jnp.sum(values * values, axis=1, keepdims=True) * (1.0 / D)
    return (values * (lax.rsqrt(mean + 1e-06) * D ** (-0.5))).astype(BF16)


def unit_kernel(emb_ref, unit_ref):
    unit_ref[...] = normalized(emb_ref[...].astype(F32))


def assign_kernel(place_ref, counts_ref, asg_ref, boxes_ref, fast_ref, sizes, bins, pairs):
    chip, core = place_ref[0], place_ref[1]
    lane = iota((LANES, LANES), 1)
    sub = iota((LANES, LANES), 0)
    eye = lane == sub
    lane1 = iota((1, LANES), 1)
    flat = counts_ref[...]
    total = dot(ones_where(iota((8, DEVICES * 8), 1) % 8 == iota((8, DEVICES * 8), 0)), flat)
    tot = [total[r : r + 1, :] for r in range(PIECES)]
    key = [tot[r] * CLUSTERS + (CLUSTERS - 1 - r * LANES - lane1).astype(F32) for r in range(PIECES)]
    col = [jnp.sum(jnp.where(eye, key[r], 0.0), axis=1, keepdims=True) for r in range(PIECES)]
    pos = []
    for r in range(PIECES):
        above = jnp.zeros((LANES, LANES), F32)
        for q in range(PIECES):
            above = above + jnp.where(col[q] > key[r], 1.0, 0.0)
        pos.append(jnp.sum(above, axis=0, keepdims=True).astype(I32))
    for q in range(PIECES):
        here = jnp.zeros((LANES, LANES), F32)
        for r in range(PIECES):
            here = here + jnp.where(pos[r] == sub + q * LANES, tot[r], 0.0)
        sizes[q * LANES : (q + 1) * LANES, :] = jnp.broadcast_to(
            jnp.sum(here, axis=1, keepdims=True), (LANES, LANES)
        )
    lane_c = iota((CHIPS, LANES), 1)
    eye_c = lane_c == iota((CHIPS, LANES), 0)
    lane_b = iota((BATCH, LANES), 1)
    sub_b = iota((BATCH, LANES), 0)

    def one_batch(step, load):
        order = jnp.where(lane1 < CHIPS, load * CHIPS + lane1.astype(F32), 3.0e7)
        order_col = jnp.sum(jnp.where(eye_c, order, 0.0), axis=1, keepdims=True)
        place = jnp.sum(jnp.where(order_col < order, 1.0, 0.0), axis=0, keepdims=True).astype(I32)
        chosen = place == sub_b
        rows = pl.ds(pl.multiple_of(CHIPS + step * BATCH, 8), BATCH)
        bins[rows, :] = jnp.broadcast_to(
            jnp.sum(jnp.where(chosen, lane_b, 0), axis=1, keepdims=True), (BATCH, LANES)
        )
        return load + jnp.sum(jnp.where(chosen, sizes[rows, :], 0.0), axis=0, keepdims=True)

    sizes[CLUSTERS:, :] = jnp.zeros((PLACES - CLUSTERS, LANES), F32)
    bins[:CHIPS, :] = iota((CHIPS, LANES), 0)
    largest = jnp.sum(jnp.where(eye_c, sizes[:CHIPS, :], 0.0), axis=0, keepdims=True)
    lax.fori_loop(0, BATCHES, one_batch, largest)
    asg = []
    for r in range(PIECES):
        found = jnp.zeros((LANES, LANES), I32)
        for q in range(PIECES):
            rows = bins[q * LANES : (q + 1) * LANES, :]
            found = found + jnp.where(pos[r] == sub + q * LANES, rows, 0)
        asg.append(jnp.sum(found, axis=0, keepdims=True))
    row8 = iota((DEVICES * 8, LANES), 0) % 8

    def pair_counts(table):
        per_row = jnp.zeros((DEVICES * 8, LANES), F32)
        for r in range(PIECES):
            per_row = jnp.where(row8 == r, dot_nt(flat, ones_where(table[r] == sub)), per_row)
        return jnp.sum(per_row.reshape(DEVICES, 8, LANES), axis=1)

    def put(table):
        sub8 = iota((8, LANES), 0)
        tile = jnp.zeros((8, LANES), I32)
        for r in range(PIECES):
            tile = jnp.where(sub8 == r, table[r], tile)
        asg_ref[...] = tile

    pairs[...] = pair_counts(asg)
    put(asg)
    device = iota((CHIPS, DEVICES), 1)
    both_cores = ones_where((device >> 3) * 4 + device % 4 == iota((CHIPS, DEVICES), 0))
    most = jnp.max(dot(both_cores, pairs[...].astype(BF16)))
    over = jnp.max(jnp.sum(jnp.maximum(pairs[...] - (FAST - 1), 0.0), axis=1, keepdims=True))
    fast = (most.astype(I32) <= 2 * (FAST - 1)) & (over.astype(I32) <= EXTRA)
    fast_ref[0] = fast.astype(I32)

    @pl.when(jnp.logical_not(fast))
    def _():
        fixed = []
        for r in range(PIECES):
            cluster = lane1 + r * LANES
            fixed.append((cluster // MEMBERS) * 2 + (cluster % MEMBERS) // 8)
        pairs[...] = pair_counts(fixed)
        put(fixed)

    mine = jnp.sum(jnp.where(lane == chip, pairs[...], 0.0), axis=1, keepdims=True)
    box = lane % CHIPS
    source_core = jnp.where(lane < CHIPS, core, 1 - core)

    def from_core(which):
        source = ((box // 4) * 2 + which) * 4 + box % 4
        return jnp.sum(jnp.where(sub == source, mine, 0.0), axis=0, keepdims=True).astype(I32)

    room = jnp.where(fast, FAST - 1, SLOW - 1)
    boxes = jnp.minimum(from_core(source_core), room)
    boxes = boxes + jnp.maximum(from_core(1 - source_core) - room, 0)
    rounded = (((boxes + 7) // 8) * 8).astype(F32).astype(BF16)
    boxes_ref[0:1, :] = boxes
    earlier = (sub < lane) & (sub // CHIPS == lane // CHIPS)
    boxes_ref[1:2, :] = dot(rounded, ones_where(earlier)).astype(I32)


def label_pieces(ident):
    cl, rank = ident >> RANK_BITS, ident & ((1 << RANK_BITS) - 1)
    return rank >> 9, (rank >> 1) & 255, (rank & 1) + 2 * (cl >> 4), (cl & 15) + 1


def route_kernel(
    asg_ref, mine_ref, other_ref, unit_ref, emb2_ref, out_ref, where_ref, index, index2, labels, extra, *, slots
):
    group = pl.program_id(0)
    room = slots - 1

    @pl.when(group == 0)
    def _():
        sub = iota((CHIPS, LANES), 0)
        lane_sub = iota((LANES, LANES), 0)
        before = ones_where(lane_sub < iota((LANES, LANES), 1))
        chip_of, chips_of, number_of, sums = [], [], [], []
        for ident_ref in (mine_ref, other_ref):
            cl = ident_ref[...] >> RANK_BITS
            chip = jnp.zeros((PARTS, LANES), I32)
            for r in range(PIECES):
                table = jnp.broadcast_to(asg_ref[r : r + 1, :], (PARTS, LANES))
                found = jnp.take_along_axis(table, cl & (LANES - 1), axis=1, mode="promise_in_bounds")
                chip = jnp.where((cl >> 7) == r, found, chip)
            to_chip = [jnp.where(chip[b : b + 1, :] == sub, 1.0, 0.0) for b in range(PARTS)]
            earlier = dot(jnp.concatenate(to_chip, axis=0).astype(BF16), before)
            carry = jnp.zeros((CHIPS, 1), F32)
            rows = []
            for b in range(PARTS):
                until = earlier[b * CHIPS : (b + 1) * CHIPS, :] + carry
                rows.append(jnp.sum(to_chip[b] * until, axis=0, keepdims=True))
                carry = carry + jnp.sum(to_chip[b], axis=1, keepdims=True)
            chip_of.append(chip)
            chips_of.append(to_chip)
            number_of.append(jnp.concatenate(rows, axis=0).astype(I32))
            sums.append(carry)
        spill = []
        for half in range(2):
            taken = [jnp.sum(part * sums[1 - half], axis=0, keepdims=True) for part in chips_of[half]]
            spill.append(jnp.concatenate(taken, axis=0).astype(I32) + number_of[half] - room)
        stays = number_of[0] < room
        target = jnp.where(stays, chip_of[0] * slots + number_of[0], -1)
        back_chip = jnp.where(stays, chip_of[0], chip_of[0] + CHIPS)
        back_slot = jnp.where(stays, number_of[0], spill[0])
        for b in range(PARTS):
            at = slice(b * LANES, (b + 1) * LANES)
            index[:, at] = target[b : b + 1, :]
            where_ref[0:1, at] = back_chip[b : b + 1, :]
            where_ref[1:2, at] = back_slot[b : b + 1, :]

        comes = jnp.where(number_of[1] >= room, 1.0, 0.0)
        within = dot(comes.astype(BF16), before)
        carry = jnp.zeros((1, 1), F32)
        chosen, zero = [], jnp.zeros((1, LANES), I32)
        pieces2 = label_pieces(other_ref[...]) + (chip_of[1], jnp.maximum(spill[1], 0))
        facts = jnp.zeros((8, LANES), F32)
        for b in range(PARTS):
            part = comes[b : b + 1, :]
            order = jnp.where(part > 0.5, within[b : b + 1, :] + carry, -1.0).astype(I32)
            carry = carry + jnp.sum(part, axis=1, keepdims=True)
            chosen.append(ones_where(order == lane_sub))
            lines = [piece[b : b + 1, :] for piece in pieces2] + [zero, zero]
            facts = facts + dot_nt(jnp.concatenate(lines, axis=0).astype(F32).astype(BF16), chosen[b])
        chosen = jnp.concatenate(chosen, axis=1)
        came = facts[3:4, :] > 0.5
        chip2, slot2 = facts[4:5, :].astype(I32), facts[5:6, :].astype(I32)
        index2[...] = jnp.where(came, chip2 * slots + slot2, -1)
        extra[...] = normalized(dot(chosen, emb2_ref[...]))

        to_chip2 = jnp.where(came & (chip2 == sub), 1.0, 0.0)
        pieces = label_pieces(mine_ref[...])
        text, slot_hot = [], []
        held = jnp.where(stays, number_of[0], -1)
        for b in range(PARTS):
            lines = [chips_of[0][b] * piece[b : b + 1, :].astype(F32) for piece in pieces]
            text.append(jnp.concatenate(lines, axis=0).astype(BF16))
            slot_hot.append(ones_where(held[b : b + 1, :] == lane_sub))
        text, slot_hot = jnp.concatenate(text, axis=1), jnp.concatenate(slot_hot, axis=1)
        text2 = jnp.concatenate([to_chip2 * facts[k : k + 1, :] for k in range(PIECES)], axis=0)
        slot_hot2 = ones_where(jnp.where(came, slot2, -1) == lane_sub)
        text = dot_nt(text, slot_hot) + dot_nt(text2.astype(BF16), slot_hot2)
        for k in range(PIECES):
            labels[:, k * LANES : (k + 1) * LANES] = text[k * CHIPS : (k + 1) * CHIPS, :].astype(BF16)

    size = GROUP * slots
    first = group * size
    rows = dot(ones_where(index[...] == iota((size, ROWS), 0) + first), unit_ref[...])
    rows = rows + dot(ones_where(index2[...] == iota((size, EXTRA), 0) + first), extra[...])
    last = (iota((size, CHIPS), 1) - group * GROUP) * slots + slots - 1
    text = dot(ones_where(last == iota((size, CHIPS), 0)), labels[...])
    out_ref[:, : PIECES * LANES] = (rows[:, : PIECES * LANES] + text).astype(BF16)
    out_ref[:, PIECES * LANES :] = rows[:, PIECES * LANES :].astype(BF16)


def pack_boxes(boxes_ref, held_boxes, box_rows, sems, keys, ids, columns, text, half, tiles):
    copies = []
    for c in range(CHIPS // CHUNK):
        some = pl.ds(c * CHUNK, CHUNK)
        copies.append(pltpu.make_async_copy(held_boxes.at[some], box_rows.at[some], sems.at[c]))
        copies[c].start()
    lane1 = iota((1, LANES), 1)
    ids[...] = jnp.full(ids.shape, -1, I32)
    label_row = ones_where(iota((CHUNK, CHUNK * 8), 1) == iota((CHUNK, CHUNK * 8), 0) * 8 + 7)
    for c in range(CHIPS // CHUNK):
        copies[c].wait()
        first = c * CHUNK
        held = box_rows[first : first + CHUNK, tiles - 1, :, : PIECES * LANES]
        words = dot(label_row, held.reshape(CHUNK * 8, PIECES * LANES)).astype(I32)
        high, low, mixed, filled = (words[:, k * LANES : (k + 1) * LANES] for k in range(PIECES))
        rank = (high << 9) + (low << 1) + (mixed & 1)
        cluster = ((mixed >> 1) << 4) + filled - 1
        text[first : first + CHUNK, :] = jnp.where(filled > 0, (cluster << RANK_BITS) + rank, -1)

        def pack(i, carry, first=first):
            b = first + i
            start = boxes_ref[1, half * CHIPS + b]
            keys[pl.ds(start // 8, tiles)] = box_rows[b]
            shift = lax.rem(start, LANES)
            row = start // LANES
            line = pltpu.roll(text[pl.ds(b, 1), :], shift, 1)
            ids[pl.ds(row, 1), :] = jnp.where(lane1 >= shift, line, ids[pl.ds(row, 1), :])
            ids[pl.ds(row + 1, 1), :] = jnp.where(lane1 < shift, line, -1)
            return carry

        lax.fori_loop(0, CHUNK, pack, 0, unroll=CHUNK)
    end = half * CHIPS + CHIPS - 1
    count = boxes_ref[1, end] + ((boxes_ref[0, end] + 7) // 8) * 8
    per_block = KB // LANES

    def column(k, carry):
        for r in range(per_block):
            line = jnp.broadcast_to(ids[pl.ds(k * per_block + r, 1), :], (LANES, LANES))
            rows = pl.ds(pl.multiple_of(k * KB + r * LANES, LANES), LANES)
            columns[rows, :] = jnp.transpose(line)
        return carry

    lax.fori_loop(0, (count + KB - 1) // KB, column, 0)
    return count


def compare(queries, q_ids, n_queries, keys, columns, n_keys, first, finish):
    parts = QB // LANES

    def block(q, carry):
        query = queries[pl.ds(q * (QB // 8), QB // 8)].reshape(QB, D)
        high = [q_ids[pl.ds(q * parts + p, 1), :] for p in range(parts)]
        low = [(h >> RANK_BITS) << RANK_BITS for h in high]
        span = [(h - l).astype(U32) for h, l in zip(high, low)]

        def key_block(k, acc):
            score = dot_nt(keys[pl.ds(k * (KB // 8), KB // 8)].reshape(KB, D), query)
            ident = columns[pl.ds(pl.multiple_of(k * KB, KB), KB), :]
            new = []
            for p in range(parts):
                piece = score[:, p * LANES : (p + 1) * LANES]
                valid = (ident - low[p]).astype(U32) < span[p]
                piece = jnp.where(valid, piece, -1.0)
                new.append(jnp.maximum(acc[p], jnp.max(piece.reshape(KB // 8, 8, LANES), axis=0)))
            return tuple(new)

        acc = tuple(first(q * parts + p) for p in range(parts))
        acc = lax.fori_loop(0, (n_keys + KB - 1) // KB, key_block, acc)
        for p in range(parts):
            finish(q * parts + p, acc[p])
        return carry

    lax.fori_loop(0, (n_queries + QB - 1) // QB, block, 0)


def own_kernel(
    boxes_ref, mine_ref, keys_ref, ids, most_ref, columns, text, box_rows, keys, sems, keys_sem, *, slots
):
    count = pack_boxes(boxes_ref, mine_ref, box_rows, sems, keys, ids, columns, text, 0, slots // 8)
    kept = pltpu.make_async_copy(keys, keys_ref, keys_sem)
    kept.start()

    def finish(p, acc):
        most_ref[p] = acc

    compare(keys, ids, count, keys, columns, count, lambda p: jnp.full((8, LANES), -1.0, F32), finish)
    kept.wait()


def other_kernel(
    boxes_ref, other_ref, queries_ref, q_ids, most_ref, out_ref, columns, text, box_rows, keys, sems, keys_sem,
    queries, ids, best, *, slots
):
    asked = pltpu.make_async_copy(queries_ref, queries, keys_sem)
    asked.start()
    count = pack_boxes(boxes_ref, other_ref, box_rows, sems, keys, ids, columns, text, 1, slots // 8)
    asked.wait()
    n_queries = boxes_ref[1, CHIPS - 1] + ((boxes_ref[0, CHIPS - 1] + 7) // 8) * 8

    def finish(p, acc):
        best[pl.ds(p, 1), :] = jnp.max(acc, axis=0, keepdims=True)

    compare(queries, q_ids, n_queries, keys, columns, count, lambda p: most_ref[p], finish)
    lane1 = iota((1, LANES), 1)

    def unpack(b, carry):
        start = boxes_ref[1, b]
        shift = lax.rem(start, LANES)
        row = start // LANES
        two = jnp.where(lane1 >= shift, best[pl.ds(row, 1), :], best[pl.ds(row + 1, 1), :])
        line = pltpu.roll(two, lax.rem(LANES - shift, LANES), 1)
        line = jnp.where(lane1 < boxes_ref[0, b], line, 0.0)
        out_ref[b] = line
        return carry

    lax.fori_loop(0, CHIPS, unpack, 0, unroll=UNROLL)


def result_kernel(back_ref, back2_ref, where_ref, out_ref):
    table = jnp.concatenate([back_ref[:, 0, :], back2_ref[:, 0, :]], axis=0).T
    to_chip = jnp.where(where_ref[0:1, :] == iota((LANES, ROWS), 0), 1.0, 0.0)
    by_slot = jnp.dot(
        table, to_chip, preferred_element_type=F32, precision=lax.Precision.HIGHEST
    )
    picked = jnp.where(where_ref[1:2, :] == iota((LANES, ROWS), 0), by_slot, 0.0)
    out_ref[...] = jnp.sum(picked, axis=0, keepdims=True)


def swap(x):
    return lax.ppermute(x, "core", [(0, 1), (1, 0)])


def exchange(slots, asg, mine, other, unit, emb2, boxes):
    size = GROUP * slots
    big = 34 if slots == FAST else 50
    outbox, where = pl.pallas_call(
        functools.partial(route_kernel, slots=slots),
        grid=(CHIPS // GROUP,),
        in_specs=[
            pl.BlockSpec((8, LANES), lambda g: (0, 0)),
            pl.BlockSpec((PARTS, LANES), lambda g: (0, 0)),
            pl.BlockSpec((PARTS, LANES), lambda g: (0, 0)),
            pl.BlockSpec((ROWS, D), lambda g: (0, 0)),
            pl.BlockSpec((ROWS, D), lambda g: (0, 0)),
        ],
        out_specs=[
            pl.BlockSpec((size, D), lambda g: (g, 0)),
            pl.BlockSpec((2, ROWS), lambda g: (0, 0)),
        ],
        out_shape=[
            jax.ShapeDtypeStruct((CHIPS * slots, D), BF16),
            jax.ShapeDtypeStruct((2, ROWS), I32),
        ],
        scratch_shapes=[
            pltpu.VMEM((1, ROWS), I32),
            pltpu.VMEM((1, EXTRA), I32),
            pltpu.VMEM((CHIPS, PIECES * LANES), BF16),
            pltpu.VMEM((EXTRA, D), BF16),
        ],
        compiler_params=params(big),
        name="route",
    )(asg, mine, other, unit, emb2)
    mine = lax.all_to_all(outbox.reshape(CHIPS, slots, D), CHIP_AXES, 0, 0, tiled=True)
    mine = mine.reshape(CHIPS, slots // 8, 8, D)
    other = swap(mine)
    n_rows = CHIPS * slots
    q_rows, k_rows = -(-n_rows // QB) * QB, -(-n_rows // KB) * KB
    n_keys = max(q_rows, k_rows)
    n_ids = n_keys // LANES + 8
    vmem = pl.BlockSpec(memory_space=pltpu.VMEM)
    smem = pl.BlockSpec(memory_space=pltpu.SMEM)
    hbm = pl.BlockSpec(memory_space=pl.ANY)
    keys = jax.ShapeDtypeStruct((n_keys // 8, 8, D), BF16)
    ids = jax.ShapeDtypeStruct((n_ids, LANES), I32)
    most = jax.ShapeDtypeStruct((q_rows // LANES, 8, LANES), F32)
    scratch = [
        pltpu.VMEM((k_rows, LANES), I32),
        pltpu.VMEM((CHIPS, LANES), I32),
        pltpu.VMEM((CHIPS, slots // 8, 8, D), BF16),
        pltpu.VMEM(keys.shape, BF16),
        pltpu.SemaphoreType.DMA((CHIPS // CHUNK,)),
        pltpu.SemaphoreType.DMA,
    ]
    own = pl.pallas_call(
        functools.partial(own_kernel, slots=slots),
        in_specs=[smem, hbm],
        out_specs=[hbm, vmem, vmem],
        out_shape=[keys, ids, most],
        scratch_shapes=scratch,
        compiler_params=params(big),
        cost_estimate=pl.CostEstimate(flops=8 * 10**9, bytes_accessed=4 * n_rows * D, transcendentals=0),
        name="own",
    )(boxes, mine)
    results = pl.pallas_call(
        functools.partial(other_kernel, slots=slots),
        in_specs=[smem, hbm, hbm, vmem, vmem],
        out_specs=vmem,
        out_shape=jax.ShapeDtypeStruct((CHIPS, 1, LANES), F32),
        scratch_shapes=scratch
        + [
            pltpu.VMEM(keys.shape, BF16),
            pltpu.VMEM(ids.shape, I32),
            pltpu.VMEM((q_rows // LANES + 8, LANES), F32),
        ],
        compiler_params=params(big),
        name="other",
    )(boxes, other, *own)
    return lax.all_to_all(results, CHIP_AXES, 0, 0, tiled=True), where


def unit_rows(emb):
    return pl.pallas_call(
        unit_kernel,
        grid=(4,),
        in_specs=[pl.BlockSpec((ROWS // 4, D), lambda i: (i, 0))],
        out_specs=pl.BlockSpec((ROWS // 4, D), lambda i: (i, 0)),
        out_shape=jax.ShapeDtypeStruct((ROWS, D), BF16),
        compiler_params=params(),
        cost_estimate=pl.CostEstimate(flops=4 * ROWS * D, bytes_accessed=4 * ROWS * D, transcendentals=ROWS),
        name="unit",
    )(emb)


def body(emb, home, member, rank):
    emb2 = swap(emb)
    mine, counts = pl.pallas_call(
        count_kernel,
        out_shape=[
            jax.ShapeDtypeStruct((PARTS, LANES), I32),
            jax.ShapeDtypeStruct((DEVICES, 8, LANES), BF16),
        ],
        compiler_params=params(56),
        name="count",
    )(*(x.reshape(PARTS, LANES) for x in (home, member, rank)))
    other = swap(mine)
    counts = lax.all_to_all(counts, ALL_AXES, 0, 0, tiled=True).reshape(DEVICES * 8, LANES)
    unit = unit_rows(emb)
    chip = lax.axis_index("yx") * lax.axis_size("z") + lax.axis_index("z")
    place = jnp.stack([chip, lax.axis_index("core")]).astype(I32)
    asg, boxes, fast = pl.pallas_call(
        assign_kernel,
        in_specs=[
            pl.BlockSpec(memory_space=pltpu.SMEM),
            pl.BlockSpec(memory_space=pltpu.VMEM),
        ],
        out_specs=[
            pl.BlockSpec(memory_space=pltpu.VMEM),
            pl.BlockSpec(memory_space=pltpu.VMEM),
            pl.BlockSpec(memory_space=pltpu.SMEM),
        ],
        out_shape=[
            jax.ShapeDtypeStruct((8, LANES), I32),
            jax.ShapeDtypeStruct((2, LANES), I32),
            jax.ShapeDtypeStruct((1,), I32),
        ],
        scratch_shapes=[
            pltpu.VMEM((PLACES, LANES), F32),
            pltpu.VMEM((PLACES, LANES), I32),
            pltpu.VMEM((DEVICES, LANES), F32),
        ],
        compiler_params=params(),
        name="assign",
    )(place, counts)
    back, where = lax.cond(
        fast[0] == 1,
        functools.partial(exchange, FAST),
        functools.partial(exchange, SLOW),
        asg,
        mine,
        other,
        unit,
        emb2,
        boxes,
    )
    out = pl.pallas_call(
        result_kernel,
        out_shape=jax.ShapeDtypeStruct((1, ROWS), F32),
        compiler_params=params(),
        name="result",
    )(back, swap(back), where)
    return out.reshape(ROWS)


def solution(mesh):
    chips = Mesh(mesh.devices.reshape(-1, 2, mesh.devices.shape[1]), ALL_AXES)
    rows = P(ALL_AXES)
    return jax.shard_map(
        body,
        mesh=chips,
        in_specs=(P(ALL_AXES, None), P(ALL_AXES, None), P(ALL_AXES, None), rows),
        out_specs=rows,
        check_vma=False,
    )
```

```python
import functools

import jax
import jax.numpy as jnp
from jax import lax
from jax.experimental import pallas as pl
from jax.experimental.pallas import tpu as pltpu
from jax.sharding import Mesh, PartitionSpec as P

D = 768
ROWS = 1024
CLUSTERS = 512
MEMBERS = 16
CHIPS = 64
DEVICES = 128
LANES = 128
PIECES = CLUSTERS // LANES
BATCH = 40
BATCHES = -(-(CLUSTERS - CHIPS) // BATCH)
PLACES = CHIPS + BATCHES * BATCH
FAST = 32
SLOW = 72
GROUP = 32
QB = 768
KB = 1536
UNROLL = 32
CHUNK = 16
EXTRA = 128
PARTS = ROWS // LANES
RANK_BITS = 17
CHIP_AXES = ("yx", "z")
ALL_AXES = ("yx", "core", "z")
F32, BF16, I32, U32 = jnp.float32, jnp.bfloat16, jnp.int32, jnp.uint32
NT = (((1,), (1,)), ((), ()))


def iota(shape, dim):
    return lax.broadcasted_iota(I32, shape, dim)


def dot(a, b):
    return jnp.dot(a, b, preferred_element_type=F32)


def dot_nt(a, b):
    return lax.dot_general(a, b, NT, preferred_element_type=F32)


def ones_where(mask):
    return jnp.where(mask, 1.0, 0.0).astype(BF16)


def params(mib=16):
    return pltpu.CompilerParams(vmem_limit_bytes=mib << 20)


def count_kernel(home_ref, member_ref, rank_ref, ident_ref, out_ref):
    cl = home_ref[...] * MEMBERS + member_ref[...]
    ident_ref[...] = (cl << RANK_BITS) + rank_ref[...]
    sub = iota((LANES, LANES), 0)
    sub8 = iota((8, LANES), 0)
    tile = jnp.zeros((8, LANES), F32)
    for r in range(PIECES):
        found = jnp.zeros((LANES, LANES), F32)
        for b in range(PARTS):
            found = found + jnp.where(cl[b : b + 1, :] == sub + r * LANES, 1.0, 0.0)
        tile = jnp.where(sub8 == r, dot_nt(jnp.ones((8, LANES), BF16), found.astype(BF16)), tile)
    out_ref[...] = jnp.broadcast_to(tile.astype(BF16)[None], out_ref.shape)


def normalized(values):
    mean = jnp.sum(values * values, axis=1, keepdims=True) * (1.0 / D)
    return (values * (lax.rsqrt(mean + 1e-06) * D ** (-0.5))).astype(BF16)


def unit_kernel(emb_ref, unit_ref):
    unit_ref[...] = normalized(emb_ref[...].astype(F32))


def assign_kernel(place_ref, counts_ref, asg_ref, boxes_ref, fast_ref, sizes, bins, pairs):
    chip, core = place_ref[0], place_ref[1]
    lane = iota((LANES, LANES), 1)
    sub = iota((LANES, LANES), 0)
    eye = lane == sub
    lane1 = iota((1, LANES), 1)
    flat = counts_ref[...]
    total = dot(ones_where(iota((8, DEVICES * 8), 1) % 8 == iota((8, DEVICES * 8), 0)), flat)
    tot = [total[r : r + 1, :] for r in range(PIECES)]
    key = [tot[r] * CLUSTERS + (CLUSTERS - 1 - r * LANES - lane1).astype(F32) for r in range(PIECES)]
    col = [jnp.sum(jnp.where(eye, key[r], 0.0), axis=1, keepdims=True) for r in range(PIECES)]
    pos = []
    for r in range(PIECES):
        above = jnp.zeros((LANES, LANES), F32)
        for q in range(PIECES):
            above = above + jnp.where(col[q] > key[r], 1.0, 0.0)
        pos.append(jnp.sum(above, axis=0, keepdims=True).astype(I32))
    for q in range(PIECES):
        here = jnp.zeros((LANES, LANES), F32)
        for r in range(PIECES):
            here = here + jnp.where(pos[r] == sub + q * LANES, tot[r], 0.0)
        sizes[q * LANES : (q + 1) * LANES, :] = jnp.broadcast_to(
            jnp.sum(here, axis=1, keepdims=True), (LANES, LANES)
        )
    lane_c = iota((CHIPS, LANES), 1)
    eye_c = lane_c == iota((CHIPS, LANES), 0)
    lane_b = iota((BATCH, LANES), 1)
    sub_b = iota((BATCH, LANES), 0)

    def one_batch(step, load):
        order = jnp.where(lane1 < CHIPS, load * CHIPS + lane1.astype(F32), 3.0e7)
        order_col = jnp.sum(jnp.where(eye_c, order, 0.0), axis=1, keepdims=True)
        place = jnp.sum(jnp.where(order_col < order, 1.0, 0.0), axis=0, keepdims=True).astype(I32)
        chosen = place == sub_b
        rows = pl.ds(pl.multiple_of(CHIPS + step * BATCH, 8), BATCH)
        bins[rows, :] = jnp.broadcast_to(
            jnp.sum(jnp.where(chosen, lane_b, 0), axis=1, keepdims=True), (BATCH, LANES)
        )
        return load + jnp.sum(jnp.where(chosen, sizes[rows, :], 0.0), axis=0, keepdims=True)

    sizes[CLUSTERS:, :] = jnp.zeros((PLACES - CLUSTERS, LANES), F32)
    bins[:CHIPS, :] = iota((CHIPS, LANES), 0)
    largest = jnp.sum(jnp.where(eye_c, sizes[:CHIPS, :], 0.0), axis=0, keepdims=True)
    lax.fori_loop(0, BATCHES, one_batch, largest, unroll=4)
    asg = []
    for r in range(PIECES):
        found = jnp.zeros((LANES, LANES), I32)
        for q in range(PIECES):
            rows = bins[q * LANES : (q + 1) * LANES, :]
            found = found + jnp.where(pos[r] == sub + q * LANES, rows, 0)
        asg.append(jnp.sum(found, axis=0, keepdims=True))
    row8 = iota((DEVICES * 8, LANES), 0) % 8

    def pair_counts(table):
        per_row = jnp.zeros((DEVICES * 8, LANES), F32)
        for r in range(PIECES):
            per_row = jnp.where(row8 == r, dot_nt(flat, ones_where(table[r] == sub)), per_row)
        return jnp.sum(per_row.reshape(DEVICES, 8, LANES), axis=1)

    def put(table):
        sub8 = iota((8, LANES), 0)
        tile = jnp.zeros((8, LANES), I32)
        for r in range(PIECES):
            tile = jnp.where(sub8 == r, table[r], tile)
        asg_ref[...] = tile

    pairs[...] = pair_counts(asg)
    put(asg)
    device = iota((CHIPS, DEVICES), 1)
    both_cores = ones_where((device >> 3) * 4 + device % 4 == iota((CHIPS, DEVICES), 0))
    most = jnp.max(dot(both_cores, pairs[...].astype(BF16)))
    over = jnp.max(jnp.sum(jnp.maximum(pairs[...] - (FAST - 1), 0.0), axis=1, keepdims=True))
    fast = (most.astype(I32) <= 2 * (FAST - 1)) & (over.astype(I32) <= EXTRA)
    fast_ref[0] = fast.astype(I32)

    @pl.when(jnp.logical_not(fast))
    def _():
        fixed = []
        for r in range(PIECES):
            cluster = lane1 + r * LANES
            fixed.append((cluster // MEMBERS) * 2 + (cluster % MEMBERS) // 8)
        pairs[...] = pair_counts(fixed)
        put(fixed)

    mine = jnp.sum(jnp.where(lane == chip, pairs[...], 0.0), axis=1, keepdims=True)
    box = lane % CHIPS
    source_core = jnp.where(lane < CHIPS, core, 1 - core)

    def from_core(which):
        source = ((box // 4) * 2 + which) * 4 + box % 4
        return jnp.sum(jnp.where(sub == source, mine, 0.0), axis=0, keepdims=True).astype(I32)

    room = jnp.where(fast, FAST - 1, SLOW - 1)
    boxes = jnp.minimum(from_core(source_core), room)
    boxes = boxes + jnp.maximum(from_core(1 - source_core) - room, 0)
    rounded = (((boxes + 7) // 8) * 8).astype(F32).astype(BF16)
    boxes_ref[0:1, :] = boxes
    earlier = (sub < lane) & (sub // CHIPS == lane // CHIPS)
    boxes_ref[1:2, :] = dot(rounded, ones_where(earlier)).astype(I32)


def label_pieces(ident):
    cl, rank = ident >> RANK_BITS, ident & ((1 << RANK_BITS) - 1)
    return rank >> 9, (rank >> 1) & 255, (rank & 1) + 2 * (cl >> 4), (cl & 15) + 1


def route_kernel(
    asg_ref, mine_ref, other_ref, unit_ref, emb2_ref, out_ref, where_ref, index, index2, labels, extra, *, slots
):
    group = pl.program_id(0)
    room = slots - 1

    @pl.when(group == 0)
    def _():
        sub = iota((CHIPS, LANES), 0)
        lane_sub = iota((LANES, LANES), 0)
        before = ones_where(lane_sub < iota((LANES, LANES), 1))
        chip_of, chips_of, number_of, sums = [], [], [], []
        for ident_ref in (mine_ref, other_ref):
            cl = ident_ref[...] >> RANK_BITS
            chip = jnp.zeros((PARTS, LANES), I32)
            for r in range(PIECES):
                table = jnp.broadcast_to(asg_ref[r : r + 1, :], (PARTS, LANES))
                found = jnp.take_along_axis(table, cl & (LANES - 1), axis=1, mode="promise_in_bounds")
                chip = jnp.where((cl >> 7) == r, found, chip)
            to_chip = [jnp.where(chip[b : b + 1, :] == sub, 1.0, 0.0) for b in range(PARTS)]
            earlier = dot(jnp.concatenate(to_chip, axis=0).astype(BF16), before)
            carry = jnp.zeros((CHIPS, 1), F32)
            rows = []
            for b in range(PARTS):
                until = earlier[b * CHIPS : (b + 1) * CHIPS, :] + carry
                rows.append(jnp.sum(to_chip[b] * until, axis=0, keepdims=True))
                carry = carry + jnp.sum(to_chip[b], axis=1, keepdims=True)
            chip_of.append(chip)
            chips_of.append(to_chip)
            number_of.append(jnp.concatenate(rows, axis=0).astype(I32))
            sums.append(carry)
        spill = []
        for half in range(2):
            taken = [jnp.sum(part * sums[1 - half], axis=0, keepdims=True) for part in chips_of[half]]
            spill.append(jnp.concatenate(taken, axis=0).astype(I32) + number_of[half] - room)
        stays = number_of[0] < room
        target = jnp.where(stays, chip_of[0] * slots + number_of[0], -1)
        back_chip = jnp.where(stays, chip_of[0], chip_of[0] + CHIPS)
        back_slot = jnp.where(stays, number_of[0], spill[0])
        for b in range(PARTS):
            at = slice(b * LANES, (b + 1) * LANES)
            index[:, at] = target[b : b + 1, :]
            where_ref[0:1, at] = back_chip[b : b + 1, :]
            where_ref[1:2, at] = back_slot[b : b + 1, :]

        comes = jnp.where(number_of[1] >= room, 1.0, 0.0)
        within = dot(comes.astype(BF16), before)
        carry = jnp.zeros((1, 1), F32)
        chosen, zero = [], jnp.zeros((1, LANES), I32)
        pieces2 = label_pieces(other_ref[...]) + (chip_of[1], jnp.maximum(spill[1], 0))
        facts = jnp.zeros((8, LANES), F32)
        for b in range(PARTS):
            part = comes[b : b + 1, :]
            order = jnp.where(part > 0.5, within[b : b + 1, :] + carry, -1.0).astype(I32)
            carry = carry + jnp.sum(part, axis=1, keepdims=True)
            chosen.append(ones_where(order == lane_sub))
            lines = [piece[b : b + 1, :] for piece in pieces2] + [zero, zero]
            facts = facts + dot_nt(jnp.concatenate(lines, axis=0).astype(F32).astype(BF16), chosen[b])
        chosen = jnp.concatenate(chosen, axis=1)
        came = facts[3:4, :] > 0.5
        chip2, slot2 = facts[4:5, :].astype(I32), facts[5:6, :].astype(I32)
        index2[...] = jnp.where(came, chip2 * slots + slot2, -1)
        extra[...] = normalized(dot(chosen, emb2_ref[...]))

        to_chip2 = jnp.where(came & (chip2 == sub), 1.0, 0.0)
        pieces = label_pieces(mine_ref[...])
        text, slot_hot = [], []
        held = jnp.where(stays, number_of[0], -1)
        for b in range(PARTS):
            lines = [chips_of[0][b] * piece[b : b + 1, :].astype(F32) for piece in pieces]
            text.append(jnp.concatenate(lines, axis=0).astype(BF16))
            slot_hot.append(ones_where(held[b : b + 1, :] == lane_sub))
        text, slot_hot = jnp.concatenate(text, axis=1), jnp.concatenate(slot_hot, axis=1)
        text2 = jnp.concatenate([to_chip2 * facts[k : k + 1, :] for k in range(PIECES)], axis=0)
        slot_hot2 = ones_where(jnp.where(came, slot2, -1) == lane_sub)
        text = dot_nt(text, slot_hot) + dot_nt(text2.astype(BF16), slot_hot2)
        for k in range(PIECES):
            labels[:, k * LANES : (k + 1) * LANES] = text[k * CHIPS : (k + 1) * CHIPS, :].astype(BF16)

    size = GROUP * slots
    first = group * size
    rows = dot(ones_where(index[...] == iota((size, ROWS), 0) + first), unit_ref[...])
    rows = rows + dot(ones_where(index2[...] == iota((size, EXTRA), 0) + first), extra[...])
    last = (iota((size, CHIPS), 1) - group * GROUP) * slots + slots - 1
    text = dot(ones_where(last == iota((size, CHIPS), 0)), labels[...])
    out_ref[:, : PIECES * LANES] = (rows[:, : PIECES * LANES] + text).astype(BF16)
    out_ref[:, PIECES * LANES :] = rows[:, PIECES * LANES :].astype(BF16)


def pack_boxes(boxes_ref, held_boxes, box_rows, sems, keys, ids, columns, text, half, tiles):
    copies = []
    for c in range(CHIPS // CHUNK):
        some = pl.ds(c * CHUNK, CHUNK)
        copies.append(pltpu.make_async_copy(held_boxes.at[some], box_rows.at[some], sems.at[c]))
        copies[c].start()
    lane1 = iota((1, LANES), 1)
    ids[...] = jnp.full(ids.shape, -1, I32)
    label_row = ones_where(iota((CHUNK, CHUNK * 8), 1) == iota((CHUNK, CHUNK * 8), 0) * 8 + 7)
    for c in range(CHIPS // CHUNK):
        copies[c].wait()
        first = c * CHUNK
        held = box_rows[first : first + CHUNK, tiles - 1, :, : PIECES * LANES]
        words = dot(label_row, held.reshape(CHUNK * 8, PIECES * LANES)).astype(I32)
        high, low, mixed, filled = (words[:, k * LANES : (k + 1) * LANES] for k in range(PIECES))
        rank = (high << 9) + (low << 1) + (mixed & 1)
        cluster = ((mixed >> 1) << 4) + filled - 1
        text[first : first + CHUNK, :] = jnp.where(filled > 0, (cluster << RANK_BITS) + rank, -1)

        def pack(i, carry, first=first):
            b = first + i
            start = boxes_ref[1, half * CHIPS + b]
            keys[pl.ds(start // 8, tiles)] = box_rows[b]
            shift = lax.rem(start, LANES)
            row = start // LANES
            line = pltpu.roll(text[pl.ds(b, 1), :], shift, 1)
            ids[pl.ds(row, 1), :] = jnp.where(lane1 >= shift, line, ids[pl.ds(row, 1), :])
            ids[pl.ds(row + 1, 1), :] = jnp.where(lane1 < shift, line, -1)
            return carry

        lax.fori_loop(0, CHUNK, pack, 0, unroll=CHUNK)
    end = half * CHIPS + CHIPS - 1
    count = boxes_ref[1, end] + ((boxes_ref[0, end] + 7) // 8) * 8
    per_block = KB // LANES

    def column(k, carry):
        for r in range(per_block):
            line = jnp.broadcast_to(ids[pl.ds(k * per_block + r, 1), :], (LANES, LANES))
            rows = pl.ds(pl.multiple_of(k * KB + r * LANES, LANES), LANES)
            columns[rows, :] = jnp.transpose(line)
        return carry

    lax.fori_loop(0, (count + KB - 1) // KB, column, 0)
    return count


def compare(queries, q_ids, n_queries, keys, columns, n_keys, first, finish):
    parts = QB // LANES

    def block(q, carry):
        query = queries[pl.ds(q * (QB // 8), QB // 8)].reshape(QB, D)
        high = [q_ids[pl.ds(q * parts + p, 1), :] for p in range(parts)]
        low = [(h >> RANK_BITS) << RANK_BITS for h in high]
        span = [(h - l).astype(U32) for h, l in zip(high, low)]

        def key_block(k, acc):
            score = dot_nt(keys[pl.ds(k * (KB // 8), KB // 8)].reshape(KB, D), query)
            ident = columns[pl.ds(pl.multiple_of(k * KB, KB), KB), :]
            new = []
            for p in range(parts):
                piece = score[:, p * LANES : (p + 1) * LANES]
                valid = (ident - low[p]).astype(U32) < span[p]
                piece = jnp.where(valid, piece, -1.0)
                new.append(jnp.maximum(acc[p], jnp.max(piece.reshape(KB // 8, 8, LANES), axis=0)))
            return tuple(new)

        acc = tuple(first(q * parts + p) for p in range(parts))
        acc = lax.fori_loop(0, (n_keys + KB - 1) // KB, key_block, acc)
        for p in range(parts):
            finish(q * parts + p, acc[p])
        return carry

    lax.fori_loop(0, (n_queries + QB - 1) // QB, block, 0)


def own_kernel(
    boxes_ref, mine_ref, keys_ref, ids, most_ref, columns, text, box_rows, keys, sems, keys_sem, *, slots
):
    count = pack_boxes(boxes_ref, mine_ref, box_rows, sems, keys, ids, columns, text, 0, slots // 8)
    kept = pltpu.make_async_copy(keys, keys_ref, keys_sem)
    kept.start()

    def finish(p, acc):
        most_ref[p] = acc

    compare(keys, ids, count, keys, columns, count, lambda p: jnp.full((8, LANES), -1.0, F32), finish)
    kept.wait()


def other_kernel(
    boxes_ref, other_ref, queries_ref, q_ids, most_ref, out_ref, columns, text, box_rows, keys, sems, keys_sem,
    queries, ids, best, *, slots
):
    asked = pltpu.make_async_copy(queries_ref, queries, keys_sem)
    asked.start()
    count = pack_boxes(boxes_ref, other_ref, box_rows, sems, keys, ids, columns, text, 1, slots // 8)
    asked.wait()
    n_queries = boxes_ref[1, CHIPS - 1] + ((boxes_ref[0, CHIPS - 1] + 7) // 8) * 8

    def finish(p, acc):
        best[pl.ds(p, 1), :] = jnp.max(acc, axis=0, keepdims=True)

    compare(queries, q_ids, n_queries, keys, columns, count, lambda p: most_ref[p], finish)
    lane1 = iota((1, LANES), 1)

    def unpack(b, carry):
        start = boxes_ref[1, b]
        shift = lax.rem(start, LANES)
        row = start // LANES
        two = jnp.where(lane1 >= shift, best[pl.ds(row, 1), :], best[pl.ds(row + 1, 1), :])
        line = pltpu.roll(two, lax.rem(LANES - shift, LANES), 1)
        line = jnp.where(lane1 < boxes_ref[0, b], line, 0.0)
        out_ref[b] = line
        return carry

    lax.fori_loop(0, CHIPS, unpack, 0, unroll=UNROLL)


def result_kernel(back_ref, back2_ref, where_ref, out_ref):
    table = jnp.concatenate([back_ref[:, 0, :], back2_ref[:, 0, :]], axis=0).T
    to_chip = jnp.where(where_ref[0:1, :] == iota((LANES, ROWS), 0), 1.0, 0.0)
    by_slot = jnp.dot(
        table, to_chip, preferred_element_type=F32, precision=lax.Precision.HIGHEST
    )
    picked = jnp.where(where_ref[1:2, :] == iota((LANES, ROWS), 0), by_slot, 0.0)
    out_ref[...] = jnp.sum(picked, axis=0, keepdims=True)


def swap(x):
    return lax.ppermute(x, "core", [(0, 1), (1, 0)])


def exchange(slots, asg, mine, other, unit, emb2, boxes):
    size = GROUP * slots
    big = 34 if slots == FAST else 50
    outbox, where = pl.pallas_call(
        functools.partial(route_kernel, slots=slots),
        grid=(CHIPS // GROUP,),
        in_specs=[
            pl.BlockSpec((8, LANES), lambda g: (0, 0)),
            pl.BlockSpec((PARTS, LANES), lambda g: (0, 0)),
            pl.BlockSpec((PARTS, LANES), lambda g: (0, 0)),
            pl.BlockSpec((ROWS, D), lambda g: (0, 0)),
            pl.BlockSpec((ROWS, D), lambda g: (0, 0)),
        ],
        out_specs=[
            pl.BlockSpec((size, D), lambda g: (g, 0)),
            pl.BlockSpec((2, ROWS), lambda g: (0, 0)),
        ],
        out_shape=[
            jax.ShapeDtypeStruct((CHIPS * slots, D), BF16),
            jax.ShapeDtypeStruct((2, ROWS), I32),
        ],
        scratch_shapes=[
            pltpu.VMEM((1, ROWS), I32),
            pltpu.VMEM((1, EXTRA), I32),
            pltpu.VMEM((CHIPS, PIECES * LANES), BF16),
            pltpu.VMEM((EXTRA, D), BF16),
        ],
        compiler_params=params(big),
        name="route",
    )(asg, mine, other, unit, emb2)
    mine = lax.all_to_all(outbox.reshape(CHIPS, slots, D), CHIP_AXES, 0, 0, tiled=True)
    mine = mine.reshape(CHIPS, slots // 8, 8, D)
    other = swap(mine)
    n_rows = CHIPS * slots
    q_rows, k_rows = -(-n_rows // QB) * QB, -(-n_rows // KB) * KB
    n_keys = max(q_rows, k_rows)
    n_ids = n_keys // LANES + 8
    vmem = pl.BlockSpec(memory_space=pltpu.VMEM)
    smem = pl.BlockSpec(memory_space=pltpu.SMEM)
    hbm = pl.BlockSpec(memory_space=pl.ANY)
    keys = jax.ShapeDtypeStruct((n_keys // 8, 8, D), BF16)
    ids = jax.ShapeDtypeStruct((n_ids, LANES), I32)
    most = jax.ShapeDtypeStruct((q_rows // LANES, 8, LANES), F32)
    scratch = [
        pltpu.VMEM((k_rows, LANES), I32),
        pltpu.VMEM((CHIPS, LANES), I32),
        pltpu.VMEM((CHIPS, slots // 8, 8, D), BF16),
        pltpu.VMEM(keys.shape, BF16),
        pltpu.SemaphoreType.DMA((CHIPS // CHUNK,)),
        pltpu.SemaphoreType.DMA,
    ]
    own = pl.pallas_call(
        functools.partial(own_kernel, slots=slots),
        in_specs=[smem, hbm],
        out_specs=[hbm, vmem, vmem],
        out_shape=[keys, ids, most],
        scratch_shapes=scratch,
        compiler_params=params(big),
        cost_estimate=pl.CostEstimate(flops=8 * 10**9, bytes_accessed=4 * n_rows * D, transcendentals=0),
        name="own",
    )(boxes, mine)
    results = pl.pallas_call(
        functools.partial(other_kernel, slots=slots),
        in_specs=[smem, hbm, hbm, vmem, vmem],
        out_specs=vmem,
        out_shape=jax.ShapeDtypeStruct((CHIPS, 1, LANES), F32),
        scratch_shapes=scratch
        + [
            pltpu.VMEM(keys.shape, BF16),
            pltpu.VMEM(ids.shape, I32),
            pltpu.VMEM((q_rows // LANES + 8, LANES), F32),
        ],
        compiler_params=params(big),
        name="other",
    )(boxes, other, *own)
    return lax.all_to_all(results, CHIP_AXES, 0, 0, tiled=True), where


def unit_rows(emb):
    return pl.pallas_call(
        unit_kernel,
        grid=(4,),
        in_specs=[pl.BlockSpec((ROWS // 4, D), lambda i: (i, 0))],
        out_specs=pl.BlockSpec((ROWS // 4, D), lambda i: (i, 0)),
        out_shape=jax.ShapeDtypeStruct((ROWS, D), BF16),
        compiler_params=params(),
        cost_estimate=pl.CostEstimate(flops=4 * ROWS * D, bytes_accessed=4 * ROWS * D, transcendentals=ROWS),
        name="unit",
    )(emb)


def body(emb, home, member, rank):
    emb2 = swap(emb)
    mine, counts = pl.pallas_call(
        count_kernel,
        out_shape=[
            jax.ShapeDtypeStruct((PARTS, LANES), I32),
            jax.ShapeDtypeStruct((DEVICES, 8, LANES), BF16),
        ],
        compiler_params=params(56),
        name="count",
    )(*(x.reshape(PARTS, LANES) for x in (home, member, rank)))
    other = swap(mine)
    counts = lax.all_to_all(counts, ALL_AXES, 0, 0, tiled=True).reshape(DEVICES * 8, LANES)
    unit = unit_rows(emb)
    chip = lax.axis_index("yx") * lax.axis_size("z") + lax.axis_index("z")
    place = jnp.stack([chip, lax.axis_index("core")]).astype(I32)
    asg, boxes, fast = pl.pallas_call(
        assign_kernel,
        in_specs=[
            pl.BlockSpec(memory_space=pltpu.SMEM),
            pl.BlockSpec(memory_space=pltpu.VMEM),
        ],
        out_specs=[
            pl.BlockSpec(memory_space=pltpu.VMEM),
            pl.BlockSpec(memory_space=pltpu.VMEM),
            pl.BlockSpec(memory_space=pltpu.SMEM),
        ],
        out_shape=[
            jax.ShapeDtypeStruct((8, LANES), I32),
            jax.ShapeDtypeStruct((2, LANES), I32),
            jax.ShapeDtypeStruct((1,), I32),
        ],
        scratch_shapes=[
            pltpu.VMEM((PLACES, LANES), F32),
            pltpu.VMEM((PLACES, LANES), I32),
            pltpu.VMEM((DEVICES, LANES), F32),
        ],
        compiler_params=params(),
        name="assign",
    )(place, counts)
    back, where = lax.cond(
        fast[0] == 1,
        functools.partial(exchange, FAST),
        functools.partial(exchange, SLOW),
        asg,
        mine,
        other,
        unit,
        emb2,
        boxes,
    )
    out = pl.pallas_call(
        result_kernel,
        out_shape=jax.ShapeDtypeStruct((1, ROWS), F32),
        compiler_params=params(),
        name="result",
    )(back, swap(back), where)
    return out.reshape(ROWS)


def solution(mesh):
    chips = Mesh(mesh.devices.reshape(-1, 2, mesh.devices.shape[1]), ALL_AXES)
    rows = P(ALL_AXES)
    return jax.shard_map(
        body,
        mesh=chips,
        in_specs=(P(ALL_AXES, None), P(ALL_AXES, None), P(ALL_AXES, None), rows),
        out_specs=rows,
        check_vma=False,
    )
```
